32 devices in a mesh: replica: 2 (over y), fsdp: 8 (over z, core), seq: 2 (over x).
Axes of the slice: x: 2, y: 2, z: 4, core: 2. Of those that a mesh axis runs over, the one named last changes fastest.
Arguments:
- series_in: bfloat16 [16, 512, 1280], P(('replica', 'fsdp'), 'seq'), may hold values from -6 to 6
- cotangent: bfloat16 [16, 512, 1280], P(('replica', 'fsdp'), 'seq'), may hold values from -6 to 6
- qkv_weight: bfloat16 [2, 1280, 3840], P(None, 'fsdp'), may hold values from -0.15625 to 0.15625
- out_weight: bfloat16 [2, 1280, 1280], P(None, 'fsdp'), may hold values from -0.625 to 0.625
- up_weight: bfloat16 [2, 1280, 1280], P(None, 'fsdp'), may hold values from -0.15625 to 0.15625
- down_weight: bfloat16 [2, 1280, 1280], P(None, 'fsdp'), may hold values from -0.15625 to 0.15625
- norm_gains: bfloat16 [2, 2, 1280], P(None, None, 'fsdp'), may hold values from 0.25 to 1.75
- up_bias: bfloat16 [2, 1280], P(None, 'fsdp'), may hold values from -3 to 3
- down_bias: bfloat16 [2, 1280], P(None, 'fsdp'), may hold values from -2 to 2
- query_scale: bfloat16 [2, 80], P(None, 'fsdp'), may hold values from -1 to 1
- pad_length: int32 [16], P(('replica', 'fsdp')), may hold values from 0 to 128, as said below
- span_starts: int32 [16, 4], P(('replica', 'fsdp')), may hold values from 0 to 480, as said below
- span_count: int32 [16], P(('replica', 'fsdp')), may hold values from 1 to 4, as said below
Outputs:
- series_out: bfloat16 [16, 512, 1280], P(('replica', 'fsdp'), 'seq')
- input_grad: bfloat16 [16, 512, 1280], P(('replica', 'fsdp'), 'seq')
- grad_qkv: float32 [2, 1280, 3840], P(None, 'fsdp')
- grad_out: float32 [2, 1280, 1280], P(None, 'fsdp')
- grad_up: float32 [2, 1280, 1280], P(None, 'fsdp')
- grad_down: float32 [2, 1280, 1280], P(None, 'fsdp')
- grad_gains: float32 [2, 2, 1280], P(None, None, 'fsdp')
- grad_up_bias: float32 [2, 1280], P(None, 'fsdp')
- grad_down_bias: float32 [2, 1280], P(None, 'fsdp')
- grad_query_scale: float32 [2, 80], P(None, 'fsdp')
The draws below stay inside these ranges and needn't reach their ends.
Inputs may be any that keep to these rules, and one draw needn't show every extreme that they name: `pad_length`: one series in every draw has exactly 128 padded positions. `span_starts`: slot 0 of every series starts within 31 positions before 256, so it holds positions 255 and 256; spans may intersect. Slot k of series b is used when k < span_count[b].
All inputs are finite; a program needn't handle non-finite values.
Results may differ from the reference program's by a relative error of at most 0.025.
Values may be sent and summed in bfloat16 or wider, within the bound.
A program may use at most 256 MiB of HBM per device.

```python
import math
import jax
import jax.numpy as jnp
from jax import lax

D = 1280
HEADS = 16
HEAD = 80
FF = 1280
LAYERS = 2
LEN = 512
SPAN = 32
SPANS = 4
SERIES = 16
LEN_DEV = 256
PAD_MOST = 128


def draw_pad_length(key, part):
    values = jax.random.randint(jax.random.fold_in(key, 11), (SERIES,), 0, PAD_MOST + 1)
    chosen = jax.random.randint(jax.random.fold_in(key, 12), (), 0, SERIES)
    return values.at[chosen].set(PAD_MOST).astype(jnp.int32)


def draw_span_count(key, part):
    values = jax.random.randint(jax.random.fold_in(key, 31), (SERIES,), 1, SPANS + 1)
    chosen = jax.random.randint(jax.random.fold_in(key, 32), (), 0, SERIES)
    return values.at[chosen].set(SPANS).astype(jnp.int32)


def draw_span_starts(key, part):
    first_col = LEN_DEV - jax.random.randint(jax.random.fold_in(key, 21), (SERIES, 1), 1, SPAN)
    other_cols = jax.random.randint(jax.random.fold_in(key, 22), (SERIES, SPANS - 1), 0, LEN - SPAN + 1)
    chosen = jax.random.randint(jax.random.fold_in(key, 23), (), 0, SERIES)
    second_row = (chosen + 1) % SERIES
    other_cols = other_cols.at[chosen, 0].set(LEN - SPAN)
    other_cols = other_cols.at[second_row, SPANS - 2].set(0)
    return jnp.concatenate([first_col, other_cols], axis=1).astype(jnp.int32)


def level_of(own_key, shape, cuts, low, high):
    level, own = 1.0, jax.random.fold_in(own_key, 6)
    for axis_at, blocks in cuts:
        heights = jnp.exp(jax.random.uniform(jax.random.fold_in(own, axis_at), (blocks,), jnp.float32, low / len(cuts), high / len(cuts)))
        level = level * jnp.repeat(heights, shape[axis_at] // blocks).reshape([-1 if axis == axis_at else 1 for axis in range(len(shape))])
    return level


def bell_draw(own_key, extent, deviation, limit, split=(), kind=jnp.bfloat16):
    values = jax.random.normal(own_key, extent, jnp.float32) * deviation
    if len(split) > 0:
        values = level_of(own_key, extent, split, -0.22, 0.18) * values
    return jnp.clip(values, min=-limit, max=limit).astype(kind)


def setup_inputs(seed: int = 0) -> dict:
    arg_keys = jax.random.split(jax.random.key(seed), 14)
    return {
        "series_in": bell_draw(arg_keys[0], (SERIES, LEN, D), 1.0, 6.0, ((0, 16), (1, 2))),
        "cotangent": bell_draw(arg_keys[1], (SERIES, LEN, D), 1.0, 6.0, ((0, 16), (1, 2))),
        "qkv_weight": bell_draw(arg_keys[2], (LAYERS, D, 3 * D), D ** -0.5, 0.15625, ((1, 8),)),
        "out_weight": bell_draw(arg_keys[3], (LAYERS, D, D), (D // 16) ** -0.5, 0.625, ((1, 8),)),
        "up_weight": bell_draw(arg_keys[4], (LAYERS, D, FF), D ** -0.5, 0.15625, ((1, 8),)),
        "down_weight": bell_draw(arg_keys[5], (LAYERS, FF, D), FF ** -0.5, 0.15625, ((1, 8),)),
        "norm_gains": jnp.clip(1.0 + 0.15 * jax.random.normal(arg_keys[6], (LAYERS, 2, D), jnp.float32), 0.25, 1.75).astype(jnp.bfloat16),
        "up_bias": bell_draw(arg_keys[7], (LAYERS, FF), 0.5, 3.0, ((1, 8),)),
        "down_bias": bell_draw(arg_keys[8], (LAYERS, D), 0.3, 2.0, ((1, 8),)),
        "query_scale": jnp.clip(jax.random.uniform(arg_keys[9], (LAYERS, HEAD), jnp.float32, -1.0, 1.0) * level_of(arg_keys[9], (LAYERS, HEAD), ((1, 8),), -0.4, 0.0), -1.0, 1.0).astype(jnp.bfloat16),
        "pad_length": draw_pad_length(jax.random.fold_in(arg_keys[13], 71), 0),
        "span_starts": draw_span_starts(jax.random.fold_in(arg_keys[13], 71), 0),
        "span_count": draw_span_count(jax.random.fold_in(arg_keys[13], 71), 0),
    }


EPSILON = 1e-06
SOFT_ONE = 1.442695041
NEG_FILL = -1e+30
PRECISE = lax.Precision.HIGHEST

@jax.custom_vjp
def low(v):
    return lax.optimization_barrier(v.astype(jnp.bfloat16)).astype(jnp.float32)

@jax.custom_vjp
def low_back(v):
    return v

def low_keep(v):
    return (low(v), None)

def low_pass(kept, grad):
    return (grad,)

def back_keep(v):
    return (v, None)

def back_low(kept, grad):
    return (low(grad),)
low.defvjp(low_keep, low_pass)
low_back.defvjp(back_keep, back_low)

def visible(pad_length, span_starts, span_count, offset, local_length, total_length):
    query_pos = offset + jnp.arange(local_length, dtype=jnp.int32)
    key_pos = jnp.arange(total_length, dtype=jnp.int32)
    shared = jnp.zeros((span_starts.shape[0], local_length, total_length), dtype=bool)
    for slot_index in range(span_starts.shape[1]):
        slot_start = span_starts[:, slot_index]
        slot_used = slot_index < span_count
        query_in = slot_used[:, None] & (query_pos[None, :] >= slot_start[:, None]) & (query_pos[None, :] < slot_start[:, None] + SPAN)
        key_in = (key_pos[None, :] >= slot_start[:, None]) & (key_pos[None, :] < slot_start[:, None] + SPAN)
        shared = shared | query_in[:, :, None] & key_in[:, None, :]
    causal = key_pos[None, :] <= query_pos[:, None]
    allowed = (key_pos[None, None, :] >= pad_length[:, None, None]) & (causal[None] | shared)
    return allowed | (key_pos[None, None, :] == query_pos[None, :, None])

def rms_scale(values, scale_gain):
    return values * lax.rsqrt(lax.optimization_barrier(jnp.mean(values * values, axis=-1, keepdims=True)) + EPSILON) * scale_gain

def one_layer(current, weights, allowed):
    qkv_weight, out_weight, up_weight, down_weight, norm_gains, up_bias, down_bias, query_scale = weights
    group_size, length, model_width = current.shape
    normed = low(rms_scale(current, norm_gains[0]))
    projected = low_back(jnp.einsum('gtd,de->gte', normed, qkv_weight, precision=PRECISE))
    factor = jax.nn.softplus(query_scale) * (SOFT_ONE / math.sqrt(HEAD))
    queries = low(projected[..., :model_width].reshape(group_size, length, HEADS, HEAD) * factor)
    keys_low = low(projected[..., model_width:2 * model_width].reshape(group_size, length, HEADS, HEAD))
    values_low = low(projected[..., 2 * model_width:].reshape(group_size, length, HEADS, HEAD))
    scores = low_back(jnp.einsum('gqhe,gkhe->ghqk', queries, keys_low, precision=PRECISE))
    scores = jnp.where(allowed[:, None], scores, NEG_FILL)
    attn_probs = low(jax.nn.softmax(scores, axis=-1))
    attended = jnp.einsum('ghqk,gkhe->gqhe', attn_probs, values_low, precision=PRECISE).reshape(group_size, length, model_width)
    attended = low(low_back(attended))
    after_attn = current + low_back(jnp.einsum('gtd,de->gte', attended, out_weight, precision=PRECISE))
    mixed_low = low(rms_scale(after_attn, norm_gains[1]))
    hidden_pre = low_back(jnp.einsum('gtd,df->gtf', mixed_low, up_weight, precision=PRECISE) + up_bias)
    hidden = low(jax.nn.silu(hidden_pre))
    return after_attn + low_back(jnp.einsum('gtf,fd->gtd', hidden, down_weight, precision=PRECISE) + down_bias)

def two_layers(current, allowed, params):
    for layer_index in range(LAYERS):
        current = one_layer(current, tuple((member[layer_index] for member in params)), allowed)
    return current

def reference(series_in, cotangent, qkv_weight, out_weight, up_weight, down_weight, norm_gains, up_bias, down_bias, query_scale, pad_length, span_starts, span_count):
    params = tuple((member.astype(jnp.float32) for member in (qkv_weight, out_weight, up_weight, down_weight, norm_gains, up_bias, down_bias, query_scale)))
    group_size = math.gcd(SERIES, max(1, 4096 // LEN))
    blocks = SERIES // group_size
    inputs = series_in.astype(jnp.float32).reshape(blocks, group_size, LEN, D)
    mask_all = visible(pad_length, span_starts, span_count, 0, LEN, LEN).reshape(blocks, group_size, LEN, LEN)
    stepper = jax.checkpoint(two_layers)

    def forward(values, weights):
        return lax.map(lambda blocked: stepper(blocked[0], blocked[1], weights), (values, mask_all))
    result, pullback = jax.vjp(forward, inputs, params)
    grad_in, weight_grads = pullback(cotangent.astype(jnp.float32).reshape(blocks, group_size, LEN, D))
    return (result.reshape(SERIES, LEN, D).astype(jnp.bfloat16), grad_in.reshape(SERIES, LEN, D).astype(jnp.bfloat16), weight_grads[0], weight_grads[1], weight_grads[2], weight_grads[3], weight_grads[4], weight_grads[5], weight_grads[6], weight_grads[7])
```

```python
import functools
import math

import jax
import jax.numpy as jnp
from jax import lax
from jax.experimental import pallas as pl
from jax.experimental.pallas import tpu as pltpu
from jax.sharding import PartitionSpec as P

HEADS = 16
HEAD = 80
SPAN = 32


EPSILON = 1e-06
SOFT_ONE = 1.442695041
NEG_FILL = -1e30


def visible(pad_length, span_starts, span_count, offset, local_length, total_length):
    query_pos = offset + jnp.arange(local_length, dtype=jnp.int32)
    key_pos = jnp.arange(total_length, dtype=jnp.int32)
    shared = jnp.zeros((span_starts.shape[0], local_length, total_length), dtype=bool)
    for slot_index in range(span_starts.shape[1]):
        slot_start = span_starts[:, slot_index]
        slot_used = slot_index < span_count
        query_in = (
            slot_used[:, None]
            & (query_pos[None, :] >= slot_start[:, None])
            & (query_pos[None, :] < slot_start[:, None] + SPAN)
        )
        key_in = (key_pos[None, :] >= slot_start[:, None]) & (
            key_pos[None, :] < slot_start[:, None] + SPAN
        )
        shared = shared | query_in[:, :, None] & key_in[:, None, :]
    causal = key_pos[None, :] <= query_pos[:, None]
    allowed = (key_pos[None, None, :] >= pad_length[:, None, None]) & (causal[None] | shared)
    return allowed | (key_pos[None, None, :] == query_pos[None, :, None])


def norm_rows(values, scale_gain):
    inverse = lax.rsqrt(jnp.mean(values * values, axis=-1, keepdims=True) + EPSILON)
    return (values * inverse * scale_gain, inverse)


def norm_back(values, inverse, scale_gain, upstream):
    scaled = upstream * scale_gain
    inner_term = jnp.mean(values * scaled, axis=-1, keepdims=True)
    result = inverse * scaled - values * (inverse * inverse * inverse) * inner_term
    return (result, jnp.sum(upstream * values * inverse, axis=0))


def query_factor(query_scale):
    return jax.nn.softplus(query_scale.astype(jnp.float32)) * (SOFT_ONE / math.sqrt(HEAD))


MESH = pl.DeviceIdType.MESH
UNITS = 6


class Place:
    def __init__(self, nz):
        self.nz = nz
        self.r = lax.axis_index("replica")
        f = lax.axis_index("fsdp")
        self.s = lax.axis_index("seq")
        self.z = lax.div(f, 2)
        self.c = lax.rem(f, 2)
        self.f = f

    def x(self):
        return (self.r, self.f, 1 - self.s)

    def y(self):
        return (1 - self.r, self.f, self.s)

    def core(self):
        return (self.r, self.f + 1 - 2 * self.c, self.s)

    def to(self, d):
        return (self.r, lax.rem(self.z + d, self.nz) * 2 + self.c, self.s)

    def source(self, d):
        return lax.rem(self.z - d + self.nz, self.nz)

    def greet(self):
        barrier = pltpu.get_barrier_semaphore()
        peers = [self.x(), self.y(), self.core()] + [self.to(d) for d in range(1, self.nz)]
        for peer in peers:
            pl.semaphore_signal(barrier, inc=1, device_id=peer, device_id_type=MESH)
        pl.semaphore_wait(barrier, len(peers))


def remote(src, dst, send, recv, device):
    return pltpu.make_async_remote_copy(
        src_ref=src, dst_ref=dst, send_sem=send, recv_sem=recv, device_id=device, device_id_type=MESH
    )


class Gather:
    def __init__(
        self, nz, layers, qkv_ref, out_ref, up_ref, down_ref, small_ref, full_ref, tiny_ref,
        mine, local_sem, keep_sem, zs, zr, xs, xr, ys, yr, fxs, fxr, fys, fyr, cs, cr, ts, tr,
    ):
        self.__dict__.update(locals())
        self.at = Place(nz)
        self.shard, self.width = out_ref.shape[1], out_ref.shape[2]
        self.half, self.wide = self.shard // 2, self.width // 2
        self.units = layers * UNITS
        self.hops = nz - 1
        self.iterations = self.units + self.hops + 2

    def source(self, way, k):
        return self.at.z - way * k

    def comes(self, way, k):
        z = self.at.z
        return z >= k if way > 0 else z + k < self.nz

    def goes(self, way):
        z = self.at.z
        return z + 1 < self.nz if way > 0 else z >= 1

    def next(self, way):
        at = self.at
        return (at.r, 2 * (at.z + way) + at.c, at.s)

    def slot(self, way, k):
        return 2 * (k - 1) + (0 if way > 0 else 1)

    def block(self, u, z, c, r, s):
        row = pl.multiple_of((2 * z + c) * self.shard + r * self.half, 8)
        col = pl.multiple_of(s * self.wide, 128)
        return self.full_ref.at[u, pl.ds(row, self.half), pl.ds(col, self.wide)]

    def quarter(self, u, z, c, r, s, part):
        step = self.half // 2
        row = pl.multiple_of((2 * z + c) * self.shard + r * self.half + part * step, 8)
        col = pl.multiple_of(s * self.wide, 128)
        return self.full_ref.at[u, pl.ds(row, step), pl.ds(col, self.wide)]

    def own(self, u, c):
        row = pl.multiple_of((2 * self.at.z + c) * self.shard, 8)
        return self.full_ref.at[u, pl.ds(row, self.shard), :]

    def local(self, layer, k):
        if k < 3:
            piece = self.qkv_ref.at[layer, :, pl.ds(k * self.width, self.width)]
        else:
            piece = (self.out_ref, self.up_ref, self.down_ref)[k - 3].at[layer]
        u = layer * UNITS + k
        return pltpu.make_async_copy(piece, self.mine.at[u], self.local_sem.at[u])

    def keep(self, u):
        return pltpu.make_async_copy(self.mine.at[u], self.own(u, self.at.c), self.keep_sem.at[u])

    def z_copy(self, u, way, k):
        at, n = self.at, self.slot(way, k)
        piece = self.block(u, self.source(way, k - 1), at.c, at.r, at.s)
        held = piece
        if k == 1:
            row = pl.multiple_of(at.r * self.half, 16)
            held = self.mine.at[u, pl.ds(row, self.half), pl.ds(pl.multiple_of(at.s * self.wide, 128), self.wide)]
        return remote(held, piece, self.zs.at[u, n], self.zr.at[u, n], self.next(way))

    def z_came(self, u, way, k):
        at, n = self.at, self.slot(way, k)
        piece = self.block(u, self.source(way, k), at.c, at.r, at.s)
        return remote(piece, piece, self.zs.at[u, n], self.zr.at[u, n], self.next(way))

    def x_copy(self, u, way, k):
        at, n = self.at, self.slot(way, k)
        piece = self.block(u, self.source(way, k), at.c, at.r, at.s)
        return remote(piece, piece, self.xs.at[u, n], self.xr.at[u, n], at.x())

    def y_copy(self, u, way, k):
        at, n = self.at, self.slot(way, k)
        piece = self.block(u, self.source(way, k), at.c, at.r, at.s)
        return remote(piece, piece, self.ys.at[u, n], self.yr.at[u, n], at.y())

    def fx_copy(self, u, way, k):
        at, n = self.at, self.slot(way, k)
        piece = self.quarter(u, self.source(way, k), at.c, 1 - at.r, at.s, 1)
        return remote(piece, piece, self.fxs.at[u, n], self.fxr.at[u, n], at.x())

    def fy_copy(self, u, way, k):
        at, n = self.at, self.slot(way, k)
        piece = self.quarter(u, self.source(way, k), at.c, at.r, 1 - at.s, 0)
        return remote(piece, piece, self.fys.at[u, n], self.fyr.at[u, n], at.y())

    def core_own(self, u):
        own, n = self.own(u, self.at.c), 8 * self.hops
        return remote(self.mine.at[u], own, self.cs.at[u, n], self.cr.at[u, n], self.at.core())

    def core_copy(self, u, way, k, which):
        at = self.at
        r = at.r if which in (0, 1) else 1 - at.r
        s = at.s if which in (0, 2) else 1 - at.s
        piece = self.block(u, self.source(way, k), at.c, r, s)
        n = 4 * self.slot(way, k) + which
        return remote(piece, piece, self.cs.at[u, n], self.cr.at[u, n], at.core())

    def tiny(self, d):
        piece = self.tiny_ref.at[self.at.f]
        return remote(piece, piece, self.ts.at[d - 1], self.tr.at[d - 1], self.at.to(d))

    def tiny_core(self, d):
        piece, n = self.tiny_ref.at[2 * self.at.source(d) + self.at.c], self.nz - 1 + d
        return remote(piece, piece, self.ts.at[n], self.tr.at[n], self.at.core())

    def begin(self):
        self.tiny_ref[self.at.f] = self.small_ref[...]
        for layer in range(self.layers):
            for k in range(UNITS):
                self.local(layer, k).start()
        self.at.greet()
        for d in range(1, self.nz):
            self.tiny(d).start()
        self.tiny_core(0).start()

    def tiny_pass(self):
        for d in range(1, self.nz):
            self.tiny(d).wait_recv()
            self.tiny_core(d).start()

    def tiny_ready(self):
        for d in range(self.nz):
            self.tiny_core(d).wait_recv()

    def tiny_done(self):
        for d in range(1, self.nz):
            self.tiny(d).wait_send()
        for d in range(self.nz):
            self.tiny_core(d).wait_send()

    def when(self, cond, work):
        pl.when(cond)(work)

    def first(self, u):
        pltpu.make_async_copy(self.out_ref.at[0], self.mine.at[u], self.local_sem.at[u]).wait()
        self.keep(u).start()
        for way in (1, -1):
            self.when(self.goes(way), lambda way=way: self.z_copy(u, way, 1).start())
        self.core_own(u).start()

    def hop(self, u, k):
        for way in (1, -1):
            def work(way=way):
                self.z_came(u, way, k).wait_recv()
                if k < self.hops:
                    self.when(self.goes(way), lambda: self.z_copy(u, way, k + 1).start())
                self.x_copy(u, way, k).start()
                self.y_copy(u, way, k).start()
                self.core_copy(u, way, k, 0).start()
            self.when(self.comes(way, k), work)

    def forward(self, u, k):
        for way in (1, -1):
            def work(way=way):
                self.x_copy(u, way, k).wait_recv()
                self.fy_copy(u, way, k).start()
                self.core_copy(u, way, k, 1).start()
                self.y_copy(u, way, k).wait_recv()
                self.fx_copy(u, way, k).start()
                self.core_copy(u, way, k, 2).start()
            self.when(self.comes(way, k), work)

    def diagonal(self, u, k):
        for way in (1, -1):
            def work(way=way):
                self.fx_copy(u, way, k).wait_recv()
                self.fy_copy(u, way, k).wait_recv()
                self.core_copy(u, way, k, 3).start()
            self.when(self.comes(way, k), work)

    def step(self, i):
        def stage(lag, work):
            u = i - lag
            self.when((u >= 0) & (u < self.units), lambda: work(u))

        stage(0, self.first)
        for k in range(1, self.hops + 1):
            stage(k, lambda u, k=k: self.hop(u, k))
        for k in range(1, self.hops + 1):
            stage(k + 1, lambda u, k=k: self.forward(u, k))
        for k in range(1, self.hops + 1):
            stage(k + 2, lambda u, k=k: self.diagonal(u, k))

    def ready(self, u):
        self.keep(u).wait()
        self.core_own(u).wait_recv()
        for k in range(1, self.hops + 1):
            for way in (1, -1):
                def work(way=way, k=k):
                    for which in range(4):
                        self.core_copy(u, way, k, which).wait_recv()
                self.when(self.comes(way, k), work)

    def drain(self, u):
        self.core_own(u).wait_send()
        for k in range(1, self.hops + 1):
            for way in (1, -1):
                def sent(way=way, k=k):
                    self.z_copy(u, way, k).wait_send()
                came = self.goes(way)
                if k > 1:
                    came = came & self.comes(way, k - 1)
                self.when(came, sent)

                def work(way=way, k=k):
                    for copy in (self.x_copy, self.y_copy, self.fx_copy, self.fy_copy):
                        copy(u, way, k).wait_send()
                    for which in range(4):
                        self.core_copy(u, way, k, which).wait_send()
                self.when(self.comes(way, k), work)

    def finish(self):
        @pl.loop(0, self.units)
        def _(u):
            self.drain(u)

        self.tiny_done()


def gather_scratch(nz, layers, shard, width):
    units, n = layers * UNITS, 2 * (nz - 1)
    dma = pltpu.SemaphoreType.DMA
    return (
        [pltpu.VMEM((units, shard, width), jnp.bfloat16), dma((units,)), dma((units,))]
        + [dma((units, n))] * 10
        + [dma((units, 1 + 4 * n))] * 2
        + [dma((2 * nz,))] * 2
    )


def dot_nn(a, b):
    return jnp.dot(a, b, preferred_element_type=jnp.float32)


def dot_nt(a, b):
    return lax.dot_general(a, b, (((1,), (1,)), ((), ())), preferred_element_type=jnp.float32)


def dot_tn(a, b):
    return lax.dot_general(a, b, (((0,), (0,)), ((), ())), preferred_element_type=jnp.float32)


ROWS = 128


def each_tile(count, body):
    @pl.loop(0, count // ROWS)
    def _(i):
        body(pl.ds(pl.multiple_of(i * ROWS, ROWS), ROWS))


def head_rows(h):
    return pl.ds(pl.multiple_of(h * HEAD, 16), HEAD)


def row_norm(values, gain):
    inverse = lax.rsqrt(jnp.mean(values * values, axis=-1, keepdims=True) + EPSILON)
    return (values * inverse * gain).astype(jnp.bfloat16)


def expand_small(tiny_ref, vec_ref, layers, shard, part):
    width = vec_ref.shape[1]
    count = tiny_ref.shape[0]
    rows, lanes = tiny_ref.shape[1:]
    line = lax.broadcasted_iota(jnp.int32, (lanes, width), 0)
    column = lax.broadcasted_iota(jnp.int32, (lanes, width), 1)
    inner = lax.rem(column, HEAD)

    def place(f, sums):
        plain, scale = sums
        piece = tiny_ref[f]
        hot = jnp.where((column - f * shard == line) & (line < shard), 1.0, 0.0).astype(jnp.bfloat16)
        spread = jnp.where((inner - f * part == line) & (line < part), 1.0, 0.0).astype(jnp.bfloat16)
        return plain + dot_nn(piece, hot), scale + dot_nn(piece, spread)

    zero = jnp.zeros((rows, width), jnp.float32)
    plain, scale = lax.fori_loop(0, count, place, (zero, zero))
    soft = jnp.maximum(scale, 0.0) + jnp.log(1.0 + jnp.exp(-jnp.abs(scale)))
    row = lax.broadcasted_iota(jnp.int32, (rows, width), 0)
    vec_ref[...] = jnp.where(row < 4 * layers, plain, soft * (SOFT_ONE / math.sqrt(HEAD)))


def attend(heads, q_ref, k_ref, v_ref, bias_ref, out_ref, lse_ref):
    queries = q_ref.shape[1]

    @pl.loop(*heads)
    def _(h):
        rows = head_rows(h)
        scores = dot_tn(k_ref[rows, :], q_ref[rows, :]) + bias_ref[:, :queries]
        top = jnp.max(scores, axis=0, keepdims=True)
        grown = jnp.exp(scores - top)
        total = jnp.sum(grown, axis=0, keepdims=True)
        out = dot_nn(v_ref[rows, :], grown.astype(jnp.bfloat16)) * (1.0 / total)
        out_ref[rows, :] = out.astype(jnp.bfloat16)
        lse_ref[h] = top + jnp.log(total)


def forward_kernel(nz, layers, part, *refs):
    series_ref, qkv_ref, out_ref, up_ref, down_ref, small_ref, bias_ref = refs[:7]
    full_ref, vec_out, series_out = refs[7:10]
    per = 11
    saved = [refs[10 + per * l : 10 + per * (l + 1)] for l in range(layers)]
    refs = refs[10 + per * layers :]
    names = ("current", "normed_t", "q", "k", "v", "lse", "att", "after", "mixed", "pre", "hidden")
    held = [dict(zip(names, refs[per * l : per * (l + 1)])) for l in range(layers)]
    refs = refs[per * layers :]
    normed, weight, vec, last, tiny_ref, swap_sem, load_sem, save_sem = refs[:8]
    gather = Gather(
        nz, layers, qkv_ref, out_ref, up_ref, down_ref, small_ref, full_ref, tiny_ref, *refs[8:]
    )
    at = gather.at
    length = series_ref.shape[0]
    total = held[0]["normed_t"].shape[1]
    other = total - length

    own_copy = pltpu.make_async_copy(series_ref, held[0]["current"].at[pl.ds(0, length)], swap_sem.at[0])
    swap_copy = remote(
        series_ref, held[0]["current"].at[pl.ds(length, other)], swap_sem.at[1], swap_sem.at[2], at.x()
    )

    def save(l, n):
        return pltpu.make_async_copy(held[l][names[n]], saved[l][n], save_sem.at[l, n])

    def fetch(u):
        gather.ready(u)
        copy = pltpu.make_async_copy(full_ref.at[u], weight, load_sem.at[0])
        copy.start()
        copy.wait()

    def vector(n):
        return vec[n : n + 1, :]

    def normalize(l):
        b = held[l]
        gain = vector(2 * l)

        def body(r):
            values = row_norm(b["current"][r, :].astype(jnp.float32), gain)
            normed[r, :] = values
            b["normed_t"][:, r] = values.T
        each_tile(total, body)
        save(l, 1).start()

    def project(l, n):
        b = held[l]
        target = b[("q", "k", "v")[n]]
        fetch(l * UNITS + n)

        def body(r):
            values = dot_nn(normed[r, :], weight[...])
            if n == 0:
                values = values * vector(4 * layers + l)
            target[:, r] = values.astype(jnp.bfloat16).T
        each_tile(target.shape[1], body)
        save(l, 2 + n).start()

    def attention(l, first):
        b = held[l]
        heads = (0, HEADS // 2) if first else (HEADS // 2, HEADS)
        attend(heads, b["q"], b["k"], b["v"], bias_ref, b["att"], b["lse"])
        if not first:
            save(l, 5).start()
            save(l, 6).start()

    def output(l):
        b = held[l]
        fetch(l * UNITS + 3)
        gain = vector(2 * l + 1)

        def body(r):
            after = b["current"][r, :].astype(jnp.float32) + dot_tn(b["att"][:, r], weight[...])
            b["after"][r, :] = after
            b["mixed"][r, :] = row_norm(after, gain)
        each_tile(b["after"].shape[0], body)
        save(l, 7).start()
        save(l, 8).start()

    def expand(l):
        b = held[l]
        fetch(l * UNITS + 4)
        bias = vector(2 * layers + l)

        def body(r):
            pre = dot_nn(b["mixed"][r, :], weight[...]) + bias
            b["pre"][r, :] = pre
            b["hidden"][r, :] = (pre * (1.0 / (1.0 + jnp.exp(-pre)))).astype(jnp.bfloat16)
        each_tile(b["pre"].shape[0], body)
        save(l, 9).start()
        save(l, 10).start()

    def contract(l):
        b = held[l]
        fetch(l * UNITS + 5)
        bias = vector(3 * layers + l)

        def body(r):
            values = b["after"][r, :] + (dot_nn(b["hidden"][r, :], weight[...]) + bias)
            if l + 1 < layers:
                held[l + 1]["current"][r, :] = values
            else:
                last[r, :] = values.astype(jnp.bfloat16)
        each_tile(b["after"].shape[0], body)
        if l + 1 < layers:
            save(l + 1, 0).start()
            normalize(l + 1)
        else:
            pltpu.make_async_copy(last, series_out, swap_sem.at[3]).start()

    tasks = {}

    def add(i, work):
        tasks.setdefault(i, []).append(work)

    lag = gather.hops + 2

    def early():
        gather.tiny_pass()
        gather.tiny_ready()
        expand_small(tiny_ref, vec, layers, gather.shard, part)
        pltpu.make_async_copy(vec, vec_out, swap_sem.at[4]).start()

    def begin():
        own_copy.wait()
        swap_copy.wait_recv()
        save(0, 0).start()
        normalize(0)

    add(1, early)
    add(2, begin)
    for l in range(layers):
        base = l * UNITS + lag
        for n in range(3):
            add(base + n, lambda l=l, n=n: project(l, n))
        add(base + 2, lambda l=l: attention(l, True))
        add(base + 3, lambda l=l: attention(l, False))
        add(base + 3, lambda l=l: output(l))
        add(base + 4, lambda l=l: expand(l))
        add(base + 5, lambda l=l: contract(l))

    own_copy.start()
    gather.begin()
    swap_copy.start()

    @pl.loop(0, gather.iterations)
    def _(i):
        gather.step(i)
        for when, work in sorted(tasks.items()):
            @pl.when(i == when)
            def _(work=work):
                for one in work:
                    one()

    swap_copy.wait_send()
    pltpu.make_async_copy(last, series_out, swap_sem.at[3]).wait()
    pltpu.make_async_copy(vec, vec_out, swap_sem.at[4]).wait()
    for l in range(layers):
        for n in range(per):
            save(l, n).wait()
    gather.finish()


def saved_shapes(layers, length, total, width):
    low, wide = jnp.bfloat16, jnp.float32
    shapes = []
    for l in range(layers):
        count = length if l == layers - 1 else total
        kind = low if l == 0 else wide
        shapes.append(
            [
                ((total, width), kind),
                ((width, total), low),
                ((width, count), low),
                ((width, total), low),
                ((width, total), low),
                ((HEADS, 1, count), wide),
                ((width, count), low),
                ((count, width), wide),
                ((count, width), low),
                ((count, width), wide),
                ((count, width), low),
            ]
        )
    return shapes


def forward_pass(nz, series, qkv_weight, out_weight, up_weight, down_weight, small, bias, part):
    layers, shard, width = out_weight.shape
    length, total = series.shape[0], bias.shape[0]
    units = layers * UNITS
    low, wide = jnp.bfloat16, jnp.float32
    shapes = [one for group in saved_shapes(layers, length, total, width) for one in group]
    dma = pltpu.SemaphoreType.DMA
    anywhere = pl.BlockSpec(memory_space=pl.ANY)
    inside = pl.BlockSpec(memory_space=pltpu.VMEM)
    count = 2 * nz
    results = pl.pallas_call(
        functools.partial(forward_kernel, nz, layers, part),
        out_shape=(
            jax.ShapeDtypeStruct((units, count * shard, width), low),
            jax.ShapeDtypeStruct((small.shape[0], width), wide),
            jax.ShapeDtypeStruct((length, width), low),
        )
        + tuple(jax.ShapeDtypeStruct(*one) for one in shapes),
        in_specs=[anywhere] * 5 + [inside] * 2,
        out_specs=(anywhere,) * (3 + len(shapes)),
        scratch_shapes=[pltpu.VMEM(*one) for one in shapes]
        + [
            pltpu.VMEM((total, width), low),
            pltpu.VMEM((width, width), low),
            pltpu.VMEM((small.shape[0], width), wide),
            pltpu.VMEM((length, width), low),
            pltpu.VMEM((count,) + small.shape, low),
            dma((5,)),
            dma((1,)),
            dma((layers, 11)),
        ]
        + gather_scratch(nz, layers, shard, width),
        compiler_params=pltpu.CompilerParams(
            collective_id=1, has_side_effects=True, vmem_limit_bytes=60 << 20
        ),
    )(series, qkv_weight, out_weight, up_weight, down_weight, small, bias)
    full, vec, out = results[:3]
    saved = [results[3 + 11 * l : 14 + 11 * l] for l in range(layers)]
    return full, vec, out, saved


def pair_bias(pad_length, span_starts, span_count, length):
    s = lax.axis_index("seq")
    place = jnp.arange(length, dtype=jnp.int32)
    position = jnp.concatenate([s * length + place, (1 - s) * length + place])
    key, query = position[:, None], position[None, :]
    seen = key <= query
    for slot in range(span_starts.shape[1]):
        start = span_starts[0, slot]
        inside = (position >= start) & (position < start + SPAN) & (slot < span_count[0])
        seen = seen | inside[:, None] & inside[None, :]
    allowed = (seen & (key >= pad_length[0])) | (key == query)
    return jnp.where(allowed, 0.0, NEG_FILL).astype(jnp.float32)


class Reduce:
    def __init__(
        self, nz, units, full_ref, tiny, tiny_out, grads, held, bx, by, dx, dy, cz, total, tiny_in,
        as_, ar, bs, br, ds_, dr, zs, zr, ls, ps, pr, ts, tr, free,
    ):
        self.__dict__.update(locals())
        self.at = Place(nz)
        self.slots, _, self.shard, self.width = held.shape
        self.half, self.wide, self.low = self.shard // 2, self.width // 2, nz // 2
        self.steps = range(1, nz)
        self.iterations = units + 6

    def rows(self, r):
        return pl.ds(pl.multiple_of(r * self.half, 16), self.half)

    def cols(self, s):
        return pl.ds(pl.multiple_of(s * self.wide, 128), self.wide)

    def slot(self, u):
        return lax.rem(u, self.slots)

    def a_copy(self, u):
        return remote(
            self.grads.at[:, 1 - self.at.c], self.held.at[self.slot(u)], self.as_.at[u], self.ar.at[u], self.at.core()
        )

    def bx_copy(self, u):
        piece = self.held.at[self.slot(u), pl.ds(0, self.low), :, self.cols(1 - self.at.s)]
        return remote(piece, self.bx.at[u], self.bs.at[u, 0], self.br.at[u, 0], self.at.x())

    def by_copy(self, u):
        piece = self.held.at[self.slot(u), pl.ds(self.low, self.low), self.rows(1 - self.at.r), :]
        return remote(piece, self.by.at[u], self.bs.at[u, 1], self.br.at[u, 1], self.at.y())

    def dy_copy(self, u):
        piece = self.held.at[self.slot(u), pl.ds(0, self.low), self.rows(1 - self.at.r), self.cols(self.at.s)]
        return remote(piece, self.dy.at[u], self.ds_.at[u, 0], self.dr.at[u, 0], self.at.y())

    def dx_copy(self, u):
        piece = self.held.at[self.slot(u), pl.ds(self.low, self.low), self.rows(self.at.r), self.cols(1 - self.at.s)]
        return remote(piece, self.dx.at[u], self.ds_.at[u, 1], self.dr.at[u, 1], self.at.x())

    def z_copy(self, u, d):
        at = self.at
        target = lax.rem(at.z + d, self.nz)
        piece = self.held.at[self.slot(u), target, self.rows(at.r), self.cols(at.s)]
        return remote(piece, self.cz.at[u, d - 1], self.zs.at[u, d - 1], self.zr.at[u, d - 1], at.to(d))

    def final(self, u, r, s):
        return self.full_ref.at[u, self.rows(r), self.cols(s)]

    def part(self, u, r, s, p):
        step = self.half // 2
        return self.full_ref.at[u, pl.ds(pl.multiple_of(r * self.half + p * step, 8), step), self.cols(s)]

    def put_copy(self, u):
        return pltpu.make_async_copy(self.total.at[u], self.final(u, self.at.r, self.at.s), self.ls.at[u])

    def px_copy(self, u):
        spot = self.final(u, self.at.r, self.at.s)
        return remote(self.total.at[u], spot, self.ps.at[u, 0], self.pr.at[u, 0], self.at.x())

    def py_copy(self, u):
        spot = self.final(u, self.at.r, self.at.s)
        return remote(self.total.at[u], spot, self.ps.at[u, 1], self.pr.at[u, 1], self.at.y())

    def gx_copy(self, u):
        piece = self.part(u, 1 - self.at.r, self.at.s, 1)
        return remote(piece, piece, self.ps.at[u, 2], self.pr.at[u, 2], self.at.x())

    def gy_copy(self, u):
        piece = self.part(u, self.at.r, 1 - self.at.s, 0)
        return remote(piece, piece, self.ps.at[u, 3], self.pr.at[u, 3], self.at.y())

    def plus(self, *values):
        return sum(v.astype(jnp.float32) for v in values).astype(jnp.bfloat16)

    def each(self, count, body):
        @pl.loop(0, count // 16)
        def _(i):
            body(i * 16)

    def line(self, row):
        return pl.ds(pl.multiple_of(row, 16), 16)

    def a_start(self, u):
        @pl.when(u >= self.slots)
        def _():
            pl.semaphore_wait(self.free, 1)
        self.a_copy(u).start()

    def a_stage(self, u):
        held, slot, c = self.held, self.slot(u), self.at.c
        self.a_copy(u).wait_recv()
        for z in range(self.nz):
            def add(row, z=z):
                row = self.line(row)
                held[slot, z, row, :] = self.plus(held[slot, z, row, :], self.grads[z, c, row, :])
            self.each(self.shard, add)
            if z == self.low - 1:
                self.bx_copy(u).start()
        self.by_copy(u).start()
        self.a_copy(u).wait_send()

    def b_stage(self, u):
        held, slot, at = self.held, self.slot(u), self.at
        self.bx_copy(u).wait_recv()
        self.bx_copy(u).wait_send()
        for z in range(self.low):
            def add(row, z=z):
                row, mine = self.line(row), self.cols(at.s)
                held[slot, z, row, mine] = self.plus(held[slot, z, row, mine], self.bx[u, z, row, :])
            self.each(self.shard, add)
        self.dy_copy(u).start()
        self.by_copy(u).wait_recv()
        self.by_copy(u).wait_send()
        for z in range(self.low):
            def add(row, z=z):
                spot, row = self.line(row), self.line(at.r * self.half + row)
                z2 = self.low + z
                held[slot, z2, row, :] = self.plus(held[slot, z2, row, :], self.by[u, z, spot, :])
            self.each(self.half, add)
        self.dx_copy(u).start()

    def d_stage(self, u):
        held, slot, at = self.held, self.slot(u), self.at
        for copy in (self.dy_copy(u), self.dx_copy(u)):
            copy.wait_recv()
            copy.wait_send()
        for z in range(self.nz):
            came = self.dy if z < self.low else self.dx

            def add(row, z=z, came=came):
                spot, row = self.line(row), self.line(at.r * self.half + row)
                mine = self.cols(at.s)
                held[slot, z, row, mine] = self.plus(held[slot, z, row, mine], came[u, z % self.low, spot, :])
            self.each(self.half, add)
        for d in self.steps:
            self.z_copy(u, d).start()

    def z_stage(self, u):
        slot, at = self.slot(u), self.at
        for d in self.steps:
            self.z_copy(u, d).wait_recv()
            self.z_copy(u, d).wait_send()

        def add(row):
            spot, row = self.line(row), self.line(at.r * self.half + row)
            came = [self.cz[u, d - 1, spot, :] for d in self.steps]
            self.total[u, spot, :] = self.plus(self.held[slot, at.z, row, self.cols(at.s)], *came)
        self.each(self.half, add)

        @pl.when(u + self.slots < self.units)
        def _():
            pl.semaphore_signal(self.free, inc=1, device_id=at.core(), device_id_type=MESH)
        self.put_copy(u).start()
        self.px_copy(u).start()
        self.py_copy(u).start()

    def forward(self, u):
        self.px_copy(u).wait_recv()
        self.gy_copy(u).start()
        self.py_copy(u).wait_recv()
        self.gx_copy(u).start()

    def close(self, u):
        self.put_copy(u).wait()
        self.px_copy(u).wait_send()
        self.py_copy(u).wait_send()
        self.gx_copy(u).wait()
        self.gy_copy(u).wait()

    def step(self, i):
        def stage(lag, work):
            u = i - lag
            pl.when((u >= 0) & (u < self.units))(lambda: work(u))

        stage(0, self.a_start)
        stage(2, self.d_stage)
        stage(3, self.z_stage)
        stage(4, self.forward)
        stage(0, self.a_stage)
        stage(1, self.b_stage)
        stage(5, self.close)

    def tiny_copy(self, n, peer):
        return remote(self.tiny, self.tiny_in.at[n], self.ts.at[n], self.tr.at[n], peer)

    def tiny_z(self, d):
        return remote(self.tiny, self.tiny_in.at[2 + d], self.ts.at[2 + d], self.tr.at[2 + d], self.at.to(d))

    def tiny_step(self, n):
        peers = (self.at.core(), self.at.x(), self.at.y())
        if 0 < n <= 3:
            copy = self.tiny_copy(n - 1, peers[n - 1])
            copy.wait()
            self.tiny[...] = self.tiny[...] + self.tiny_in[n - 1]
        if n < 3:
            self.tiny_copy(n, peers[n]).start()
        if n == 3:
            for d in self.steps:
                self.tiny_z(d).start()
        if n == 4:
            for d in self.steps:
                self.tiny_z(d).wait()
            self.tiny_out[...] = self.tiny[...] + sum(self.tiny_in[2 + d] for d in self.steps)


def backward_kernel(nz, layers, length, total, *refs):
    cot_ref, full_ref, vec, bias_ref = refs[:4]
    per = 11
    saved = [refs[4 + per * l : 4 + per * (l + 1)] for l in range(layers)]
    refs = refs[4 + per * layers :]
    share_ref, tiny_out, input_ref = refs[:3]
    (
        up, wide_a, wide_b, hidden, mixed, pre_low, low, q, k, v, att, do, lse, weight, came, sent,
        load_sem, weight_sem, x_sem, tiny, grads,
    ) = refs[3:24]
    units = layers * UNITS
    reduce = Reduce(nz, units, share_ref, tiny, tiny_out, grads, *refs[24:])
    at = reduce.at
    width = up.shape[1]
    wide, half_z = width // 2, nz // 2
    shard = reduce.shard
    names = ("current", "normed_t", "q", "k", "v", "lse", "att", "after", "mixed", "pre", "hidden")
    homes = dict(
        normed_t=att, q=q, k=k, v=v, lse=lse, att=att, after=wide_b, mixed=mixed, pre=wide_a, hidden=hidden
    )

    def load(l, name):
        n = names.index(name)
        source = saved[l][n]
        home = homes.get(name, hidden if source.dtype == jnp.bfloat16 else wide_b)
        if home.shape != source.shape:
            if len(source.shape) == 3:
                home = home.at[:, :, pl.ds(0, source.shape[2])]
            elif source.shape[0] != home.shape[0]:
                home = home.at[pl.ds(0, source.shape[0]), :]
            else:
                home = home.at[:, pl.ds(0, source.shape[1])]
        return pltpu.make_async_copy(source, home, load_sem.at[l, n])

    def fetch(u):
        return pltpu.make_async_copy(full_ref.at[u], weight, weight_sem.at[0])

    def fill(product):
        @pl.loop(0, 2)
        def _(i):
            @pl.loop(0, 2)
            def _(j):
                r = pl.ds(pl.multiple_of(i * wide, 128), wide)
                c = pl.ds(pl.multiple_of(j * wide, 128), wide)
                value = product(r, c).astype(jnp.bfloat16).reshape(half_z, 2, shard, wide)
                grads[pl.ds(i * half_z, half_z), :, :, c] = value

    def vector(n):
        return vec[n : n + 1, :]

    def gather_row(n, values):
        tiny[n : n + 1, :] = tiny[n : n + 1, :] + jnp.sum(values, axis=0, keepdims=True)

    def norm_tile(values, gain, w, n):
        inverse = lax.rsqrt(jnp.mean(values * values, axis=-1, keepdims=True) + EPSILON)
        scaled = w * gain
        inner = jnp.mean(values * scaled, axis=-1, keepdims=True)
        gather_row(n, w * values * inverse)
        return inverse * scaled - values * (inverse * inverse * inverse) * inner

    def count(l):
        return length if l == layers - 1 else total

    def next_load(l, *which):
        if l > 0:
            for name in which:
                load(l - 1, name).start()

    def down(l):
        m = count(l)
        load(l, "hidden").wait()

        def body(r):
            value = up[r, :].astype(jnp.bfloat16)
            low[r, :] = value
            gather_row(3 * layers + l, value.astype(jnp.float32))
        each_tile(m, body)
        fill(lambda r, c: dot_tn(hidden[:m, r], low[:m, c]))
        if saved[l][0].dtype == jnp.bfloat16:
            load(l, "current").start()
        else:
            next_load(l, "hidden")

    def expand(l):
        m = count(l)
        fetch(l * UNITS + 5).wait()
        load(l, "pre").wait()

        def body(r):
            grown = dot_nt(low[r, :], weight[...])
            value = wide_a[r, :]
            gate = 1.0 / (1.0 + jnp.exp(-value))
            result = (grown * gate * (1.0 + value * (1.0 - gate))).astype(jnp.bfloat16)
            pre_low[r, :] = result
            gather_row(2 * layers + l, result.astype(jnp.float32))
        each_tile(m, body)
        fetch(l * UNITS + 4).start()
        load(l, "mixed").wait()
        fill(lambda r, c: dot_tn(mixed[:m, r], pre_low[:m, c]))
        next_load(l, "mixed")

    def output(l):
        m = count(l)
        fetch(l * UNITS + 4).wait()
        load(l, "after").wait()
        gain = vector(2 * l + 1)

        def body(r):
            w = dot_nt(pre_low[r, :], weight[...])
            value = up[r, :] + norm_tile(wide_b[r, :], gain, w, 2 * l + 1)
            up[r, :] = value
            low[r, :] = value.astype(jnp.bfloat16)
        each_tile(m, body)
        fetch(l * UNITS + 3).start()
        if saved[l][0].dtype != jnp.bfloat16:
            load(l, "current").start()
        load(l, "att").wait()
        fill(lambda r, c: dot_nn(att[r, :m], low[:m, c]))
        load(l, "normed_t").start()

    def attention(l):
        m = count(l)
        fetch(l * UNITS + 3).wait()

        def body(r):
            do[r, :m] = dot_nt(weight[r, :], low[:m, :]).astype(jnp.bfloat16)
        each_tile(width, body)
        fetch(l * UNITS + 1).start()
        for name in ("q", "k", "v", "lse"):
            load(l, name).wait()
        row = 4 * layers + l
        factor = jnp.broadcast_to(vec[row : row + 1, 0:128], (128, 128)).T[0:HEAD, 0:1]

        def head(h, sums):
            rows = head_rows(h)
            kh, vh, qh, oh = k[rows, :], v[rows, :], q[rows, :m], do[rows, :m]
            scores = dot_tn(kh, qh) + bias_ref[:, :m]
            probs = jnp.exp(scores - lse[h, :, :m])
            weighted = probs * dot_tn(vh, oh)
            inner = jnp.sum(weighted, axis=0, keepdims=True)
            score = (weighted - probs * inner).astype(jnp.bfloat16)
            v[rows, :] = dot_nt(oh, probs.astype(jnp.bfloat16)).astype(jnp.bfloat16)
            k[rows, :] = dot_nt(qh, score).astype(jnp.bfloat16)
            query = dot_nn(kh, score)
            q[rows, :m] = (query * factor).astype(jnp.bfloat16)
            return sums + jnp.sum(query * qh.astype(jnp.float32), axis=1, keepdims=True)

        sums = lax.fori_loop(0, HEADS, head, jnp.zeros((HEAD, 1), jnp.float32))
        flat = jnp.broadcast_to(sums, (HEAD, 128)).T
        tiny[row : row + 1, 0:HEAD] = flat[0:1, :]
        next_load(l, "lse")

    def project(l, n):
        source = (k, v, q)[n]
        m = total if n < 2 else count(l)
        if n == 0:
            attention(l)
            load(l, "normed_t").wait()
        fill(lambda r, c: dot_nt(att[r, :m], source[c, :m]))
        fetch(l * UNITS + (1, 2, 0)[n]).wait()
        if n == 2:
            load(l, "current").wait()
        gain = vector(2 * l)
        current = hidden if saved[l][0].dtype == jnp.bfloat16 else wide_b

        def body(r):
            value = dot_nt(source[:, r].T, weight[...])
            if n > 0:
                value = value + wide_a[r, :]
            wide_a[r, :] = value
        each_tile(m, body)
        if n < 2:
            fetch(l * UNITS + (2, 0)[n]).start()
            return
        if l > 0:
            fetch((l - 1) * UNITS + 5).start()

        def close(r):
            return norm_tile(current[r, :].astype(jnp.float32), gain, wide_a[r, :], 2 * l)

        own = count(l)

        def first(r):
            up[r, :] = up[r, :] + close(r)
        each_tile(own, first)
        if own < total:
            @pl.loop(own // ROWS, total // ROWS)
            def _(i):
                r = pl.ds(pl.multiple_of(i * ROWS, ROWS), ROWS)
                up[r, :] = close(r)
        next_load(l, "pre", "after", "att", "q", "k", "v")
        if l == 0:
            sent[...] = up[length:, :].astype(jnp.bfloat16)
            reply.start()

    reply = remote(sent, came, x_sem.at[0], x_sem.at[1], at.x())
    work = (
        down, expand, output,
        lambda l: project(l, 0), lambda l: project(l, 1), lambda l: project(l, 2),
    )
    last = layers - 1
    start_copy = pltpu.make_async_copy(cot_ref, sent, x_sem.at[2])
    start_copy.start()
    for name in ("hidden", "pre", "mixed", "after", "att", "q", "k", "v", "lse"):
        load(last, name).start()
    fetch(last * UNITS + 5).start()
    tiny[...] = jnp.zeros_like(tiny)
    at.greet()
    start_copy.wait()
    up[:length, :] = sent[...].astype(jnp.float32)

    @pl.loop(0, reduce.iterations)
    def _(i):
        for n in range(units):
            @pl.when(i == n)
            def _(n=n):
                work[n % UNITS](last - n // UNITS)
        reduce.step(i)
        for n in range(5):
            @pl.when(i == units + n)
            def _(n=n):
                reduce.tiny_step(n)
                if n == 2:
                    reply.wait()
                    input_ref[...] = (up[:length, :] + came[...].astype(jnp.float32)).astype(jnp.bfloat16)


def backward_pass(nz, cotangent, full, vec, bias, saved):
    layers = len(saved)
    units = layers * UNITS
    length, width = cotangent.shape
    total = bias.shape[0]
    shard = width // (2 * nz)
    half, wide, low, n = shard // 2, width // 2, nz // 2, nz - 1
    slots = min(5, units)
    flat = [one for group in saved for one in group]
    rows = vec.shape[0]
    dma = pltpu.SemaphoreType.DMA
    small, large = jnp.bfloat16, jnp.float32
    anywhere = pl.BlockSpec(memory_space=pl.ANY)
    inside = pl.BlockSpec(memory_space=pltpu.VMEM)
    natural, turned = (total, width), (width, total)
    return pl.pallas_call(
        functools.partial(backward_kernel, nz, layers, length, total),
        out_shape=(
            jax.ShapeDtypeStruct((units, shard, width), small),
            jax.ShapeDtypeStruct((rows, width), large),
            jax.ShapeDtypeStruct((length, width), small),
        ),
        in_specs=[anywhere, anywhere, inside, inside] + [anywhere] * len(flat),
        out_specs=(anywhere, inside, inside),
        scratch_shapes=[
            pltpu.VMEM(natural, large),
            pltpu.VMEM(natural, large),
            pltpu.VMEM(natural, large),
            pltpu.VMEM(natural, small),
            pltpu.VMEM(natural, small),
            pltpu.VMEM(natural, small),
            pltpu.VMEM(natural, small),
            pltpu.VMEM(turned, small),
            pltpu.VMEM(turned, small),
            pltpu.VMEM(turned, small),
            pltpu.VMEM(turned, small),
            pltpu.VMEM(turned, small),
            pltpu.VMEM((HEADS, 1, total), large),
            pltpu.VMEM((width, width), small),
            pltpu.VMEM((length, width), small),
            pltpu.VMEM((length, width), small),
            dma((layers, 11)),
            dma((1,)),
            dma((3,)),
            pltpu.VMEM((rows, width), large),
            pltpu.VMEM((nz, 2, shard, width), small),
            pltpu.VMEM((slots, nz, shard, width), small),
            pltpu.VMEM((units, low, shard, wide), small),
            pltpu.VMEM((units, low, half, width), small),
            pltpu.VMEM((units, low, half, wide), small),
            pltpu.VMEM((units, low, half, wide), small),
            pltpu.VMEM((units, n, half, wide), small),
            pltpu.VMEM((units, half, wide), small),
            pltpu.VMEM((3 + n, rows, width), large),
            dma((units,)), dma((units,)),
            dma((units, 2)), dma((units, 2)),
            dma((units, 2)), dma((units, 2)),
            dma((units, n)), dma((units, n)),
            dma((units,)),
            dma((units, 4)), dma((units, 4)),
            dma((3 + n,)), dma((3 + n,)),
            pltpu.SemaphoreType.REGULAR,
        ],
        compiler_params=pltpu.CompilerParams(
            collective_id=2, has_side_effects=True, vmem_limit_bytes=63 << 20
        ),
    )(cotangent, full, vec, bias, *flat)


def forward_layer(current, weights, allowed, series_count, local_length, total_length):
    qkv_weight, out_weight, up_weight, down_weight, norm_gains, up_bias, down_bias, query_scale = (
        weights
    )
    token_count, model_width = current.shape
    normed, inverse_one = norm_rows(current, norm_gains[0].astype(jnp.float32))
    normed_low = normed.astype(jnp.bfloat16).reshape(series_count, local_length, model_width)
    projected = jnp.einsum(
        "bld,kdc->bkcl", normed_low, qkv_weight, preferred_element_type=jnp.float32
    ).reshape(series_count, 3 * model_width, local_length)
    query_raw = projected[:, :model_width]
    factor = query_factor(query_scale)
    query_low = (
        query_raw.reshape(series_count, HEADS, HEAD, local_length) * factor[None, None, :, None]
    ).astype(jnp.bfloat16)
    pair_low = projected[:, model_width:].astype(jnp.bfloat16)
    pair_all = lax.all_gather(pair_low, "seq", axis=2, tiled=True)
    key_all = pair_all[:, :model_width].reshape(series_count, HEADS, HEAD, total_length)
    value_all = pair_all[:, model_width:].reshape(series_count, HEADS, HEAD, total_length)
    scores = jnp.einsum("bheq,bhek->bhqk", query_low, key_all, preferred_element_type=jnp.float32)
    scores = jnp.where(allowed[:, None], scores, NEG_FILL)
    top_score = jnp.max(scores, axis=-1, keepdims=True)
    exp_scores = jnp.exp(scores - top_score)
    exp_total = jnp.sum(exp_scores, axis=-1, keepdims=True)
    probs_low = (exp_scores / exp_total).astype(jnp.bfloat16)
    log_total = top_score + jnp.log(exp_total)
    attended = jnp.einsum(
        "bhqk,bhek->bheq", probs_low, value_all, preferred_element_type=jnp.float32
    )
    attended_low = attended.astype(jnp.bfloat16).reshape(series_count, model_width, local_length)
    attn_out = jnp.einsum(
        "bdl,de->ble", attended_low, out_weight, preferred_element_type=jnp.float32
    )
    after_attn = current + attn_out.reshape(token_count, model_width)
    normed_two, inverse_two = norm_rows(after_attn, norm_gains[1].astype(jnp.float32))
    mixed_low = normed_two.astype(jnp.bfloat16)
    hidden_pre = jnp.dot(mixed_low, up_weight, preferred_element_type=jnp.float32) + up_bias.astype(
        jnp.float32
    )
    hidden_low = jax.nn.silu(hidden_pre).astype(jnp.bfloat16)
    result = after_attn + (
        jnp.dot(hidden_low, down_weight, preferred_element_type=jnp.float32)
        + down_bias.astype(jnp.float32)
    )
    stored = (
        current,
        inverse_one,
        normed_low,
        query_raw,
        query_low,
        key_all,
        value_all,
        log_total,
        attended_low,
        after_attn,
        inverse_two,
        mixed_low,
        hidden_pre,
        hidden_low,
    )
    return (result, stored)


def backward_layer(upstream, weights, stored, allowed, series_count, local_length, total_length):
    qkv_weight, out_weight, up_weight, down_weight, norm_gains, up_bias, down_bias, query_scale = (
        weights
    )
    (
        current,
        inverse_one,
        normed_low,
        query_raw,
        query_low,
        key_all,
        value_all,
        log_total,
        attended_low,
        after_attn,
        inverse_two,
        mixed_low,
        hidden_pre,
        hidden_low,
    ) = stored
    token_count, model_width = current.shape
    down_low = upstream.astype(jnp.bfloat16)
    grad_down_bias = jnp.sum(down_low, axis=0, dtype=jnp.float32)
    grad_down = jnp.einsum("tf,td->fd", hidden_low, down_low, preferred_element_type=jnp.float32)
    hidden_grad = jnp.einsum("td,fd->tf", down_low, down_weight, preferred_element_type=jnp.float32)
    sigmoid_pre = jax.nn.sigmoid(hidden_pre)
    pre_low = (hidden_grad * sigmoid_pre * (1.0 + hidden_pre * (1.0 - sigmoid_pre))).astype(
        jnp.bfloat16
    )
    grad_up_bias = jnp.sum(pre_low, axis=0, dtype=jnp.float32)
    grad_up = jnp.einsum("td,tf->df", mixed_low, pre_low, preferred_element_type=jnp.float32)
    mixed_grad = jnp.einsum("tf,df->td", pre_low, up_weight, preferred_element_type=jnp.float32)
    norm_grad_two, gain_grad_two = norm_back(
        after_attn, inverse_two, norm_gains[1].astype(jnp.float32), mixed_grad
    )
    attn_grad = upstream + norm_grad_two
    branch_low = attn_grad.astype(jnp.bfloat16).reshape(series_count, local_length, model_width)
    grad_out = jnp.einsum(
        "bdl,ble->de", attended_low, branch_low, preferred_element_type=jnp.float32
    )
    output_low = (
        jnp.einsum("ble,de->bdl", branch_low, out_weight, preferred_element_type=jnp.float32)
        .astype(jnp.bfloat16)
        .reshape(series_count, HEADS, HEAD, local_length)
    )
    scores = jnp.einsum("bheq,bhek->bhqk", query_low, key_all, preferred_element_type=jnp.float32)
    scores = jnp.where(allowed[:, None], scores, NEG_FILL)
    attn_probs = jnp.exp(scores - log_total)
    prob_grad = jnp.einsum(
        "bheq,bhek->bhqk", output_low, value_all, preferred_element_type=jnp.float32
    )
    row_inner = jnp.sum(attn_probs * prob_grad, axis=-1, keepdims=True)
    score_low = (attn_probs * (prob_grad - row_inner)).astype(jnp.bfloat16)
    value_grad = jnp.einsum(
        "bhqk,bheq->bhek",
        attn_probs.astype(jnp.bfloat16),
        output_low,
        preferred_element_type=jnp.float32,
    )
    key_grad = jnp.einsum(
        "bhqk,bheq->bhek", score_low, query_low, preferred_element_type=jnp.float32
    )
    query_grad = jnp.einsum(
        "bhqk,bhek->bheq", score_low, key_all, preferred_element_type=jnp.float32
    )
    pair_grad = jnp.concatenate(
        [
            key_grad.reshape(series_count, model_width, total_length),
            value_grad.reshape(series_count, model_width, total_length),
        ],
        axis=1,
    )
    pair_local = lax.psum_scatter(pair_grad, "seq", scatter_dimension=2, tiled=True)
    key_local, value_local = pair_local[:, :model_width], pair_local[:, model_width:]
    factor = query_factor(query_scale)
    factor_grad = jnp.sum(
        query_grad * query_raw.reshape(series_count, HEADS, HEAD, local_length), axis=(0, 1, 3)
    )
    grad_scale = (
        factor_grad * jax.nn.sigmoid(query_scale.astype(jnp.float32)) * (SOFT_ONE / math.sqrt(HEAD))
    )
    raw_low = (
        (query_grad * factor[None, None, :, None])
        .astype(jnp.bfloat16)
        .reshape(series_count, model_width, local_length)
    )
    projected_grad = jnp.concatenate(
        [raw_low, key_local.astype(jnp.bfloat16), value_local.astype(jnp.bfloat16)], axis=1
    )
    grad_qkv = jnp.einsum(
        "bld,bcl->dc", normed_low, projected_grad, preferred_element_type=jnp.float32
    )
    normed_grad = jnp.einsum(
        "bkcl,kdc->bld",
        projected_grad.reshape(series_count, 3, model_width, local_length),
        qkv_weight,
        preferred_element_type=jnp.float32,
    ).reshape(token_count, model_width)
    norm_grad_one, gain_grad_one = norm_back(
        current, inverse_one, norm_gains[0].astype(jnp.float32), normed_grad
    )
    result = attn_grad + norm_grad_one
    layer_grads = (
        grad_qkv,
        grad_out,
        grad_up,
        grad_down,
        jnp.stack([gain_grad_one, gain_grad_two]),
        grad_up_bias,
        grad_down_bias,
        grad_scale,
    )
    return (result, layer_grads)


def pack_small(norm_gains, up_bias, down_bias, query_scale):
    layers, _, shard = norm_gains.shape
    scale = jnp.pad(query_scale, ((0, 0), (0, shard - query_scale.shape[1])))
    rows = jnp.concatenate([norm_gains.reshape(2 * layers, shard), up_bias, down_bias, scale])
    return jnp.pad(rows, ((0, -rows.shape[0] % 16), (0, -shard % 128)))


def unpack_small(tiny, layers, shard, scale_shard):
    count = tiny.shape[0]
    vectors = tiny[:, : 4 * layers, :shard].transpose(1, 0, 2).reshape(4 * layers, count * shard)
    scale = tiny[:, 4 * layers : 5 * layers, :scale_shard].transpose(1, 0, 2).reshape(layers, count * scale_shard)
    gains = vectors[: 2 * layers].reshape(layers, 2, count * shard)
    return gains, vectors[2 * layers : 3 * layers], vectors[3 * layers :], scale


def pack_tiny(layer_grads, count):
    gains = jnp.concatenate([g[4] for g in layer_grads])
    vectors = jnp.concatenate(
        [gains, jnp.stack([g[5] for g in layer_grads]), jnp.stack([g[6] for g in layer_grads])]
    )
    scale = jnp.stack([g[7] for g in layer_grads])
    shard, part = vectors.shape[1] // count, scale.shape[1] // count
    vectors = vectors.reshape(-1, count, shard)
    scale = jnp.pad(scale.reshape(-1, count, part), ((0, 0), (0, 0), (0, shard - part)))
    rows = jnp.concatenate([vectors, scale]).transpose(1, 0, 2)
    return jnp.pad(rows, ((0, 0), (0, -rows.shape[1] % 16), (0, -shard % 128)))


def unpack_tiny(tiny, layers, shard, part):
    gains = tiny[: 2 * layers, :shard].reshape(layers, 2, shard)
    up, down = tiny[2 * layers : 3 * layers, :shard], tiny[3 * layers : 4 * layers, :shard]
    return gains, up, down, tiny[4 * layers : 5 * layers, :part]


def gather_plain(qkv_weight, out_weight, up_weight, down_weight, small):
    layers, shard, width = out_weight.shape
    qkv = qkv_weight.reshape(layers, shard, 3, width).transpose(0, 2, 1, 3)
    square = jnp.stack([out_weight, up_weight, down_weight], axis=1)
    units = jnp.concatenate([qkv, square], axis=1).reshape(layers * UNITS, shard, width)
    full = lax.all_gather(units, "fsdp", axis=1, tiled=True)
    return full, lax.all_gather(small, "fsdp", axis=0)


def reduce_plain(layer_grads, tiny):
    units = []
    for grads in layer_grads:
        width = grads[0].shape[1]
        units += list(grads[:3]) + [grads[3][:, k * width : (k + 1) * width] for k in range(3)]
    shares = lax.psum_scatter(jnp.stack(units), "fsdp", scatter_dimension=1, tiled=True)
    small = lax.psum_scatter(tiny, "fsdp", scatter_dimension=0, tiled=True)[0]
    return lax.psum(shares, ("replica", "seq")), lax.psum(small, ("replica", "seq"))


def plain(
    series_in,
    cotangent,
    qkv_weight,
    out_weight,
    up_weight,
    down_weight,
    norm_gains,
    up_bias,
    down_bias,
    query_scale,
    pad_length,
    span_starts,
    span_count,
):
    series_count, local_length, model_width = series_in.shape
    seq_count = lax.axis_size("seq")
    group = lax.axis_size("fsdp")
    total_length = local_length * seq_count
    offset = lax.axis_index("seq") * local_length
    allowed = visible(pad_length, span_starts, span_count, offset, local_length, total_length)
    layer_count, shard = qkv_weight.shape[:2]
    scale_shard = query_scale.shape[1]
    small = pack_small(norm_gains, up_bias, down_bias, query_scale)
    full, tiny = gather_plain(qkv_weight, out_weight, up_weight, down_weight, small)
    gains, up_full, down_full, scale_full = unpack_small(tiny, layer_count, shard, scale_shard)
    weights = [
        (
            full[UNITS * l : UNITS * l + 3],
            full[UNITS * l + 3],
            full[UNITS * l + 4],
            full[UNITS * l + 5],
            gains[l],
            up_full[l],
            down_full[l],
            scale_full[l],
        )
        for l in range(layer_count)
    ]
    current = series_in.reshape(series_count * local_length, model_width).astype(jnp.float32)
    stored_list = []
    for l in range(layer_count):
        current, stored = forward_layer(
            current, weights[l], allowed, series_count, local_length, total_length
        )
        stored_list.append(stored)
    series_out = current.reshape(series_count, local_length, model_width).astype(jnp.bfloat16)
    upstream = cotangent.reshape(series_count * local_length, model_width).astype(jnp.float32)
    order = list(reversed(range(layer_count)))
    grads_list = {}
    for l in order:
        upstream, grads_list[l] = backward_layer(
            upstream, weights[l], stored_list[l], allowed, series_count, local_length, total_length
        )
    tiny_grads = pack_tiny([grads_list[l] for l in range(layer_count)], group)
    big = [
        tuple(grads_list[l][k].astype(jnp.bfloat16) for k in (3, 2, 1, 0)) for l in order
    ]
    shares, tiny_sum = reduce_plain(big, tiny_grads)
    shares = shares.reshape(layer_count, UNITS, shard, model_width)[::-1]
    grad_gains, grad_up_bias, grad_down_bias, grad_scale = unpack_tiny(
        tiny_sum, layer_count, shard, scale_shard
    )
    grad_qkv = shares[:, 3:].transpose(0, 2, 1, 3).reshape(layer_count, shard, 3 * model_width)
    input_grad = upstream.reshape(series_count, local_length, model_width).astype(jnp.bfloat16)
    return (
        series_out,
        input_grad,
        grad_qkv.astype(jnp.float32),
        shares[:, 2].astype(jnp.float32),
        shares[:, 1].astype(jnp.float32),
        shares[:, 0].astype(jnp.float32),
        grad_gains,
        grad_up_bias,
        grad_down_bias,
        grad_scale,
    )


def finish(shares, tiny, layers, shard, width, query_scale):
    shares = shares.reshape(layers, UNITS, shard, width)[::-1]
    low = jnp.float32
    place = lax.axis_index("fsdp")
    part = query_scale.shape[1]
    vectors = lax.dynamic_slice_in_dim(tiny[: 4 * layers], place * shard, shard, axis=1)
    scale = lax.dynamic_slice_in_dim(tiny[4 * layers : 5 * layers], place * part, part, axis=1)
    raw = query_scale.astype(jnp.float32)
    scale = scale * (jax.nn.sigmoid(raw) * (SOFT_ONE / math.sqrt(HEAD))) / query_factor(query_scale)
    qkv = jnp.concatenate([shares[:, 5], shares[:, 3], shares[:, 4]], axis=2)
    return (
        qkv.astype(low),
        shares[:, 2].astype(low),
        shares[:, 1].astype(low),
        shares[:, 0].astype(low),
        vectors[: 2 * layers].reshape(layers, 2, shard),
        vectors[2 * layers : 3 * layers],
        vectors[3 * layers :],
        scale,
    )


def fused(
    series_in,
    cotangent,
    qkv_weight,
    out_weight,
    up_weight,
    down_weight,
    norm_gains,
    up_bias,
    down_bias,
    query_scale,
    pad_length,
    span_starts,
    span_count,
):
    length = series_in.shape[1]
    layers, shard, width = out_weight.shape
    nz = lax.axis_size("fsdp") // 2
    small = pack_small(norm_gains, up_bias, down_bias, query_scale)
    bias = pair_bias(pad_length, span_starts, span_count, length)
    full, vec, series_out, saved = forward_pass(
        nz, series_in[0], qkv_weight, out_weight, up_weight, down_weight, small, bias, query_scale.shape[1]
    )
    shares, tiny, input_grad = backward_pass(nz, cotangent[0], full, vec, bias, saved)
    rest = finish(shares, tiny, layers, shard, width, query_scale)
    return (series_out[None], input_grad[None]) + rest


def shards(*args):
    series_in, out_weight = args[0], args[3]
    group = lax.axis_size("fsdp")
    width = series_in.shape[2]
    block = lax.axis_size("replica") == 2 and lax.axis_size("seq") == 2 and group % 4 == 0
    block = block and series_in.shape[0] == 1 and width == out_weight.shape[2] == HEADS * HEAD
    block = block and (width // group) % 32 == 0 and width % 256 == 0
    return fused(*args) if block else plain(*args)


def solution(mesh):
    return jax.shard_map(
        shards,
        mesh=mesh,
        in_specs=(
            P(("replica", "fsdp"), "seq", None),
            P(("replica", "fsdp"), "seq", None),
            P(None, "fsdp", None),
            P(None, "fsdp", None),
            P(None, "fsdp", None),
            P(None, "fsdp", None),
            P(None, None, "fsdp"),
            P(None, "fsdp"),
            P(None, "fsdp"),
            P(None, "fsdp"),
            P(("replica", "fsdp")),
            P(("replica", "fsdp"), None),
            P(("replica", "fsdp")),
        ),
        out_specs=(
            P(("replica", "fsdp"), "seq", None),
            P(("replica", "fsdp"), "seq", None),
            P(None, "fsdp", None),
            P(None, "fsdp", None),
            P(None, "fsdp", None),
            P(None, "fsdp", None),
            P(None, None, "fsdp"),
            P(None, "fsdp"),
            P(None, "fsdp"),
            P(None, "fsdp"),
        ),
        check_vma=False,
    )
```

```python
import functools
import math

import jax
import jax.numpy as jnp
from jax import lax
from jax.experimental import pallas as pl
from jax.experimental.pallas import tpu as pltpu
from jax.sharding import PartitionSpec as P

HEADS = 16
HEAD = 80
SPAN = 32


EPSILON = 1e-06
SOFT_ONE = 1.442695041
NEG_FILL = -1e30


def visible(pad_length, span_starts, span_count, offset, local_length, total_length):
    query_pos = offset + jnp.arange(local_length, dtype=jnp.int32)
    key_pos = jnp.arange(total_length, dtype=jnp.int32)
    shared = jnp.zeros((span_starts.shape[0], local_length, total_length), dtype=bool)
    for slot_index in range(span_starts.shape[1]):
        slot_start = span_starts[:, slot_index]
        slot_used = slot_index < span_count
        query_in = (
            slot_used[:, None]
            & (query_pos[None, :] >= slot_start[:, None])
            & (query_pos[None, :] < slot_start[:, None] + SPAN)
        )
        key_in = (key_pos[None, :] >= slot_start[:, None]) & (
            key_pos[None, :] < slot_start[:, None] + SPAN
        )
        shared = shared | query_in[:, :, None] & key_in[:, None, :]
    causal = key_pos[None, :] <= query_pos[:, None]
    allowed = (key_pos[None, None, :] >= pad_length[:, None, None]) & (causal[None] | shared)
    return allowed | (key_pos[None, None, :] == query_pos[None, :, None])


def norm_rows(values, scale_gain):
    inverse = lax.rsqrt(jnp.mean(values * values, axis=-1, keepdims=True) + EPSILON)
    return (values * inverse * scale_gain, inverse)


def norm_back(values, inverse, scale_gain, upstream):
    scaled = upstream * scale_gain
    inner_term = jnp.mean(values * scaled, axis=-1, keepdims=True)
    result = inverse * scaled - values * (inverse * inverse * inverse) * inner_term
    return (result, jnp.sum(upstream * values * inverse, axis=0))


def query_factor(query_scale):
    return jax.nn.softplus(query_scale.astype(jnp.float32)) * (SOFT_ONE / math.sqrt(HEAD))


MESH = pl.DeviceIdType.MESH
UNITS = 6
LAG = 1


class Place:
    def __init__(self, nz):
        self.nz = nz
        self.r = lax.axis_index("replica")
        f = lax.axis_index("fsdp")
        self.s = lax.axis_index("seq")
        self.z = lax.div(f, 2)
        self.c = lax.rem(f, 2)
        self.f = f

    def x(self):
        return (self.r, self.f, 1 - self.s)

    def y(self):
        return (1 - self.r, self.f, self.s)

    def core(self):
        return (self.r, self.f + 1 - 2 * self.c, self.s)

    def to(self, d):
        return (self.r, lax.rem(self.z + d, self.nz) * 2 + self.c, self.s)

    def source(self, d):
        return lax.rem(self.z - d + self.nz, self.nz)

    def greet(self):
        barrier = pltpu.get_barrier_semaphore()
        peers = [self.x(), self.y(), self.core()] + [self.to(d) for d in range(1, self.nz)]
        for peer in peers:
            pl.semaphore_signal(barrier, inc=1, device_id=peer, device_id_type=MESH)
        pl.semaphore_wait(barrier, len(peers))


def remote(src, dst, send, recv, device):
    return pltpu.make_async_remote_copy(
        src_ref=src, dst_ref=dst, send_sem=send, recv_sem=recv, device_id=device, device_id_type=MESH
    )


class Gather:
    def __init__(
        self, nz, layers, qkv_ref, out_ref, up_ref, down_ref, small_ref, full_ref, tiny_ref,
        mine, local_sem, keep_sem, zs, zr, xs, xr, ys, yr, fxs, fxr, fys, fyr, cs, cr, ts, tr,
    ):
        self.__dict__.update(locals())
        self.at = Place(nz)
        self.shard, self.width = out_ref.shape[1], out_ref.shape[2]
        self.half, self.wide = self.shard // 2, self.width // 2
        self.units = layers * UNITS
        self.hops = nz - 1
        self.iterations = self.units + LAG * (self.hops + 2)

    def source(self, way, k):
        return self.at.z - way * k

    def comes(self, way, k):
        z = self.at.z
        return z >= k if way > 0 else z + k < self.nz

    def goes(self, way):
        z = self.at.z
        return z + 1 < self.nz if way > 0 else z >= 1

    def next(self, way):
        at = self.at
        return (at.r, 2 * (at.z + way) + at.c, at.s)

    def slot(self, way, k):
        return 2 * (k - 1) + (0 if way > 0 else 1)

    def block(self, u, z, c, r, s):
        row = pl.multiple_of((2 * z + c) * self.shard + r * self.half, 8)
        col = pl.multiple_of(s * self.wide, 128)
        return self.full_ref.at[u, pl.ds(row, self.half), pl.ds(col, self.wide)]

    def quarter(self, u, z, c, r, s, part):
        step = self.half // 2
        row = pl.multiple_of((2 * z + c) * self.shard + r * self.half + part * step, 8)
        col = pl.multiple_of(s * self.wide, 128)
        return self.full_ref.at[u, pl.ds(row, step), pl.ds(col, self.wide)]

    def own(self, u, c):
        row = pl.multiple_of((2 * self.at.z + c) * self.shard, 8)
        return self.full_ref.at[u, pl.ds(row, self.shard), :]

    def local(self, layer, k):
        if k < 3:
            piece = self.qkv_ref.at[layer, :, pl.ds(k * self.width, self.width)]
        else:
            piece = (self.out_ref, self.up_ref, self.down_ref)[k - 3].at[layer]
        u = layer * UNITS + k
        return pltpu.make_async_copy(piece, self.mine.at[u], self.local_sem.at[u])

    def keep(self, u):
        return pltpu.make_async_copy(self.mine.at[u], self.own(u, self.at.c), self.keep_sem.at[u])

    def z_copy(self, u, way, k):
        at, n = self.at, self.slot(way, k)
        piece = self.block(u, self.source(way, k - 1), at.c, at.r, at.s)
        held = piece
        if k == 1:
            row = pl.multiple_of(at.r * self.half, 16)
            held = self.mine.at[u, pl.ds(row, self.half), pl.ds(pl.multiple_of(at.s * self.wide, 128), self.wide)]
        return remote(held, piece, self.zs.at[u, n], self.zr.at[u, n], self.next(way))

    def z_came(self, u, way, k):
        at, n = self.at, self.slot(way, k)
        piece = self.block(u, self.source(way, k), at.c, at.r, at.s)
        return remote(piece, piece, self.zs.at[u, n], self.zr.at[u, n], self.next(way))

    def x_copy(self, u, way, k):
        at, n = self.at, self.slot(way, k)
        piece = self.block(u, self.source(way, k), at.c, at.r, at.s)
        return remote(piece, piece, self.xs.at[u, n], self.xr.at[u, n], at.x())

    def y_copy(self, u, way, k):
        at, n = self.at, self.slot(way, k)
        piece = self.block(u, self.source(way, k), at.c, at.r, at.s)
        return remote(piece, piece, self.ys.at[u, n], self.yr.at[u, n], at.y())

    def fx_copy(self, u, way, k):
        at, n = self.at, self.slot(way, k)
        piece = self.quarter(u, self.source(way, k), at.c, 1 - at.r, at.s, 1)
        return remote(piece, piece, self.fxs.at[u, n], self.fxr.at[u, n], at.x())

    def fy_copy(self, u, way, k):
        at, n = self.at, self.slot(way, k)
        piece = self.quarter(u, self.source(way, k), at.c, at.r, 1 - at.s, 0)
        return remote(piece, piece, self.fys.at[u, n], self.fyr.at[u, n], at.y())

    def core_own(self, u):
        own, n = self.own(u, self.at.c), 8 * self.hops
        return remote(self.mine.at[u], own, self.cs.at[u, n], self.cr.at[u, n], self.at.core())

    def core_copy(self, u, way, k, which):
        at = self.at
        r = at.r if which in (0, 1) else 1 - at.r
        s = at.s if which in (0, 2) else 1 - at.s
        piece = self.block(u, self.source(way, k), at.c, r, s)
        n = 4 * self.slot(way, k) + which
        return remote(piece, piece, self.cs.at[u, n], self.cr.at[u, n], at.core())

    def tiny(self, d):
        piece = self.tiny_ref.at[self.at.f]
        return remote(piece, piece, self.ts.at[d - 1], self.tr.at[d - 1], self.at.to(d))

    def tiny_core(self, d):
        piece, n = self.tiny_ref.at[2 * self.at.source(d) + self.at.c], self.nz - 1 + d
        return remote(piece, piece, self.ts.at[n], self.tr.at[n], self.at.core())

    def begin(self):
        self.tiny_ref[self.at.f] = self.small_ref[...]
        for layer in range(self.layers):
            for k in range(UNITS):
                self.local(layer, k).start()
        self.at.greet()
        for d in range(1, self.nz):
            self.tiny(d).start()
        self.tiny_core(0).start()

    def tiny_pass(self):
        for d in range(1, self.nz):
            self.tiny(d).wait_recv()
            self.tiny_core(d).start()

    def tiny_ready(self):
        for d in range(self.nz):
            self.tiny_core(d).wait_recv()

    def tiny_done(self):
        for d in range(1, self.nz):
            self.tiny(d).wait_send()
        for d in range(self.nz):
            self.tiny_core(d).wait_send()

    def when(self, cond, work):
        pl.when(cond)(work)

    def first(self, u):
        pltpu.make_async_copy(self.out_ref.at[0], self.mine.at[u], self.local_sem.at[u]).wait()
        self.keep(u).start()
        for way in (1, -1):
            self.when(self.goes(way), lambda way=way: self.z_copy(u, way, 1).start())
        self.core_own(u).start()

    def hop(self, u, k):
        for way in (1, -1):
            def work(way=way):
                self.z_came(u, way, k).wait_recv()
                if k < self.hops:
                    self.when(self.goes(way), lambda: self.z_copy(u, way, k + 1).start())
                self.x_copy(u, way, k).start()
                self.y_copy(u, way, k).start()
                self.core_copy(u, way, k, 0).start()
            self.when(self.comes(way, k), work)

    def forward(self, u, k):
        for way in (1, -1):
            def work(way=way):
                self.x_copy(u, way, k).wait_recv()
                self.fy_copy(u, way, k).start()
                self.core_copy(u, way, k, 1).start()
                self.y_copy(u, way, k).wait_recv()
                self.fx_copy(u, way, k).start()
                self.core_copy(u, way, k, 2).start()
            self.when(self.comes(way, k), work)

    def diagonal(self, u, k):
        for way in (1, -1):
            def work(way=way):
                self.fx_copy(u, way, k).wait_recv()
                self.fy_copy(u, way, k).wait_recv()
                self.core_copy(u, way, k, 3).start()
            self.when(self.comes(way, k), work)

    def step(self, i):
        def stage(lag, work):
            u = i - lag
            self.when((u >= 0) & (u < self.units), lambda: work(u))

        stage(0, self.first)
        for k in range(1, self.hops + 1):
            stage(LAG * k, lambda u, k=k: self.hop(u, k))
        for k in range(1, self.hops + 1):
            stage(LAG * (k + 1), lambda u, k=k: self.forward(u, k))
        for k in range(1, self.hops + 1):
            stage(LAG * (k + 2), lambda u, k=k: self.diagonal(u, k))

    def ready(self, u):
        self.keep(u).wait()
        self.core_own(u).wait_recv()
        for k in range(1, self.hops + 1):
            for way in (1, -1):
                def work(way=way, k=k):
                    for which in range(4):
                        self.core_copy(u, way, k, which).wait_recv()
                self.when(self.comes(way, k), work)

    def drain(self, u):
        self.core_own(u).wait_send()
        for k in range(1, self.hops + 1):
            for way in (1, -1):
                def sent(way=way, k=k):
                    self.z_copy(u, way, k).wait_send()
                came = self.goes(way)
                if k > 1:
                    came = came & self.comes(way, k - 1)
                self.when(came, sent)

                def work(way=way, k=k):
                    for copy in (self.x_copy, self.y_copy, self.fx_copy, self.fy_copy):
                        copy(u, way, k).wait_send()
                    for which in range(4):
                        self.core_copy(u, way, k, which).wait_send()
                self.when(self.comes(way, k), work)

    def finish(self):
        @pl.loop(0, self.units)
        def _(u):
            self.drain(u)

        self.tiny_done()


def gather_scratch(nz, layers, shard, width):
    units, n = layers * UNITS, 2 * (nz - 1)
    dma = pltpu.SemaphoreType.DMA
    return (
        [pltpu.VMEM((units, shard, width), jnp.bfloat16), dma((units,)), dma((units,))]
        + [dma((units, n))] * 10
        + [dma((units, 1 + 4 * n))] * 2
        + [dma((2 * nz,))] * 2
    )


def dot_nn(a, b):
    return jnp.dot(a, b, preferred_element_type=jnp.float32)


def dot_nt(a, b):
    return lax.dot_general(a, b, (((1,), (1,)), ((), ())), preferred_element_type=jnp.float32)


def dot_tn(a, b):
    return lax.dot_general(a, b, (((0,), (0,)), ((), ())), preferred_element_type=jnp.float32)


ROWS = 128
TALL = 256
BEGIN = 3


def each_tile(count, body, rows=ROWS):
    @pl.loop(0, count // rows)
    def _(i):
        body(pl.ds(pl.multiple_of(i * rows, rows), rows))


def head_rows(h):
    return pl.ds(pl.multiple_of(h * HEAD, 16), HEAD)


def row_norm(values, gain):
    inverse = lax.rsqrt(jnp.mean(values * values, axis=-1, keepdims=True) + EPSILON)
    return (values * inverse * gain).astype(jnp.bfloat16)


def expand_small(tiny_ref, vec_ref, layers, shard, part):
    width = vec_ref.shape[1]
    count = tiny_ref.shape[0]
    rows, lanes = tiny_ref.shape[1:]
    line = lax.broadcasted_iota(jnp.int32, (lanes, width), 0)
    column = lax.broadcasted_iota(jnp.int32, (lanes, width), 1)
    inner = lax.rem(column, HEAD)

    def place(f, sums):
        plain, scale = sums
        piece = tiny_ref[f]
        hot = jnp.where((column - f * shard == line) & (line < shard), 1.0, 0.0).astype(jnp.bfloat16)
        spread = jnp.where((inner - f * part == line) & (line < part), 1.0, 0.0).astype(jnp.bfloat16)
        return plain + dot_nn(piece, hot), scale + dot_nn(piece, spread)

    zero = jnp.zeros((rows, width), jnp.float32)
    plain, scale = lax.fori_loop(0, count, place, (zero, zero))
    soft = jnp.maximum(scale, 0.0) + jnp.log(1.0 + jnp.exp(-jnp.abs(scale)))
    row = lax.broadcasted_iota(jnp.int32, (rows, width), 0)
    vec_ref[...] = jnp.where(row < 4 * layers, plain, soft * (SOFT_ONE / math.sqrt(HEAD)))


def attend(heads, q_ref, k_ref, v_ref, bias_ref, out_ref, lse_ref):
    queries = q_ref.shape[1]

    @pl.loop(*heads)
    def _(h):
        rows = head_rows(h)
        scores = dot_tn(k_ref[rows, :], q_ref[rows, :]) + bias_ref[:, :queries]
        top = jnp.max(scores, axis=0, keepdims=True)
        grown = jnp.exp(scores - top)
        total = jnp.sum(grown, axis=0, keepdims=True)
        out = dot_nn(v_ref[rows, :], grown.astype(jnp.bfloat16)) * (1.0 / total)
        out_ref[rows, :] = out.astype(jnp.bfloat16)
        lse_ref[h] = top + jnp.log(total)


def forward_kernel(nz, layers, part, *refs):
    series_ref, qkv_ref, out_ref, up_ref, down_ref, small_ref, bias_ref = refs[:7]
    full_ref, vec_out, series_out = refs[7:10]
    per = 11
    saved = [refs[10 + per * l : 10 + per * (l + 1)] for l in range(layers)]
    refs = refs[10 + per * layers :]
    names = ("current", "normed_t", "q", "k", "v", "lse", "att", "after", "mixed", "pre", "hidden")
    held = [dict(zip(names, refs[per * l : per * (l + 1)])) for l in range(layers)]
    refs = refs[per * layers :]
    normed, weights, vec, last, tiny_ref, swap_sem, load_sem, save_sem = refs[:8]
    gather = Gather(
        nz, layers, qkv_ref, out_ref, up_ref, down_ref, small_ref, full_ref, tiny_ref, *refs[8:]
    )
    at = gather.at
    length = series_ref.shape[0]
    total = held[0]["normed_t"].shape[1]
    other = total - length

    own_copy = pltpu.make_async_copy(series_ref, held[0]["current"].at[pl.ds(0, length)], swap_sem.at[0])
    swap_copy = remote(
        series_ref, held[0]["current"].at[pl.ds(length, other)], swap_sem.at[1], swap_sem.at[2], at.x()
    )

    def save(l, n):
        return pltpu.make_async_copy(held[l][names[n]], saved[l][n], save_sem.at[l, n])

    def fetch(u):
        return pltpu.make_async_copy(full_ref.at[u], weights.at[u % 2], load_sem.at[u % 2])

    def arrived(u):
        fetch(u).wait()
        return weights.at[u % 2]

    def vector(n):
        return vec[n : n + 1, :]

    def normalize(l):
        b = held[l]
        gain = vector(2 * l)

        def body(r):
            values = row_norm(b["current"][r, :].astype(jnp.float32), gain)
            normed[r, :] = values
            b["normed_t"][:, r] = values.T
        each_tile(total, body)
        save(l, 1).start()

    def project(l, n):
        b = held[l]
        target = b[("q", "k", "v")[n]]
        weight = arrived(l * UNITS + n)

        def body(r):
            values = dot_nn(normed[r, :], weight[...])
            if n == 0:
                values = values * vector(4 * layers + l)
            target[:, r] = values.astype(jnp.bfloat16).T
        each_tile(target.shape[1], body)
        save(l, 2 + n).start()

    def attention(l, first):
        b = held[l]
        heads = (0, HEADS // 2) if first else (HEADS // 2, HEADS)
        attend(heads, b["q"], b["k"], b["v"], bias_ref, b["att"], b["lse"])
        if not first:
            save(l, 5).start()
            save(l, 6).start()

    def output(l):
        b = held[l]
        weight = arrived(l * UNITS + 3)
        gain = vector(2 * l + 1)

        def body(r):
            after = b["current"][r, :].astype(jnp.float32) + dot_tn(b["att"][:, r], weight[...])
            b["after"][r, :] = after
            b["mixed"][r, :] = row_norm(after, gain)
        each_tile(b["after"].shape[0], body)
        save(l, 7).start()
        save(l, 8).start()

    def expand(l):
        b = held[l]
        weight = arrived(l * UNITS + 4)
        bias = vector(2 * layers + l)

        def body(r):
            pre = dot_nn(b["mixed"][r, :], weight[...]) + bias
            b["pre"][r, :] = pre
            b["hidden"][r, :] = (pre * (1.0 / (1.0 + jnp.exp(-pre)))).astype(jnp.bfloat16)
        each_tile(b["pre"].shape[0], body)
        save(l, 9).start()
        save(l, 10).start()

    def contract(l):
        b = held[l]
        weight = arrived(l * UNITS + 5)
        bias = vector(3 * layers + l)

        def body(r):
            values = b["after"][r, :] + (dot_nn(b["hidden"][r, :], weight[...]) + bias)
            if l + 1 < layers:
                held[l + 1]["current"][r, :] = values
            else:
                last[r, :] = values.astype(jnp.bfloat16)
        each_tile(b["after"].shape[0], body)
        if l + 1 < layers:
            save(l + 1, 0).start()
            normalize(l + 1)
        else:
            pltpu.make_async_copy(last, series_out, swap_sem.at[3]).start()

    tasks = {}

    def add(i, work):
        tasks.setdefault(i, []).append(work)

    lag = gather.iterations - layers * UNITS

    def early():
        gather.tiny_pass()
        gather.tiny_ready()
        expand_small(tiny_ref, vec, layers, gather.shard, part)
        pltpu.make_async_copy(vec, vec_out, swap_sem.at[4]).start()

    def begin():
        own_copy.wait()
        swap_copy.wait_recv()
        save(0, 0).start()
        normalize(0)

    def pull(u):
        gather.ready(u)
        fetch(u).start()

    add(1, early)
    add(BEGIN, begin)
    units = layers * UNITS
    computing = []
    for l in range(layers):
        computing += [[lambda l=l, n=n: project(l, n)] for n in range(3)]
        computing[-1].append(lambda l=l: attention(l, True))
        computing.append([lambda l=l: attention(l, False), lambda l=l: output(l)])
        computing.append([lambda l=l: expand(l)])
        computing.append([lambda l=l: contract(l)])
    for u in range(units):
        add(u + lag, lambda u=u: pull(u))
        for one in computing[u]:
            add(min(u + lag + 1, gather.iterations - 1), one)

    own_copy.start()
    gather.begin()
    swap_copy.start()

    @pl.loop(0, gather.iterations)
    def _(i):
        gather.step(i)
        for when, work in sorted(tasks.items()):
            @pl.when(i == when)
            def _(work=work):
                for one in work:
                    one()

    swap_copy.wait_send()
    pltpu.make_async_copy(last, series_out, swap_sem.at[3]).wait()
    pltpu.make_async_copy(vec, vec_out, swap_sem.at[4]).wait()
    for l in range(layers):
        for n in range(per):
            save(l, n).wait()
    gather.finish()


def saved_shapes(layers, length, total, width):
    low, wide = jnp.bfloat16, jnp.float32
    shapes = []
    for l in range(layers):
        count = length if l == layers - 1 else total
        kind = low if l == 0 else wide
        shapes.append(
            [
                ((total, width), kind),
                ((width, total), low),
                ((width, count), low),
                ((width, total), low),
                ((width, total), low),
                ((HEADS, 1, count), wide),
                ((width, count), low),
                ((count, width), wide),
                ((count, width), low),
                ((count, width), wide),
                ((count, width), low),
            ]
        )
    return shapes


def forward_pass(nz, series, qkv_weight, out_weight, up_weight, down_weight, small, bias, part):
    layers, shard, width = out_weight.shape
    length, total = series.shape[0], bias.shape[0]
    units = layers * UNITS
    low, wide = jnp.bfloat16, jnp.float32
    shapes = [one for group in saved_shapes(layers, length, total, width) for one in group]
    dma = pltpu.SemaphoreType.DMA
    anywhere = pl.BlockSpec(memory_space=pl.ANY)
    inside = pl.BlockSpec(memory_space=pltpu.VMEM)
    count = 2 * nz
    results = pl.pallas_call(
        functools.partial(forward_kernel, nz, layers, part),
        out_shape=(
            jax.ShapeDtypeStruct((units, count * shard, width), low),
            jax.ShapeDtypeStruct((small.shape[0], width), wide),
            jax.ShapeDtypeStruct((length, width), low),
        )
        + tuple(jax.ShapeDtypeStruct(*one) for one in shapes),
        in_specs=[anywhere] * 5 + [inside] * 2,
        out_specs=(anywhere,) * (3 + len(shapes)),
        scratch_shapes=[pltpu.VMEM(*one) for one in shapes]
        + [
            pltpu.VMEM((total, width), low),
            pltpu.VMEM((2, width, width), low),
            pltpu.VMEM((small.shape[0], width), wide),
            pltpu.VMEM((length, width), low),
            pltpu.VMEM((count,) + small.shape, low),
            dma((5,)),
            dma((2,)),
            dma((layers, 11)),
        ]
        + gather_scratch(nz, layers, shard, width),
        compiler_params=pltpu.CompilerParams(
            collective_id=1, has_side_effects=True, vmem_limit_bytes=60 << 20
        ),
    )(series, qkv_weight, out_weight, up_weight, down_weight, small, bias)
    full, vec, out = results[:3]
    saved = [results[3 + 11 * l : 14 + 11 * l] for l in range(layers)]
    return full, vec, out, saved


def pair_bias(pad_length, span_starts, span_count, length):
    s = lax.axis_index("seq")
    place = jnp.arange(length, dtype=jnp.int32)
    position = jnp.concatenate([s * length + place, (1 - s) * length + place])
    key, query = position[:, None], position[None, :]
    seen = key <= query
    for slot in range(span_starts.shape[1]):
        start = span_starts[0, slot]
        inside = (position >= start) & (position < start + SPAN) & (slot < span_count[0])
        seen = seen | inside[:, None] & inside[None, :]
    allowed = (seen & (key >= pad_length[0])) | (key == query)
    return jnp.where(allowed, 0.0, NEG_FILL).astype(jnp.float32)


SLOTS = 10


class Reduce:
    def __init__(
        self, nz, units, full_ref, tiny, tiny_out, grads, held, bx, by, near, far, swap, tiny_in,
        as_, ar, bs, br, zs, zr, es, er, ls, ps, pr, ts, tr, free,
    ):
        self.__dict__.update(locals())
        self.at = Place(nz)
        self.slots, _, self.half, self.width = held.shape
        self.shard = 2 * self.half
        self.wide, self.low = self.width // 2, nz // 2
        self.steps = range(1, nz)
        self.parts = 2 * units
        self.iterations = self.parts + 5
        self.side = self.column(self.at.z)

    def column(self, z):
        return jnp.where(z < self.low, self.at.s, self.at.r)

    def cols(self, side):
        return pl.ds(pl.multiple_of(side * self.wide, 128), self.wide)

    def slot(self, h):
        return lax.rem(h, self.slots)

    def band(self, h):
        return pl.ds(pl.multiple_of(lax.rem(h, 2) * self.half, 16), self.half)

    def z_peer(self, d):
        at = self.at
        z = lax.rem(at.z + d, self.nz) if 2 * d == self.nz else at.z + 1 - 2 * lax.rem(at.z, 2)
        return z, (at.r, 2 * z + at.c, at.s)

    def pair_peer(self):
        at, first = self.at, self.at.z < self.low
        return (jnp.where(first, 1 - at.r, at.r), at.f, jnp.where(first, at.s, 1 - at.s))

    def last_peer(self):
        at, first = self.at, self.at.z < self.low
        return (jnp.where(first, at.r, 1 - at.r), at.f, jnp.where(first, 1 - at.s, at.s))

    def a_copy(self, h):
        piece = self.grads.at[:, 1 - self.at.c, self.band(h), :]
        return remote(piece, self.held.at[self.slot(h)], self.as_.at[h], self.ar.at[h], self.at.core())

    def bx_copy(self, h):
        piece = self.held.at[self.slot(h), pl.ds(0, self.low), :, self.cols(1 - self.at.s)]
        return remote(piece, self.bx.at[h], self.bs.at[h, 0], self.br.at[h, 0], self.at.x())

    def by_copy(self, h):
        piece = self.held.at[self.slot(h), pl.ds(self.low, self.low), :, self.cols(1 - self.at.r)]
        return remote(piece, self.by.at[h], self.bs.at[h, 1], self.br.at[h, 1], self.at.y())

    def near_copy(self, h, n):
        target = n * 2 + 1 - lax.rem(self.at.z, 2)
        side = (self.at.s, self.at.r)[n]
        piece = self.held.at[self.slot(h), target, :, self.cols(side)]
        return remote(piece, self.near.at[h, n], self.zs.at[h, n], self.zr.at[h, n], self.z_peer(1)[1])

    def far_copy(self, h):
        z, peer = self.z_peer(2)
        piece = self.held.at[self.slot(h), z, :, self.cols(self.column(z))]
        return remote(piece, self.far.at[h], self.zs.at[h, 2], self.zr.at[h, 2], peer)

    def pair_copy(self, h):
        piece = self.held.at[self.slot(h), self.at.z, :, self.cols(self.side)]
        return remote(piece, self.swap.at[h], self.es.at[h], self.er.at[h], self.pair_peer())

    def spot(self, h):
        return self.full_ref.at[lax.div(h, 2), self.band(h), self.cols(self.side)]

    def put_copy(self, h):
        return pltpu.make_async_copy(self.bx.at[h, 0], self.spot(h), self.ls.at[h])

    def last_copy(self, h):
        return remote(self.bx.at[h, 0], self.spot(h), self.ps.at[h], self.pr.at[h], self.last_peer())

    def plus(self, *values):
        return sum(v.astype(jnp.float32) for v in values).astype(jnp.bfloat16)

    def a_start(self, h):
        @pl.when(h >= self.slots)
        def _():
            pl.semaphore_wait(self.free, 1)
        self.a_copy(h).start()

    def a_stage(self, h):
        held, slot, c = self.held, self.slot(h), self.at.c
        self.a_copy(h).wait_recv()

        @pl.loop(0, self.nz)
        def _(z):
            held[slot, z] = self.plus(held[slot, z], self.grads[z, c, self.band(h), :])
        self.bx_copy(h).start()
        self.by_copy(h).start()
        self.a_copy(h).wait_send()

    def b_stage(self, h):
        held, slot, at = self.held, self.slot(h), self.at
        for copy, came, base, side in (
            (self.bx_copy(h), self.bx, 0, at.s),
            (self.by_copy(h), self.by, self.low, at.r),
        ):
            copy.wait()

            @pl.loop(0, self.low)
            def _(z, came=came, base=base, side=side):
                mine = self.cols(side)
                held[slot, base + z, :, mine] = self.plus(held[slot, base + z, :, mine], came[h, z])
        for n in range(2):
            self.near_copy(h, n).start()

    def near_stage(self, h):
        held, slot, at = self.held, self.slot(h), self.at
        for n in range(2):
            self.near_copy(h, n).wait()
            target, mine = 2 * n + lax.rem(at.z, 2), self.cols((at.s, at.r)[n])
            held[slot, target, :, mine] = self.plus(held[slot, target, :, mine], self.near[h, n])
        self.far_copy(h).start()

    def far_stage(self, h):
        held, slot, z, mine = self.held, self.slot(h), self.at.z, self.cols(self.side)
        self.far_copy(h).wait()
        held[slot, z, :, mine] = self.plus(held[slot, z, :, mine], self.far[h])
        self.pair_copy(h).start()

    def pair_stage(self, h):
        held, slot, z, mine = self.held, self.slot(h), self.at.z, self.cols(self.side)
        self.pair_copy(h).wait()
        self.bx[h, 0] = self.plus(held[slot, z, :, mine], self.swap[h])

        @pl.when(h + self.slots < self.parts)
        def _():
            pl.semaphore_signal(self.free, inc=1, device_id=self.at.core(), device_id_type=MESH)
        self.put_copy(h).start()
        self.last_copy(h).start()

    def close(self, h):
        self.put_copy(h).wait()
        self.last_copy(h).wait()

    def step(self, i):
        def stage(lag, work):
            h = i - lag
            pl.when((h >= 0) & (h < self.parts))(lambda: work(h))

        @pl.when((lax.rem(i, 2) == 0) & (i < self.parts))
        def _():
            self.a_start(i)
            self.a_start(i + 1)

        stage(1, self.b_stage)
        stage(2, self.near_stage)
        stage(3, self.far_stage)
        stage(4, self.pair_stage)
        stage(0, self.a_stage)
        stage(5, self.close)

    def tiny_copy(self, n, peer):
        return remote(self.tiny, self.tiny_in.at[n], self.ts.at[n], self.tr.at[n], peer)

    def tiny_z(self, d):
        return remote(self.tiny, self.tiny_in.at[2 + d], self.ts.at[2 + d], self.tr.at[2 + d], self.at.to(d))

    def tiny_step(self, n):
        peers = (self.at.core(), self.at.x(), self.at.y())
        if 0 < n <= 3:
            copy = self.tiny_copy(n - 1, peers[n - 1])
            copy.wait()
            self.tiny[...] = self.tiny[...] + self.tiny_in[n - 1]
        if n < 3:
            self.tiny_copy(n, peers[n]).start()
        if n == 3:
            for d in self.steps:
                self.tiny_z(d).start()
        if n == 4:
            for d in self.steps:
                self.tiny_z(d).wait()
            self.tiny_out[...] = self.tiny[...] + sum(self.tiny_in[2 + d] for d in self.steps)


def backward_kernel(nz, layers, length, total, *refs):
    cot_ref, full_ref, vec, bias_ref = refs[:4]
    per = 11
    saved = [refs[4 + per * l : 4 + per * (l + 1)] for l in range(layers)]
    refs = refs[4 + per * layers :]
    share_ref, tiny_out, input_ref = refs[:3]
    (
        up, wide_a, wide_b, hidden, mixed, pre_low, low, q, k, v, att, do, lse, weight, came, sent,
        load_sem, weight_sem, x_sem, tiny, grads,
    ) = refs[3:24]
    units = layers * UNITS
    reduce = Reduce(nz, units, share_ref, tiny, tiny_out, grads, *refs[24:])
    at = reduce.at
    width = up.shape[1]
    wide, half_z = width // 2, nz // 2
    shard = reduce.shard
    names = ("current", "normed_t", "q", "k", "v", "lse", "att", "after", "mixed", "pre", "hidden")
    homes = dict(
        normed_t=att, q=q, k=k, v=v, lse=lse, att=att, after=wide_b, mixed=mixed, pre=wide_a, hidden=hidden
    )

    def load(l, name):
        n = names.index(name)
        source = saved[l][n]
        home = homes.get(name, hidden if source.dtype == jnp.bfloat16 else wide_b)
        if home.shape != source.shape:
            if len(source.shape) == 3:
                home = home.at[:, :, pl.ds(0, source.shape[2])]
            elif source.shape[0] != home.shape[0]:
                home = home.at[pl.ds(0, source.shape[0]), :]
            else:
                home = home.at[:, pl.ds(0, source.shape[1])]
        return pltpu.make_async_copy(source, home, load_sem.at[l, n])

    def fetch(u):
        return pltpu.make_async_copy(full_ref.at[u], weight, weight_sem.at[0])

    def fill(product):
        @pl.loop(0, 2)
        def _(i):
            @pl.loop(0, 2)
            def _(j):
                r = pl.ds(pl.multiple_of(i * wide, 128), wide)
                c = pl.ds(pl.multiple_of(j * wide, 128), wide)
                value = product(r, c).astype(jnp.bfloat16).reshape(half_z, 2, shard, wide)
                grads[pl.ds(i * half_z, half_z), :, :, c] = value

    def vector(n):
        return vec[n : n + 1, :]

    def gather_row(n, values):
        tiny[n : n + 1, :] = tiny[n : n + 1, :] + jnp.sum(values, axis=0, keepdims=True)

    def norm_tile(values, gain, w, n):
        inverse = lax.rsqrt(jnp.mean(values * values, axis=-1, keepdims=True) + EPSILON)
        scaled = w * gain
        inner = jnp.mean(values * scaled, axis=-1, keepdims=True)
        gather_row(n, w * values * inverse)
        return inverse * scaled - values * (inverse * inverse * inverse) * inner

    def count(l):
        return length if l == layers - 1 else total

    def next_load(l, *which):
        if l > 0:
            for name in which:
                load(l - 1, name).start()

    def down(l):
        m = count(l)
        load(l, "hidden").wait()

        def body(r):
            value = up[r, :].astype(jnp.bfloat16)
            low[r, :] = value
            gather_row(3 * layers + l, value.astype(jnp.float32))
        each_tile(m, body)
        fill(lambda r, c: dot_tn(hidden[:m, r], low[:m, c]))
        if saved[l][0].dtype == jnp.bfloat16:
            load(l, "current").start()
        else:
            next_load(l, "hidden")

    def expand(l):
        fetch(l * UNITS + 5).wait()
        load(l, "pre").wait()

        def body(r):
            grown = dot_nt(low[r, :], weight[...])
            value = wide_a[r, :]
            gate = 1.0 / (1.0 + jnp.exp(-value))
            result = (grown * gate * (1.0 + value * (1.0 - gate))).astype(jnp.bfloat16)
            pre_low[r, :] = result
            gather_row(2 * layers + l, result.astype(jnp.float32))
        each_tile(count(l), body, TALL)
        fetch(l * UNITS + 4).start()

    def fill_up(l):
        m = count(l)
        load(l, "mixed").wait()
        fill(lambda r, c: dot_tn(mixed[:m, r], pre_low[:m, c]))
        next_load(l, "mixed")

    def output(l):
        fetch(l * UNITS + 4).wait()
        load(l, "after").wait()
        gain = vector(2 * l + 1)

        def body(r):
            w = dot_nt(pre_low[r, :], weight[...])
            value = up[r, :] + norm_tile(wide_b[r, :], gain, w, 2 * l + 1)
            up[r, :] = value
            low[r, :] = value.astype(jnp.bfloat16)
        each_tile(count(l), body, TALL)
        fetch(l * UNITS + 3).start()
        if saved[l][0].dtype != jnp.bfloat16:
            load(l, "current").start()

    def fill_out(l):
        m = count(l)
        load(l, "att").wait()
        fill(lambda r, c: dot_nn(att[r, :m], low[:m, c]))
        load(l, "normed_t").start()

    def attention(l, start, stop):
        m = count(l)
        row = 4 * layers + l
        factor = jnp.broadcast_to(vec[row : row + 1, 0:128], (128, 128)).T[0:HEAD, 0:1]

        def head(h, sums):
            rows = head_rows(h)
            kh, vh, qh, oh = k[rows, :], v[rows, :], q[rows, :m], do[rows, :m]
            scores = dot_tn(kh, qh) + bias_ref[:, :m]
            probs = jnp.exp(scores - lse[h, :, :m])
            weighted = probs * dot_tn(vh, oh)
            inner = jnp.sum(weighted, axis=0, keepdims=True)
            score = (weighted - probs * inner).astype(jnp.bfloat16)
            v[rows, :] = dot_nt(oh, probs.astype(jnp.bfloat16)).astype(jnp.bfloat16)
            k[rows, :] = dot_nt(qh, score).astype(jnp.bfloat16)
            query = dot_nn(kh, score)
            q[rows, :m] = (query * factor).astype(jnp.bfloat16)
            return sums + jnp.sum(query * qh.astype(jnp.float32), axis=1, keepdims=True)

        sums = lax.fori_loop(start, stop, head, jnp.zeros((HEAD, 1), jnp.float32))
        flat = jnp.broadcast_to(sums, (HEAD, 128)).T
        tiny[row : row + 1, 0:HEAD] = tiny[row : row + 1, 0:HEAD] + flat[0:1, :]

    def attend_first(l):
        m = count(l)
        fetch(l * UNITS + 3).wait()

        def body(r):
            do[r, :m] = dot_nt(weight[r, :], low[:m, :]).astype(jnp.bfloat16)
        each_tile(width, body, wide)
        fetch(l * UNITS + 1).start()
        for name in ("q", "k", "v", "lse"):
            load(l, name).wait()
        attention(l, 0, HEADS // 2)

    def fill_project(l, n):
        source = (k, v, q)[n]
        m = total if n < 2 else count(l)
        if n == 0:
            attention(l, HEADS // 2, HEADS)
            next_load(l, "lse")
            load(l, "normed_t").wait()
        fill(lambda r, c: dot_nt(att[r, :m], source[c, :m]))

    def project(l, n):
        source = (k, v, q)[n]
        m = total if n < 2 else count(l)
        fetch(l * UNITS + (1, 2, 0)[n]).wait()

        def body(r):
            value = dot_nt(source[:, r].T, weight[...])
            if n > 0:
                value = value + wide_a[r, :]
            wide_a[r, :] = value
        each_tile(m, body, TALL)
        if n < 2:
            fetch(l * UNITS + (2, 0)[n]).start()
            return
        if l > 0:
            fetch((l - 1) * UNITS + 5).start()
        load(l, "current").wait()
        gain = vector(2 * l)
        current = hidden if saved[l][0].dtype == jnp.bfloat16 else wide_b

        def close(r):
            return norm_tile(current[r, :].astype(jnp.float32), gain, wide_a[r, :], 2 * l)

        own = count(l)

        def first(r):
            up[r, :] = up[r, :] + close(r)
        each_tile(own, first)
        if own < total:
            @pl.loop(own // ROWS, total // ROWS)
            def _(i):
                r = pl.ds(pl.multiple_of(i * ROWS, ROWS), ROWS)
                up[r, :] = close(r)
        next_load(l, "pre", "after", "att", "q", "k", "v")
        if l == 0:
            sent[...] = up[length:, :].astype(jnp.bfloat16)
            reply.start()

    reply = remote(sent, came, x_sem.at[0], x_sem.at[1], at.x())
    work = (
        down, expand, fill_up, output, fill_out, attend_first,
        lambda l: fill_project(l, 0), lambda l: project(l, 0),
        lambda l: fill_project(l, 1), lambda l: project(l, 1),
        lambda l: fill_project(l, 2), lambda l: project(l, 2),
    )
    last = layers - 1
    start_copy = pltpu.make_async_copy(cot_ref, sent, x_sem.at[2])
    start_copy.start()
    for name in ("hidden", "pre", "mixed", "after", "att", "q", "k", "v", "lse"):
        load(last, name).start()
    fetch(last * UNITS + 5).start()
    tiny[...] = jnp.zeros_like(tiny)
    at.greet()
    start_copy.wait()
    up[:length, :] = sent[...].astype(jnp.float32)

    @pl.loop(0, reduce.iterations)
    def _(i):
        for n in range(reduce.parts):
            @pl.when(i == n)
            def _(n=n):
                work[n % len(work)](last - n // len(work))
        reduce.step(i)
        for n in range(5):
            @pl.when(i == reduce.parts + n)
            def _(n=n):
                reduce.tiny_step(n)
                if n == 2:
                    reply.wait()
                    input_ref[...] = (up[:length, :] + came[...].astype(jnp.float32)).astype(jnp.bfloat16)


def backward_pass(nz, cotangent, full, vec, bias, saved):
    layers = len(saved)
    units = layers * UNITS
    length, width = cotangent.shape
    total = bias.shape[0]
    shard = width // (2 * nz)
    half, wide, low, n = shard // 2, width // 2, nz // 2, nz - 1
    parts = 2 * units
    slots = min(SLOTS, parts)
    flat = [one for group in saved for one in group]
    rows = vec.shape[0]
    dma = pltpu.SemaphoreType.DMA
    small, large = jnp.bfloat16, jnp.float32
    anywhere = pl.BlockSpec(memory_space=pl.ANY)
    inside = pl.BlockSpec(memory_space=pltpu.VMEM)
    natural, turned = (total, width), (width, total)
    return pl.pallas_call(
        functools.partial(backward_kernel, nz, layers, length, total),
        out_shape=(
            jax.ShapeDtypeStruct((units, shard, width), small),
            jax.ShapeDtypeStruct((rows, width), large),
            jax.ShapeDtypeStruct((length, width), small),
        ),
        in_specs=[anywhere, anywhere, inside, inside] + [anywhere] * len(flat),
        out_specs=(anywhere, inside, inside),
        scratch_shapes=[
            pltpu.VMEM(natural, large),
            pltpu.VMEM(natural, large),
            pltpu.VMEM(natural, large),
            pltpu.VMEM(natural, small),
            pltpu.VMEM(natural, small),
            pltpu.VMEM(natural, small),
            pltpu.VMEM(natural, small),
            pltpu.VMEM(turned, small),
            pltpu.VMEM(turned, small),
            pltpu.VMEM(turned, small),
            pltpu.VMEM(turned, small),
            pltpu.VMEM(turned, small),
            pltpu.VMEM((HEADS, 1, total), large),
            pltpu.VMEM((width, width), small),
            pltpu.VMEM((length, width), small),
            pltpu.VMEM((length, width), small),
            dma((layers, 11)),
            dma((1,)),
            dma((3,)),
            pltpu.VMEM((rows, width), large),
            pltpu.VMEM((nz, 2, shard, width), small),
            pltpu.VMEM((slots, nz, half, width), small),
            pltpu.VMEM((parts, low, half, wide), small),
            pltpu.VMEM((parts, low, half, wide), small),
            pltpu.VMEM((parts, 2, half, wide), small),
            pltpu.VMEM((parts, half, wide), small),
            pltpu.VMEM((parts, half, wide), small),
            pltpu.VMEM((3 + n, rows, width), large),
            dma((parts,)), dma((parts,)),
            dma((parts, 2)), dma((parts, 2)),
            dma((parts, 3)), dma((parts, 3)),
            dma((parts,)), dma((parts,)),
            dma((parts,)),
            dma((parts,)), dma((parts,)),
            dma((3 + n,)), dma((3 + n,)),
            pltpu.SemaphoreType.REGULAR,
        ],
        compiler_params=pltpu.CompilerParams(
            collective_id=2, has_side_effects=True, vmem_limit_bytes=63 << 20
        ),
    )(cotangent, full, vec, bias, *flat)


def forward_layer(current, weights, allowed, series_count, local_length, total_length):
    qkv_weight, out_weight, up_weight, down_weight, norm_gains, up_bias, down_bias, query_scale = (
        weights
    )
    token_count, model_width = current.shape
    normed, inverse_one = norm_rows(current, norm_gains[0].astype(jnp.float32))
    normed_low = normed.astype(jnp.bfloat16).reshape(series_count, local_length, model_width)
    projected = jnp.einsum(
        "bld,kdc->bkcl", normed_low, qkv_weight, preferred_element_type=jnp.float32
    ).reshape(series_count, 3 * model_width, local_length)
    query_raw = projected[:, :model_width]
    factor = query_factor(query_scale)
    query_low = (
        query_raw.reshape(series_count, HEADS, HEAD, local_length) * factor[None, None, :, None]
    ).astype(jnp.bfloat16)
    pair_low = projected[:, model_width:].astype(jnp.bfloat16)
    pair_all = lax.all_gather(pair_low, "seq", axis=2, tiled=True)
    key_all = pair_all[:, :model_width].reshape(series_count, HEADS, HEAD, total_length)
    value_all = pair_all[:, model_width:].reshape(series_count, HEADS, HEAD, total_length)
    scores = jnp.einsum("bheq,bhek->bhqk", query_low, key_all, preferred_element_type=jnp.float32)
    scores = jnp.where(allowed[:, None], scores, NEG_FILL)
    top_score = jnp.max(scores, axis=-1, keepdims=True)
    exp_scores = jnp.exp(scores - top_score)
    exp_total = jnp.sum(exp_scores, axis=-1, keepdims=True)
    probs_low = (exp_scores / exp_total).astype(jnp.bfloat16)
    log_total = top_score + jnp.log(exp_total)
    attended = jnp.einsum(
        "bhqk,bhek->bheq", probs_low, value_all, preferred_element_type=jnp.float32
    )
    attended_low = attended.astype(jnp.bfloat16).reshape(series_count, model_width, local_length)
    attn_out = jnp.einsum(
        "bdl,de->ble", attended_low, out_weight, preferred_element_type=jnp.float32
    )
    after_attn = current + attn_out.reshape(token_count, model_width)
    normed_two, inverse_two = norm_rows(after_attn, norm_gains[1].astype(jnp.float32))
    mixed_low = normed_two.astype(jnp.bfloat16)
    hidden_pre = jnp.dot(mixed_low, up_weight, preferred_element_type=jnp.float32) + up_bias.astype(
        jnp.float32
    )
    hidden_low = jax.nn.silu(hidden_pre).astype(jnp.bfloat16)
    result = after_attn + (
        jnp.dot(hidden_low, down_weight, preferred_element_type=jnp.float32)
        + down_bias.astype(jnp.float32)
    )
    stored = (
        current,
        inverse_one,
        normed_low,
        query_raw,
        query_low,
        key_all,
        value_all,
        log_total,
        attended_low,
        after_attn,
        inverse_two,
        mixed_low,
        hidden_pre,
        hidden_low,
    )
    return (result, stored)


def backward_layer(upstream, weights, stored, allowed, series_count, local_length, total_length):
    qkv_weight, out_weight, up_weight, down_weight, norm_gains, up_bias, down_bias, query_scale = (
        weights
    )
    (
        current,
        inverse_one,
        normed_low,
        query_raw,
        query_low,
        key_all,
        value_all,
        log_total,
        attended_low,
        after_attn,
        inverse_two,
        mixed_low,
        hidden_pre,
        hidden_low,
    ) = stored
    token_count, model_width = current.shape
    down_low = upstream.astype(jnp.bfloat16)
    grad_down_bias = jnp.sum(down_low, axis=0, dtype=jnp.float32)
    grad_down = jnp.einsum("tf,td->fd", hidden_low, down_low, preferred_element_type=jnp.float32)
    hidden_grad = jnp.einsum("td,fd->tf", down_low, down_weight, preferred_element_type=jnp.float32)
    sigmoid_pre = jax.nn.sigmoid(hidden_pre)
    pre_low = (hidden_grad * sigmoid_pre * (1.0 + hidden_pre * (1.0 - sigmoid_pre))).astype(
        jnp.bfloat16
    )
    grad_up_bias = jnp.sum(pre_low, axis=0, dtype=jnp.float32)
    grad_up = jnp.einsum("td,tf->df", mixed_low, pre_low, preferred_element_type=jnp.float32)
    mixed_grad = jnp.einsum("tf,df->td", pre_low, up_weight, preferred_element_type=jnp.float32)
    norm_grad_two, gain_grad_two = norm_back(
        after_attn, inverse_two, norm_gains[1].astype(jnp.float32), mixed_grad
    )
    attn_grad = upstream + norm_grad_two
    branch_low = attn_grad.astype(jnp.bfloat16).reshape(series_count, local_length, model_width)
    grad_out = jnp.einsum(
        "bdl,ble->de", attended_low, branch_low, preferred_element_type=jnp.float32
    )
    output_low = (
        jnp.einsum("ble,de->bdl", branch_low, out_weight, preferred_element_type=jnp.float32)
        .astype(jnp.bfloat16)
        .reshape(series_count, HEADS, HEAD, local_length)
    )
    scores = jnp.einsum("bheq,bhek->bhqk", query_low, key_all, preferred_element_type=jnp.float32)
    scores = jnp.where(allowed[:, None], scores, NEG_FILL)
    attn_probs = jnp.exp(scores - log_total)
    prob_grad = jnp.einsum(
        "bheq,bhek->bhqk", output_low, value_all, preferred_element_type=jnp.float32
    )
    row_inner = jnp.sum(attn_probs * prob_grad, axis=-1, keepdims=True)
    score_low = (attn_probs * (prob_grad - row_inner)).astype(jnp.bfloat16)
    value_grad = jnp.einsum(
        "bhqk,bheq->bhek",
        attn_probs.astype(jnp.bfloat16),
        output_low,
        preferred_element_type=jnp.float32,
    )
    key_grad = jnp.einsum(
        "bhqk,bheq->bhek", score_low, query_low, preferred_element_type=jnp.float32
    )
    query_grad = jnp.einsum(
        "bhqk,bhek->bheq", score_low, key_all, preferred_element_type=jnp.float32
    )
    pair_grad = jnp.concatenate(
        [
            key_grad.reshape(series_count, model_width, total_length),
            value_grad.reshape(series_count, model_width, total_length),
        ],
        axis=1,
    )
    pair_local = lax.psum_scatter(pair_grad, "seq", scatter_dimension=2, tiled=True)
    key_local, value_local = pair_local[:, :model_width], pair_local[:, model_width:]
    factor = query_factor(query_scale)
    factor_grad = jnp.sum(
        query_grad * query_raw.reshape(series_count, HEADS, HEAD, local_length), axis=(0, 1, 3)
    )
    grad_scale = (
        factor_grad * jax.nn.sigmoid(query_scale.astype(jnp.float32)) * (SOFT_ONE / math.sqrt(HEAD))
    )
    raw_low = (
        (query_grad * factor[None, None, :, None])
        .astype(jnp.bfloat16)
        .reshape(series_count, model_width, local_length)
    )
    projected_grad = jnp.concatenate(
        [raw_low, key_local.astype(jnp.bfloat16), value_local.astype(jnp.bfloat16)], axis=1
    )
    grad_qkv = jnp.einsum(
        "bld,bcl->dc", normed_low, projected_grad, preferred_element_type=jnp.float32
    )
    normed_grad = jnp.einsum(
        "bkcl,kdc->bld",
        projected_grad.reshape(series_count, 3, model_width, local_length),
        qkv_weight,
        preferred_element_type=jnp.float32,
    ).reshape(token_count, model_width)
    norm_grad_one, gain_grad_one = norm_back(
        current, inverse_one, norm_gains[0].astype(jnp.float32), normed_grad
    )
    result = attn_grad + norm_grad_one
    layer_grads = (
        grad_qkv,
        grad_out,
        grad_up,
        grad_down,
        jnp.stack([gain_grad_one, gain_grad_two]),
        grad_up_bias,
        grad_down_bias,
        grad_scale,
    )
    return (result, layer_grads)


def pack_small(norm_gains, up_bias, down_bias, query_scale):
    layers, _, shard = norm_gains.shape
    scale = jnp.pad(query_scale, ((0, 0), (0, shard - query_scale.shape[1])))
    rows = jnp.concatenate([norm_gains.reshape(2 * layers, shard), up_bias, down_bias, scale])
    return jnp.pad(rows, ((0, -rows.shape[0] % 16), (0, -shard % 128)))


def unpack_small(tiny, layers, shard, scale_shard):
    count = tiny.shape[0]
    vectors = tiny[:, : 4 * layers, :shard].transpose(1, 0, 2).reshape(4 * layers, count * shard)
    scale = tiny[:, 4 * layers : 5 * layers, :scale_shard].transpose(1, 0, 2).reshape(layers, count * scale_shard)
    gains = vectors[: 2 * layers].reshape(layers, 2, count * shard)
    return gains, vectors[2 * layers : 3 * layers], vectors[3 * layers :], scale


def pack_tiny(layer_grads, count):
    gains = jnp.concatenate([g[4] for g in layer_grads])
    vectors = jnp.concatenate(
        [gains, jnp.stack([g[5] for g in layer_grads]), jnp.stack([g[6] for g in layer_grads])]
    )
    scale = jnp.stack([g[7] for g in layer_grads])
    shard, part = vectors.shape[1] // count, scale.shape[1] // count
    vectors = vectors.reshape(-1, count, shard)
    scale = jnp.pad(scale.reshape(-1, count, part), ((0, 0), (0, 0), (0, shard - part)))
    rows = jnp.concatenate([vectors, scale]).transpose(1, 0, 2)
    return jnp.pad(rows, ((0, 0), (0, -rows.shape[1] % 16), (0, -shard % 128)))


def unpack_tiny(tiny, layers, shard, part):
    gains = tiny[: 2 * layers, :shard].reshape(layers, 2, shard)
    up, down = tiny[2 * layers : 3 * layers, :shard], tiny[3 * layers : 4 * layers, :shard]
    return gains, up, down, tiny[4 * layers : 5 * layers, :part]


def gather_plain(qkv_weight, out_weight, up_weight, down_weight, small):
    layers, shard, width = out_weight.shape
    qkv = qkv_weight.reshape(layers, shard, 3, width).transpose(0, 2, 1, 3)
    square = jnp.stack([out_weight, up_weight, down_weight], axis=1)
    units = jnp.concatenate([qkv, square], axis=1).reshape(layers * UNITS, shard, width)
    full = lax.all_gather(units, "fsdp", axis=1, tiled=True)
    return full, lax.all_gather(small, "fsdp", axis=0)


def reduce_plain(layer_grads, tiny):
    units = []
    for grads in layer_grads:
        width = grads[0].shape[1]
        units += list(grads[:3]) + [grads[3][:, k * width : (k + 1) * width] for k in range(3)]
    shares = lax.psum_scatter(jnp.stack(units), "fsdp", scatter_dimension=1, tiled=True)
    small = lax.psum_scatter(tiny, "fsdp", scatter_dimension=0, tiled=True)[0]
    return lax.psum(shares, ("replica", "seq")), lax.psum(small, ("replica", "seq"))


def plain(
    series_in,
    cotangent,
    qkv_weight,
    out_weight,
    up_weight,
    down_weight,
    norm_gains,
    up_bias,
    down_bias,
    query_scale,
    pad_length,
    span_starts,
    span_count,
):
    series_count, local_length, model_width = series_in.shape
    seq_count = lax.axis_size("seq")
    group = lax.axis_size("fsdp")
    total_length = local_length * seq_count
    offset = lax.axis_index("seq") * local_length
    allowed = visible(pad_length, span_starts, span_count, offset, local_length, total_length)
    layer_count, shard = qkv_weight.shape[:2]
    scale_shard = query_scale.shape[1]
    small = pack_small(norm_gains, up_bias, down_bias, query_scale)
    full, tiny = gather_plain(qkv_weight, out_weight, up_weight, down_weight, small)
    gains, up_full, down_full, scale_full = unpack_small(tiny, layer_count, shard, scale_shard)
    weights = [
        (
            full[UNITS * l : UNITS * l + 3],
            full[UNITS * l + 3],
            full[UNITS * l + 4],
            full[UNITS * l + 5],
            gains[l],
            up_full[l],
            down_full[l],
            scale_full[l],
        )
        for l in range(layer_count)
    ]
    current = series_in.reshape(series_count * local_length, model_width).astype(jnp.float32)
    stored_list = []
    for l in range(layer_count):
        current, stored = forward_layer(
            current, weights[l], allowed, series_count, local_length, total_length
        )
        stored_list.append(stored)
    series_out = current.reshape(series_count, local_length, model_width).astype(jnp.bfloat16)
    upstream = cotangent.reshape(series_count * local_length, model_width).astype(jnp.float32)
    order = list(reversed(range(layer_count)))
    grads_list = {}
    for l in order:
        upstream, grads_list[l] = backward_layer(
            upstream, weights[l], stored_list[l], allowed, series_count, local_length, total_length
        )
    tiny_grads = pack_tiny([grads_list[l] for l in range(layer_count)], group)
    big = [
        tuple(grads_list[l][k].astype(jnp.bfloat16) for k in (3, 2, 1, 0)) for l in order
    ]
    shares, tiny_sum = reduce_plain(big, tiny_grads)
    shares = shares.reshape(layer_count, UNITS, shard, model_width)[::-1]
    grad_gains, grad_up_bias, grad_down_bias, grad_scale = unpack_tiny(
        tiny_sum, layer_count, shard, scale_shard
    )
    grad_qkv = shares[:, 3:].transpose(0, 2, 1, 3).reshape(layer_count, shard, 3 * model_width)
    input_grad = upstream.reshape(series_count, local_length, model_width).astype(jnp.bfloat16)
    return (
        series_out,
        input_grad,
        grad_qkv.astype(jnp.float32),
        shares[:, 2].astype(jnp.float32),
        shares[:, 1].astype(jnp.float32),
        shares[:, 0].astype(jnp.float32),
        grad_gains,
        grad_up_bias,
        grad_down_bias,
        grad_scale,
    )


def finish(shares, tiny, layers, shard, width, query_scale):
    shares = shares.reshape(layers, UNITS, shard, width)[::-1]
    low = jnp.float32
    place = lax.axis_index("fsdp")
    part = query_scale.shape[1]
    vectors = lax.dynamic_slice_in_dim(tiny[: 4 * layers], place * shard, shard, axis=1)
    scale = lax.dynamic_slice_in_dim(tiny[4 * layers : 5 * layers], place * part, part, axis=1)
    raw = query_scale.astype(jnp.float32)
    scale = scale * (jax.nn.sigmoid(raw) * (SOFT_ONE / math.sqrt(HEAD))) / query_factor(query_scale)
    qkv = jnp.concatenate([shares[:, 5], shares[:, 3], shares[:, 4]], axis=2)
    return (
        qkv.astype(low),
        shares[:, 2].astype(low),
        shares[:, 1].astype(low),
        shares[:, 0].astype(low),
        vectors[: 2 * layers].reshape(layers, 2, shard),
        vectors[2 * layers : 3 * layers],
        vectors[3 * layers :],
        scale,
    )


def fused(
    series_in,
    cotangent,
    qkv_weight,
    out_weight,
    up_weight,
    down_weight,
    norm_gains,
    up_bias,
    down_bias,
    query_scale,
    pad_length,
    span_starts,
    span_count,
):
    length = series_in.shape[1]
    layers, shard, width = out_weight.shape
    nz = lax.axis_size("fsdp") // 2
    small = pack_small(norm_gains, up_bias, down_bias, query_scale)
    bias = pair_bias(pad_length, span_starts, span_count, length)
    full, vec, series_out, saved = forward_pass(
        nz, series_in[0], qkv_weight, out_weight, up_weight, down_weight, small, bias, query_scale.shape[1]
    )
    shares, tiny, input_grad = backward_pass(nz, cotangent[0], full, vec, bias, saved)
    rest = finish(shares, tiny, layers, shard, width, query_scale)
    return (series_out[None], input_grad[None]) + rest


def shards(*args):
    series_in, out_weight = args[0], args[3]
    group = lax.axis_size("fsdp")
    width = series_in.shape[2]
    block = lax.axis_size("replica") == 2 and lax.axis_size("seq") == 2 and group == 8
    block = block and series_in.shape[0] == 1 and width == out_weight.shape[2] == HEADS * HEAD
    block = block and (width // group) % 32 == 0 and width % 256 == 0
    return fused(*args) if block else plain(*args)


def solution(mesh):
    return jax.shard_map(
        shards,
        mesh=mesh,
        in_specs=(
            P(("replica", "fsdp"), "seq", None),
            P(("replica", "fsdp"), "seq", None),
            P(None, "fsdp", None),
            P(None, "fsdp", None),
            P(None, "fsdp", None),
            P(None, "fsdp", None),
            P(None, None, "fsdp"),
            P(None, "fsdp"),
            P(None, "fsdp"),
            P(None, "fsdp"),
            P(("replica", "fsdp")),
            P(("replica", "fsdp"), None),
            P(("replica", "fsdp")),
        ),
        out_specs=(
            P(("replica", "fsdp"), "seq", None),
            P(("replica", "fsdp"), "seq", None),
            P(None, "fsdp", None),
            P(None, "fsdp", None),
            P(None, "fsdp", None),
            P(None, "fsdp", None),
            P(None, None, "fsdp"),
            P(None, "fsdp"),
            P(None, "fsdp"),
            P(None, "fsdp"),
        ),
        check_vma=False,
    )
```

```python
import functools
import math

import jax
import jax.numpy as jnp
from jax import lax
from jax.experimental import pallas as pl
from jax.experimental.pallas import tpu as pltpu
from jax.sharding import PartitionSpec as P

HEADS = 16
HEAD = 80
SPAN = 32


EPSILON = 1e-06
SOFT_ONE = 1.442695041
NEG_FILL = -1e30


def visible(pad_length, span_starts, span_count, offset, local_length, total_length):
    query_pos = offset + jnp.arange(local_length, dtype=jnp.int32)
    key_pos = jnp.arange(total_length, dtype=jnp.int32)
    shared = jnp.zeros((span_starts.shape[0], local_length, total_length), dtype=bool)
    for slot_index in range(span_starts.shape[1]):
        slot_start = span_starts[:, slot_index]
        slot_used = slot_index < span_count
        query_in = (
            slot_used[:, None]
            & (query_pos[None, :] >= slot_start[:, None])
            & (query_pos[None, :] < slot_start[:, None] + SPAN)
        )
        key_in = (key_pos[None, :] >= slot_start[:, None]) & (
            key_pos[None, :] < slot_start[:, None] + SPAN
        )
        shared = shared | query_in[:, :, None] & key_in[:, None, :]
    causal = key_pos[None, :] <= query_pos[:, None]
    allowed = (key_pos[None, None, :] >= pad_length[:, None, None]) & (causal[None] | shared)
    return allowed | (key_pos[None, None, :] == query_pos[None, :, None])


def norm_rows(values, scale_gain):
    inverse = lax.rsqrt(jnp.mean(values * values, axis=-1, keepdims=True) + EPSILON)
    return (values * inverse * scale_gain, inverse)


def norm_back(values, inverse, scale_gain, upstream):
    scaled = upstream * scale_gain
    inner_term = jnp.mean(values * scaled, axis=-1, keepdims=True)
    result = inverse * scaled - values * (inverse * inverse * inverse) * inner_term
    return (result, jnp.sum(upstream * values * inverse, axis=0))


def query_factor(query_scale):
    return jax.nn.softplus(query_scale.astype(jnp.float32)) * (SOFT_ONE / math.sqrt(HEAD))


MESH = pl.DeviceIdType.MESH
UNITS = 6
LAG = 1


class Place:
    def __init__(self, nz):
        self.nz = nz
        self.r = lax.axis_index("replica")
        f = lax.axis_index("fsdp")
        self.s = lax.axis_index("seq")
        self.z = lax.div(f, 2)
        self.c = lax.rem(f, 2)
        self.f = f

    def x(self):
        return (self.r, self.f, 1 - self.s)

    def y(self):
        return (1 - self.r, self.f, self.s)

    def core(self):
        return (self.r, self.f + 1 - 2 * self.c, self.s)

    def to(self, d):
        return (self.r, lax.rem(self.z + d, self.nz) * 2 + self.c, self.s)

    def source(self, d):
        return lax.rem(self.z - d + self.nz, self.nz)

    def greet(self):
        barrier = pltpu.get_barrier_semaphore()
        peers = [self.x(), self.y(), self.core()] + [self.to(d) for d in range(1, self.nz)]
        for peer in peers:
            pl.semaphore_signal(barrier, inc=1, device_id=peer, device_id_type=MESH)
        pl.semaphore_wait(barrier, len(peers))


def remote(src, dst, send, recv, device):
    return pltpu.make_async_remote_copy(
        src_ref=src, dst_ref=dst, send_sem=send, recv_sem=recv, device_id=device, device_id_type=MESH
    )


class Gather:
    def __init__(
        self, nz, layers, qkv_ref, out_ref, up_ref, down_ref, small_ref, full_ref, tiny_ref,
        mine, local_sem, keep_sem, zds, zdr, zs, zr, xs, xr, ys, yr, fxs, fxr, fys, fyr, cs, cr, ts, tr,
    ):
        self.__dict__.update(locals())
        self.at = Place(nz)
        self.shard, self.width = out_ref.shape[1], out_ref.shape[2]
        self.half, self.wide = self.shard // 2, self.width // 2
        self.units = layers * UNITS
        self.hops = nz - 1
        self.iterations = self.units + LAG * (self.hops + 2)

    def source(self, way, k):
        return self.at.z - way * k

    def comes(self, way, k):
        z = self.at.z
        return z >= k if way > 0 else z + k < self.nz

    def goes(self, way):
        z = self.at.z
        return z + 1 < self.nz if way > 0 else z >= 1

    def next(self, way):
        at = self.at
        return (at.r, 2 * (at.z + way) + at.c, at.s)

    def slot(self, way, k):
        return 2 * (k - 1) + (0 if way > 0 else 1)

    def block(self, u, z, c, r, s):
        row = pl.multiple_of((2 * z + c) * self.shard + r * self.half, 8)
        col = pl.multiple_of(s * self.wide, 128)
        return self.full_ref.at[u, pl.ds(row, self.half), pl.ds(col, self.wide)]

    def quarter(self, u, z, c, r, s, part):
        step = self.half // 2
        row = pl.multiple_of((2 * z + c) * self.shard + r * self.half + part * step, 8)
        col = pl.multiple_of(s * self.wide, 128)
        return self.full_ref.at[u, pl.ds(row, step), pl.ds(col, self.wide)]

    def own(self, u, c):
        row = pl.multiple_of((2 * self.at.z + c) * self.shard, 8)
        return self.full_ref.at[u, pl.ds(row, self.shard), :]

    def local(self, layer, k):
        if k < 3:
            piece = self.qkv_ref.at[layer, :, pl.ds(k * self.width, self.width)]
        else:
            piece = (self.out_ref, self.up_ref, self.down_ref)[k - 3].at[layer]
        u = layer * UNITS + k
        return pltpu.make_async_copy(piece, self.mine.at[u], self.local_sem.at[u])

    def keep(self, u):
        return pltpu.make_async_copy(self.mine.at[u], self.own(u, self.at.c), self.keep_sem.at[u])

    def z_copy(self, u, way, k):
        at, n = self.at, self.slot(way, k)
        piece = self.block(u, self.source(way, k - 1), at.c, at.r, at.s)
        held = piece
        if k == 1:
            row = pl.multiple_of(at.r * self.half, 16)
            held = self.mine.at[u, pl.ds(row, self.half), pl.ds(pl.multiple_of(at.s * self.wide, 128), self.wide)]
        return remote(held, piece, self.zs.at[u, n], self.zr.at[u, n], self.next(way))

    def z_diag(self, u, way):
        at, n = self.at, 0 if way > 0 else 1
        piece = self.block(u, at.z, at.c, 1 - at.r, 1 - at.s)
        row = pl.multiple_of((1 - at.r) * self.half, 16)
        col = pl.multiple_of((1 - at.s) * self.wide, 128)
        held = self.mine.at[u, pl.ds(row, self.half), pl.ds(col, self.wide)]
        return remote(held, piece, self.zds.at[u, n], self.zdr.at[u, n], self.next(way))

    def z_came(self, u, way, k):
        at, n = self.at, self.slot(way, k)
        piece = self.block(u, self.source(way, k), at.c, at.r, at.s)
        return remote(piece, piece, self.zs.at[u, n], self.zr.at[u, n], self.next(way))

    def x_copy(self, u, way, k):
        at, n = self.at, self.slot(way, k)
        piece = self.block(u, self.source(way, k), at.c, at.r, at.s)
        return remote(piece, piece, self.xs.at[u, n], self.xr.at[u, n], at.x())

    def y_copy(self, u, way, k):
        at, n = self.at, self.slot(way, k)
        piece = self.block(u, self.source(way, k), at.c, at.r, at.s)
        return remote(piece, piece, self.ys.at[u, n], self.yr.at[u, n], at.y())

    def fx_copy(self, u, way, k):
        at, n = self.at, self.slot(way, k)
        piece = self.quarter(u, self.source(way, k), at.c, 1 - at.r, at.s, 1)
        return remote(piece, piece, self.fxs.at[u, n], self.fxr.at[u, n], at.x())

    def fy_copy(self, u, way, k):
        at, n = self.at, self.slot(way, k)
        piece = self.quarter(u, self.source(way, k), at.c, at.r, 1 - at.s, 0)
        return remote(piece, piece, self.fys.at[u, n], self.fyr.at[u, n], at.y())

    def core_own(self, u):
        own, n = self.own(u, self.at.c), 8 * self.hops
        return remote(self.mine.at[u], own, self.cs.at[u, n], self.cr.at[u, n], self.at.core())

    def core_copy(self, u, way, k, which):
        at = self.at
        r = at.r if which in (0, 1) else 1 - at.r
        s = at.s if which in (0, 2) else 1 - at.s
        piece = self.block(u, self.source(way, k), at.c, r, s)
        n = 4 * self.slot(way, k) + which
        return remote(piece, piece, self.cs.at[u, n], self.cr.at[u, n], at.core())

    def tiny(self, d):
        piece = self.tiny_ref.at[self.at.f]
        return remote(piece, piece, self.ts.at[d - 1], self.tr.at[d - 1], self.at.to(d))

    def tiny_core(self, d):
        piece, n = self.tiny_ref.at[2 * self.at.source(d) + self.at.c], self.nz - 1 + d
        return remote(piece, piece, self.ts.at[n], self.tr.at[n], self.at.core())

    def begin(self):
        self.tiny_ref[self.at.f] = self.small_ref[...].astype(jnp.bfloat16)
        for layer in range(self.layers):
            for k in range(UNITS):
                self.local(layer, k).start()
        self.at.greet()
        for d in range(1, self.nz):
            self.tiny(d).start()
        self.tiny_core(0).start()

    def tiny_pass(self):
        for d in range(1, self.nz):
            self.tiny(d).wait_recv()
            self.tiny_core(d).start()

    def tiny_ready(self):
        for d in range(self.nz):
            self.tiny_core(d).wait_recv()

    def tiny_done(self):
        for d in range(1, self.nz):
            self.tiny(d).wait_send()
        for d in range(self.nz):
            self.tiny_core(d).wait_send()

    def when(self, cond, work):
        pl.when(cond)(work)

    def first(self, u):
        pltpu.make_async_copy(self.out_ref.at[0], self.mine.at[u], self.local_sem.at[u]).wait()
        self.keep(u).start()
        for way in (1, -1):
            def work(way=way):
                self.z_copy(u, way, 1).start()
                self.z_diag(u, way).start()
            self.when(self.goes(way), work)
        self.core_own(u).start()

    def hop(self, u, k):
        for way in (1, -1):
            def work(way=way):
                self.z_came(u, way, k).wait_recv()
                if k < self.hops:
                    self.when(self.goes(way), lambda: self.z_copy(u, way, k + 1).start())
                self.x_copy(u, way, k).start()
                self.y_copy(u, way, k).start()
                self.core_copy(u, way, k, 0).start()
                if k == 1:
                    self.z_diag(u, way).wait_recv()
                    self.core_copy(u, way, k, 3).start()
            self.when(self.comes(way, k), work)

    def forward(self, u, k):
        for way in (1, -1):
            def work(way=way):
                self.x_copy(u, way, k).wait_recv()
                if k > 1:
                    self.fy_copy(u, way, k).start()
                self.core_copy(u, way, k, 1).start()
                self.y_copy(u, way, k).wait_recv()
                if k > 1:
                    self.fx_copy(u, way, k).start()
                self.core_copy(u, way, k, 2).start()
            self.when(self.comes(way, k), work)

    def diagonal(self, u, k):
        for way in (1, -1):
            def work(way=way):
                self.fx_copy(u, way, k).wait_recv()
                self.fy_copy(u, way, k).wait_recv()
                self.core_copy(u, way, k, 3).start()
            self.when(self.comes(way, k), work)

    def step(self, i):
        def stage(lag, work):
            u = i - lag
            self.when((u >= 0) & (u < self.units), lambda: work(u))

        stage(0, self.first)
        for k in range(1, self.hops + 1):
            stage(LAG * k, lambda u, k=k: self.hop(u, k))
        for k in range(1, self.hops + 1):
            stage(LAG * (k + 1), lambda u, k=k: self.forward(u, k))
        for k in range(2, self.hops + 1):
            stage(LAG * (k + 2), lambda u, k=k: self.diagonal(u, k))

    def ready(self, u):
        self.keep(u).wait()
        self.core_own(u).wait_recv()
        for k in range(1, self.hops + 1):
            for way in (1, -1):
                def work(way=way, k=k):
                    for which in range(4):
                        self.core_copy(u, way, k, which).wait_recv()
                self.when(self.comes(way, k), work)

    def drain(self, u):
        self.core_own(u).wait_send()
        for k in range(1, self.hops + 1):
            for way in (1, -1):
                def sent(way=way, k=k):
                    self.z_copy(u, way, k).wait_send()
                    if k == 1:
                        self.z_diag(u, way).wait_send()
                came = self.goes(way)
                if k > 1:
                    came = came & self.comes(way, k - 1)
                self.when(came, sent)

                def work(way=way, k=k):
                    copies = (self.x_copy, self.y_copy, self.fx_copy, self.fy_copy)
                    for copy in copies if k > 1 else copies[:2]:
                        copy(u, way, k).wait_send()
                    for which in range(4):
                        self.core_copy(u, way, k, which).wait_send()
                self.when(self.comes(way, k), work)

    def finish(self):
        @pl.loop(0, self.units)
        def _(u):
            self.drain(u)

        self.tiny_done()


def gather_scratch(nz, layers, shard, width):
    units, n = layers * UNITS, 2 * (nz - 1)
    dma = pltpu.SemaphoreType.DMA
    return (
        [pltpu.VMEM((units, shard, width), jnp.bfloat16), dma((units,)), dma((units,))]
        + [dma((units, 2))] * 2
        + [dma((units, n))] * 10
        + [dma((units, 1 + 4 * n))] * 2
        + [dma((2 * nz,))] * 2
    )


def dot_nn(a, b):
    return jnp.dot(a, b, preferred_element_type=jnp.float32)


def dot_nt(a, b):
    return lax.dot_general(a, b, (((1,), (1,)), ((), ())), preferred_element_type=jnp.float32)


def dot_tn(a, b):
    return lax.dot_general(a, b, (((0,), (0,)), ((), ())), preferred_element_type=jnp.float32)


ROWS = 128
TALL = 256
BEGIN = 3


def each_tile(count, body, rows=ROWS):
    @pl.loop(0, count // rows)
    def _(i):
        body(pl.ds(pl.multiple_of(i * rows, rows), rows))


def head_rows(h):
    return pl.ds(pl.multiple_of(h * HEAD, 16), HEAD)


def row_norm(values, gain):
    inverse = lax.rsqrt(jnp.mean(values * values, axis=-1, keepdims=True) + EPSILON)
    return (values * inverse * gain).astype(jnp.bfloat16)


def expand_small(tiny_ref, vec_ref, layers, shard, part):
    width = vec_ref.shape[1]
    count = tiny_ref.shape[0]
    rows, lanes = tiny_ref.shape[1:]
    line = lax.broadcasted_iota(jnp.int32, (lanes, width), 0)
    column = lax.broadcasted_iota(jnp.int32, (lanes, width), 1)
    inner = lax.rem(column, HEAD)

    def place(f, sums):
        plain, scale = sums
        piece = tiny_ref[f]
        hot = jnp.where((column - f * shard == line) & (line < shard), 1.0, 0.0).astype(jnp.bfloat16)
        spread = jnp.where((inner - f * part == line) & (line < part), 1.0, 0.0).astype(jnp.bfloat16)
        return plain + dot_nn(piece, hot), scale + dot_nn(piece, spread)

    zero = jnp.zeros((rows, width), jnp.float32)
    plain, scale = lax.fori_loop(0, count, place, (zero, zero))
    soft = jnp.maximum(scale, 0.0) + jnp.log(1.0 + jnp.exp(-jnp.abs(scale)))
    row = lax.broadcasted_iota(jnp.int32, (rows, width), 0)
    vec_ref[...] = jnp.where(row < 4 * layers, plain, soft * (SOFT_ONE / math.sqrt(HEAD)))


def attend(heads, q_ref, k_ref, v_ref, bias_ref, out_ref, lse_ref):
    queries = q_ref.shape[1]

    @pl.loop(*heads)
    def _(h):
        rows = head_rows(h)
        scores = dot_tn(k_ref[rows, :], q_ref[rows, :]) + bias_ref[:, :queries]
        top = jnp.max(scores, axis=0, keepdims=True)
        grown = jnp.exp(scores - top)
        total = jnp.sum(grown, axis=0, keepdims=True)
        out = dot_nn(v_ref[rows, :], grown.astype(jnp.bfloat16)) * (1.0 / total)
        out_ref[rows, :] = out.astype(jnp.bfloat16)
        lse_ref[h] = top + jnp.log(total)


def forward_kernel(nz, layers, part, *refs):
    series_ref, qkv_ref, out_ref, up_ref, down_ref = refs[:5]
    gains_ref, up_bias_ref, down_bias_ref, scale_ref, pad_ref, starts_ref, count_ref = refs[5:12]
    full_ref, vec_out, series_out, bias_out = refs[12:16]
    per = 11
    saved = [refs[16 + per * l : 16 + per * (l + 1)] for l in range(layers)]
    refs = refs[16 + per * layers :]
    names = ("current", "normed_t", "q", "k", "v", "lse", "att", "after", "mixed", "pre", "hidden")
    held = [dict(zip(names, refs[per * l : per * (l + 1)])) for l in range(layers)]
    refs = refs[per * layers :]
    normed, weights, vec, last, tiny_ref, small_ref, bias_ref, swap_sem, load_sem, save_sem = refs[:10]
    gather = Gather(
        nz, layers, qkv_ref, out_ref, up_ref, down_ref, small_ref, full_ref, tiny_ref, *refs[10:]
    )
    at = gather.at
    length = series_ref.shape[0]
    total = held[0]["normed_t"].shape[1]
    other = total - length

    own_copy = pltpu.make_async_copy(series_ref, held[0]["current"].at[pl.ds(0, length)], swap_sem.at[0])
    swap_copy = remote(
        series_ref, held[0]["current"].at[pl.ds(length, other)], swap_sem.at[1], swap_sem.at[2], at.x()
    )

    def save(l, n):
        return pltpu.make_async_copy(held[l][names[n]], saved[l][n], save_sem.at[l, n])

    def fetch(u):
        return pltpu.make_async_copy(full_ref.at[u], weights.at[u % 2], load_sem.at[u % 2])

    def arrived(u):
        fetch(u).wait()
        return weights.at[u % 2]

    def vector(n):
        return vec[n : n + 1, :]

    def normalize(l):
        b = held[l]
        gain = vector(2 * l)

        def body(r):
            values = row_norm(b["current"][r, :].astype(jnp.float32), gain)
            normed[r, :] = values
            b["normed_t"][:, r] = values.T
        each_tile(total, body)
        save(l, 1).start()

    def project(l, n):
        b = held[l]
        target = b[("q", "k", "v")[n]]
        weight = arrived(l * UNITS + n)

        def body(r):
            values = dot_nn(normed[r, :], weight[...])
            if n == 0:
                values = values * vector(4 * layers + l)
            target[:, r] = values.astype(jnp.bfloat16).T
        each_tile(target.shape[1], body)
        save(l, 2 + n).start()

    def attention(l, first):
        b = held[l]
        heads = (0, HEADS // 2) if first else (HEADS // 2, HEADS)
        attend(heads, b["q"], b["k"], b["v"], bias_ref, b["att"], b["lse"])
        if not first:
            save(l, 5).start()
            save(l, 6).start()

    def output(l):
        b = held[l]
        weight = arrived(l * UNITS + 3)
        gain = vector(2 * l + 1)

        def body(r):
            after = b["current"][r, :].astype(jnp.float32) + dot_tn(b["att"][:, r], weight[...])
            b["after"][r, :] = after
            b["mixed"][r, :] = row_norm(after, gain)
        each_tile(b["after"].shape[0], body)
        save(l, 7).start()
        save(l, 8).start()

    def expand(l):
        b = held[l]
        weight = arrived(l * UNITS + 4)
        bias = vector(2 * layers + l)

        def body(r):
            pre = dot_nn(b["mixed"][r, :], weight[...]) + bias
            b["pre"][r, :] = pre
            b["hidden"][r, :] = (pre * (1.0 / (1.0 + jnp.exp(-pre)))).astype(jnp.bfloat16)
        each_tile(b["pre"].shape[0], body)
        save(l, 9).start()
        save(l, 10).start()

    def contract(l):
        b = held[l]
        weight = arrived(l * UNITS + 5)
        bias = vector(3 * layers + l)

        def body(r):
            values = b["after"][r, :] + (dot_nn(b["hidden"][r, :], weight[...]) + bias)
            if l + 1 < layers:
                held[l + 1]["current"][r, :] = values
            else:
                last[r, :] = values.astype(jnp.bfloat16)
        each_tile(b["after"].shape[0], body)
        if l + 1 < layers:
            save(l + 1, 0).start()
            normalize(l + 1)
        else:
            pltpu.make_async_copy(last, series_out, swap_sem.at[3]).start()

    tasks = {}

    def add(i, work):
        tasks.setdefault(i, []).append(work)

    lag = gather.iterations - layers * UNITS

    def early():
        gather.tiny_pass()
        gather.tiny_ready()
        expand_small(tiny_ref, vec, layers, gather.shard, part)
        pltpu.make_async_copy(vec, vec_out, swap_sem.at[4]).start()
        fill_bias(bias_ref, length, pad_ref, starts_ref, count_ref)
        pltpu.make_async_copy(bias_ref, bias_out, swap_sem.at[5]).start()

    def begin():
        own_copy.wait()
        swap_copy.wait_recv()
        save(0, 0).start()
        normalize(0)

    def pull(u):
        gather.ready(u)
        fetch(u).start()

    add(1, early)
    add(BEGIN, begin)
    units = layers * UNITS
    computing = []
    for l in range(layers):
        computing += [[lambda l=l, n=n: project(l, n)] for n in range(3)]
        computing[-1].append(lambda l=l: attention(l, True))
        computing.append([lambda l=l: attention(l, False), lambda l=l: output(l)])
        computing.append([lambda l=l: expand(l)])
        computing.append([lambda l=l: contract(l)])
    for u in range(units):
        add(u + lag, lambda u=u: pull(u))
        for one in computing[u]:
            add(min(u + lag + 1, gather.iterations - 1), one)

    own_copy.start()
    small_ref[...] = jnp.zeros_like(small_ref)
    shard = gather.shard
    for l in range(layers):
        for n in range(2):
            small_ref[2 * l + n : 2 * l + n + 1, :shard] = gains_ref[l, n : n + 1, :].astype(jnp.float32)
    groups = ((2 * layers, up_bias_ref, shard), (3 * layers, down_bias_ref, shard), (4 * layers, scale_ref, part))
    for base, ref, size in groups:
        small_ref[base : base + layers, :size] = ref[...].astype(jnp.float32)
    gather.begin()
    swap_copy.start()

    @pl.loop(0, gather.iterations)
    def _(i):
        gather.step(i)
        for when, work in sorted(tasks.items()):
            @pl.when(i == when)
            def _(work=work):
                for one in work:
                    one()

    swap_copy.wait_send()
    pltpu.make_async_copy(last, series_out, swap_sem.at[3]).wait()
    pltpu.make_async_copy(vec, vec_out, swap_sem.at[4]).wait()
    pltpu.make_async_copy(bias_ref, bias_out, swap_sem.at[5]).wait()
    for l in range(layers):
        for n in range(per):
            save(l, n).wait()
    gather.finish()


def saved_shapes(layers, length, total, width):
    low, wide = jnp.bfloat16, jnp.float32
    shapes = []
    for l in range(layers):
        count = length if l == layers - 1 else total
        kind = low if l == 0 else wide
        shapes.append(
            [
                ((total, width), kind),
                ((width, total), low),
                ((width, count), low),
                ((width, total), low),
                ((width, total), low),
                ((HEADS, 1, count), wide),
                ((width, count), low),
                ((count, width), wide),
                ((count, width), low),
                ((count, width), wide),
                ((count, width), low),
            ]
        )
    return shapes


def forward_pass(nz, series, matrices, vectors, spans):
    layers, shard, width = matrices[1].shape
    length, part = series.shape[0], vectors[3].shape[1]
    total = 2 * length
    units = layers * UNITS
    low, wide = jnp.bfloat16, jnp.float32
    shapes = [one for group in saved_shapes(layers, length, total, width) for one in group]
    small = (5 * layers + -5 * layers % 16, shard + -shard % 128)
    dma = pltpu.SemaphoreType.DMA
    anywhere = pl.BlockSpec(memory_space=pl.ANY)
    inside = pl.BlockSpec(memory_space=pltpu.VMEM)
    scalars = pl.BlockSpec(memory_space=pltpu.SMEM)
    count = 2 * nz
    results = pl.pallas_call(
        functools.partial(forward_kernel, nz, layers, part),
        out_shape=(
            jax.ShapeDtypeStruct((units, count * shard, width), low),
            jax.ShapeDtypeStruct((small[0], width), wide),
            jax.ShapeDtypeStruct((length, width), low),
            jax.ShapeDtypeStruct((total, total), wide),
        )
        + tuple(jax.ShapeDtypeStruct(*one) for one in shapes),
        in_specs=[anywhere] * 5 + [inside] * 4 + [scalars] * 3,
        out_specs=(anywhere,) * (4 + len(shapes)),
        scratch_shapes=[pltpu.VMEM(*one) for one in shapes]
        + [
            pltpu.VMEM((total, width), low),
            pltpu.VMEM((2, width, width), low),
            pltpu.VMEM((small[0], width), wide),
            pltpu.VMEM((length, width), low),
            pltpu.VMEM((count,) + small, low),
            pltpu.VMEM(small, wide),
            pltpu.VMEM((total, total), wide),
            dma((6,)),
            dma((2,)),
            dma((layers, 11)),
        ]
        + gather_scratch(nz, layers, shard, width),
        compiler_params=pltpu.CompilerParams(
            collective_id=1, has_side_effects=True, vmem_limit_bytes=60 << 20
        ),
    )(series, *matrices, *vectors, *spans)
    full, vec, out, bias = results[:4]
    saved = [results[4 + 11 * l : 15 + 11 * l] for l in range(layers)]
    return full, vec, out, bias, saved


def fill_bias(bias_ref, length, pad_ref, starts_ref, count_ref):
    s = lax.axis_index("seq")
    total = bias_ref.shape[0]
    pad, count = pad_ref[0], count_ref[0]

    def place(index):
        return jnp.where(index < length, s * length + index, -s * length + index)

    query = place(lax.broadcasted_iota(jnp.int32, (ROWS, total), 1))

    @pl.loop(0, total // ROWS)
    def _(i):
        key = place(lax.broadcasted_iota(jnp.int32, (ROWS, total), 0) + i * ROWS)
        seen = key <= query
        for slot in range(starts_ref.shape[1]):
            start = jnp.where(slot < count, starts_ref[0, slot], -2 * SPAN)
            stop = start + SPAN
            seen = seen | (key >= start) & (key < stop) & (query >= start) & (query < stop)
        allowed = (seen & (key >= pad)) | (key == query)
        rows = pl.ds(pl.multiple_of(i * ROWS, ROWS), ROWS)
        bias_ref[rows, :] = jnp.where(allowed, 0.0, NEG_FILL)


SLOTS = 14
LAGS = (1, 3, 6, 8, 10, 12)


class Reduce:
    def __init__(
        self, nz, units, full_ref, tiny, tiny_out, grads, held, bx, by, near, far, swap, tiny_in,
        as_, ar, bs, br, zs, zr, es, er, ls, ps, pr, ts, tr, free,
    ):
        self.__dict__.update(locals())
        self.at = Place(nz)
        self.slots, _, self.half, self.width = held.shape
        self.shard = 2 * self.half
        self.wide, self.low = self.width // 2, nz // 2
        self.steps = range(1, nz)
        self.parts = 2 * units
        self.iterations = self.parts + LAGS[-1]
        self.side = self.column(self.at.z)

    def column(self, z):
        return jnp.where(z < self.low, self.at.s, self.at.r)

    def cols(self, side):
        return pl.ds(pl.multiple_of(side * self.wide, 128), self.wide)

    def slot(self, h):
        return lax.rem(h, self.slots)

    def band(self, h):
        return pl.ds(pl.multiple_of(lax.rem(h, 2) * self.half, 16), self.half)

    def z_peer(self, d):
        at = self.at
        z = lax.rem(at.z + d, self.nz) if 2 * d == self.nz else at.z + 1 - 2 * lax.rem(at.z, 2)
        return z, (at.r, 2 * z + at.c, at.s)

    def pair_peer(self):
        at, first = self.at, self.at.z < self.low
        return (jnp.where(first, 1 - at.r, at.r), at.f, jnp.where(first, at.s, 1 - at.s))

    def last_peer(self):
        at, first = self.at, self.at.z < self.low
        return (jnp.where(first, at.r, 1 - at.r), at.f, jnp.where(first, 1 - at.s, at.s))

    def a_copy(self, h):
        piece = self.grads.at[:, 1 - self.at.c, self.band(h), :]
        return remote(piece, self.held.at[self.slot(h)], self.as_.at[h], self.ar.at[h], self.at.core())

    def bx_copy(self, h):
        piece = self.held.at[self.slot(h), pl.ds(0, self.low), :, self.cols(1 - self.at.s)]
        return remote(piece, self.bx.at[h], self.bs.at[h, 0], self.br.at[h, 0], self.at.x())

    def by_copy(self, h):
        piece = self.held.at[self.slot(h), pl.ds(self.low, self.low), :, self.cols(1 - self.at.r)]
        return remote(piece, self.by.at[h], self.bs.at[h, 1], self.br.at[h, 1], self.at.y())

    def near_copy(self, h, n):
        target = n * 2 + 1 - lax.rem(self.at.z, 2)
        side = (self.at.s, self.at.r)[n]
        piece = self.held.at[self.slot(h), target, :, self.cols(side)]
        return remote(piece, self.near.at[h, n], self.zs.at[h, n], self.zr.at[h, n], self.z_peer(1)[1])

    def far_copy(self, h):
        z, peer = self.z_peer(2)
        piece = self.held.at[self.slot(h), z, :, self.cols(self.column(z))]
        return remote(piece, self.far.at[h], self.zs.at[h, 2], self.zr.at[h, 2], peer)

    def pair_copy(self, h):
        piece = self.held.at[self.slot(h), self.at.z, :, self.cols(self.side)]
        return remote(piece, self.swap.at[h], self.es.at[h], self.er.at[h], self.pair_peer())

    def spot(self, h):
        return self.full_ref.at[lax.div(h, 2), self.band(h), self.cols(self.side)]

    def put_copy(self, h):
        return pltpu.make_async_copy(self.bx.at[h, 0], self.spot(h), self.ls.at[h])

    def last_copy(self, h):
        return remote(self.bx.at[h, 0], self.spot(h), self.ps.at[h], self.pr.at[h], self.last_peer())

    def plus(self, *values):
        return sum(v.astype(jnp.float32) for v in values).astype(jnp.bfloat16)

    def a_start(self, h):
        @pl.when(h >= self.slots)
        def _():
            pl.semaphore_wait(self.free, 1)
        self.a_copy(h).start()

    def a_stage(self, h):
        held, slot, c = self.held, self.slot(h), self.at.c
        self.a_copy(h).wait_recv()

        @pl.loop(0, self.nz)
        def _(z):
            held[slot, z] = self.plus(held[slot, z], self.grads[z, c, self.band(h), :])
        self.bx_copy(h).start()
        self.by_copy(h).start()
        self.a_copy(h).wait_send()

    def b_stage(self, h):
        held, slot, at = self.held, self.slot(h), self.at
        for copy, came, base, side in (
            (self.bx_copy(h), self.bx, 0, at.s),
            (self.by_copy(h), self.by, self.low, at.r),
        ):
            copy.wait()

            @pl.loop(0, self.low)
            def _(z, came=came, base=base, side=side):
                mine = self.cols(side)
                held[slot, base + z, :, mine] = self.plus(held[slot, base + z, :, mine], came[h, z])
        for n in range(2):
            self.near_copy(h, n).start()

    def near_stage(self, h):
        held, slot, at = self.held, self.slot(h), self.at
        for n in range(2):
            self.near_copy(h, n).wait()
            target, mine = 2 * n + lax.rem(at.z, 2), self.cols((at.s, at.r)[n])
            held[slot, target, :, mine] = self.plus(held[slot, target, :, mine], self.near[h, n])
        self.far_copy(h).start()

    def far_stage(self, h):
        held, slot, z, mine = self.held, self.slot(h), self.at.z, self.cols(self.side)
        self.far_copy(h).wait()
        held[slot, z, :, mine] = self.plus(held[slot, z, :, mine], self.far[h])
        self.pair_copy(h).start()

    def pair_stage(self, h):
        held, slot, z, mine = self.held, self.slot(h), self.at.z, self.cols(self.side)
        self.pair_copy(h).wait()
        self.bx[h, 0] = self.plus(held[slot, z, :, mine], self.swap[h])

        @pl.when(h + self.slots < self.parts)
        def _():
            pl.semaphore_signal(self.free, inc=1, device_id=self.at.core(), device_id_type=MESH)
        self.put_copy(h).start()
        self.last_copy(h).start()

    def close(self, h):
        self.put_copy(h).wait()
        self.last_copy(h).wait()

    def step(self, i):
        def stage(lag, work):
            h = i - lag
            pl.when((h >= 0) & (h < self.parts))(lambda: work(h))

        works = (self.a_stage, self.b_stage, self.near_stage, self.far_stage, self.pair_stage, self.close)
        for lag, work in zip(LAGS, works):
            stage(lag, work)

    def launch(self, i):
        @pl.when((lax.rem(i, 2) == 0) & (i < self.parts))
        def _():
            self.a_start(i)
            self.a_start(i + 1)

    def tiny_copy(self, n, peer):
        return remote(self.tiny, self.tiny_in.at[n], self.ts.at[n], self.tr.at[n], peer)

    def tiny_z(self, d):
        return remote(self.tiny, self.tiny_in.at[2 + d], self.ts.at[2 + d], self.tr.at[2 + d], self.at.to(d))

    def tiny_step(self, n):
        peers = (self.at.core(), self.at.x(), self.at.y())
        if 0 < n <= 3:
            copy = self.tiny_copy(n - 1, peers[n - 1])
            copy.wait()
            self.tiny[...] = self.tiny[...] + self.tiny_in[n - 1]
        if n < 3:
            self.tiny_copy(n, peers[n]).start()
        if n == 3:
            for d in self.steps:
                self.tiny_z(d).start()
        if n == 4:
            for d in self.steps:
                self.tiny_z(d).wait()
            self.tiny_out[...] = self.tiny[...] + sum(self.tiny_in[2 + d] for d in self.steps)


def backward_kernel(nz, layers, length, total, *refs):
    cot_ref, full_ref, vec, bias_ref = refs[:4]
    per = 11
    saved = [refs[4 + per * l : 4 + per * (l + 1)] for l in range(layers)]
    refs = refs[4 + per * layers :]
    share_ref, tiny_out, input_ref = refs[:3]
    (
        up, wide_a, wide_b, hidden, mixed, pre_low, low, trio, att, do, lse, weight, came, sent,
        load_sem, weight_sem, x_sem, tiny, grads,
    ) = refs[3:22]
    units = layers * UNITS
    k, v, q = trio.at[0], trio.at[1], trio.at[2]
    reduce = Reduce(nz, units, share_ref, tiny, tiny_out, grads, *refs[22:])
    at = reduce.at
    width = up.shape[1]
    wide, half_z = width // 2, nz // 2
    shard = reduce.shard
    names = ("current", "normed_t", "q", "k", "v", "lse", "att", "after", "mixed", "pre", "hidden")
    homes = dict(
        normed_t=att, q=q, k=k, v=v, lse=lse, att=att, after=wide_b, mixed=mixed, pre=wide_a, hidden=hidden
    )

    def load(l, name):
        n = names.index(name)
        source = saved[l][n]
        home = homes.get(name, hidden if source.dtype == jnp.bfloat16 else wide_b)
        if home.shape != source.shape:
            if len(source.shape) == 3:
                home = home.at[:, :, pl.ds(0, source.shape[2])]
            elif source.shape[0] != home.shape[0]:
                home = home.at[pl.ds(0, source.shape[0]), :]
            else:
                home = home.at[:, pl.ds(0, source.shape[1])]
        return pltpu.make_async_copy(source, home, load_sem.at[l, n])

    def fetch(u):
        return pltpu.make_async_copy(full_ref.at[u], weight, weight_sem.at[0])

    def fill(product):
        @pl.loop(0, 2)
        def _(i):
            @pl.loop(0, 2)
            def _(j):
                r = pl.ds(pl.multiple_of(i * wide, 128), wide)
                c = pl.ds(pl.multiple_of(j * wide, 128), wide)
                value = product(r, c).astype(jnp.bfloat16).reshape(half_z, 2, shard, wide)
                grads[pl.ds(i * half_z, half_z), :, :, c] = value

    def vector(n):
        return vec[n : n + 1, :]

    def gather_row(n, values):
        tiny[n : n + 1, :] = tiny[n : n + 1, :] + jnp.sum(values, axis=0, keepdims=True)

    def norm_tile(values, gain, w, n):
        inverse = lax.rsqrt(jnp.mean(values * values, axis=-1, keepdims=True) + EPSILON)
        scaled = w * gain
        inner = jnp.mean(values * scaled, axis=-1, keepdims=True)
        gather_row(n, w * values * inverse)
        return inverse * scaled - values * (inverse * inverse * inverse) * inner

    def count(l):
        return length if l == layers - 1 else total

    def next_load(l, *which):
        if l > 0:
            for name in which:
                load(l - 1, name).start()

    def down(l):
        m = count(l)
        load(l, "hidden").wait()

        def body(r):
            value = up[r, :].astype(jnp.bfloat16)
            low[r, :] = value
            gather_row(3 * layers + l, value.astype(jnp.float32))
        each_tile(m, body)
        fill(lambda r, c: dot_tn(hidden[:m, r], low[:m, c]))
        if saved[l][0].dtype == jnp.bfloat16:
            load(l, "current").start()
        else:
            next_load(l, "hidden")

    def expand(l):
        fetch(l * UNITS + 5).wait()
        load(l, "pre").wait()

        def body(r):
            grown = dot_nt(low[r, :], weight[...])
            value = wide_a[r, :]
            gate = 1.0 / (1.0 + jnp.exp(-value))
            result = (grown * gate * (1.0 + value * (1.0 - gate))).astype(jnp.bfloat16)
            pre_low[r, :] = result
            gather_row(2 * layers + l, result.astype(jnp.float32))
        each_tile(count(l), body, TALL)
        fetch(l * UNITS + 4).start()

    def fill_up(l):
        m = count(l)
        load(l, "mixed").wait()
        fill(lambda r, c: dot_tn(mixed[:m, r], pre_low[:m, c]))
        next_load(l, "mixed")

    def output(l):
        fetch(l * UNITS + 4).wait()
        load(l, "after").wait()
        gain = vector(2 * l + 1)

        def body(r):
            w = dot_nt(pre_low[r, :], weight[...])
            value = up[r, :] + norm_tile(wide_b[r, :], gain, w, 2 * l + 1)
            up[r, :] = value
            low[r, :] = value.astype(jnp.bfloat16)
        each_tile(count(l), body, TALL)
        fetch(l * UNITS + 3).start()
        if saved[l][0].dtype != jnp.bfloat16:
            load(l, "current").start()

    def fill_out(l):
        m = count(l)
        load(l, "att").wait()
        fill(lambda r, c: dot_nn(att[r, :m], low[:m, c]))
        load(l, "normed_t").start()

    def attention(l, start, stop):
        m = count(l)
        row = 4 * layers + l
        factor = jnp.broadcast_to(vec[row : row + 1, 0:128], (128, 128)).T[0:HEAD, 0:1]

        def head(h, sums):
            rows = head_rows(h)
            kh, vh, qh, oh = k[rows, :], v[rows, :], q[rows, :m], do[rows, :m]
            scores = dot_tn(kh, qh) + bias_ref[:, :m]
            probs = jnp.exp(scores - lse[h, :, :m])
            weighted = probs * dot_tn(vh, oh)
            inner = jnp.sum(weighted, axis=0, keepdims=True)
            score = (weighted - probs * inner).astype(jnp.bfloat16)
            v[rows, :] = dot_nt(oh, probs.astype(jnp.bfloat16)).astype(jnp.bfloat16)
            k[rows, :] = dot_nt(qh, score).astype(jnp.bfloat16)
            query = dot_nn(kh, score)
            q[rows, :m] = (query * factor).astype(jnp.bfloat16)
            return sums + jnp.sum(query * qh.astype(jnp.float32), axis=1, keepdims=True)

        sums = lax.fori_loop(start, stop, head, jnp.zeros((HEAD, 1), jnp.float32))
        flat = jnp.broadcast_to(sums, (HEAD, 128)).T
        tiny[row : row + 1, 0:HEAD] = tiny[row : row + 1, 0:HEAD] + flat[0:1, :]

    def open_heads(l):
        m = count(l)
        fetch(l * UNITS + 3).wait()

        def body(r):
            do[r, :m] = dot_nt(weight[r, :], low[:m, :]).astype(jnp.bfloat16)
        each_tile(width, body, wide)
        fetch(l * UNITS + 1).start()
        for name in ("q", "k", "v", "lse"):
            load(l, name).wait()

    def turn(l):
        next_load(l, "lse")
        load(l, "normed_t").wait()

    def fill_project(n):
        fill(lambda r, c: dot_nt(att[r, :], trio[n, c, :]))

    def project(l, n):
        fetch(l * UNITS + lax.rem(n + 1, 3)).wait()
        count = jnp.where((n == 2) & (l == layers - 1), length, total)

        @pl.loop(0, lax.div(count, TALL))
        def _(i):
            r = pl.ds(pl.multiple_of(i * TALL, TALL), TALL)
            value = dot_nt(trio[n, :, r].T, weight[...])
            wide_a[r, :] = value + jnp.where(n > 0, wide_a[r, :], 0.0)

    def settle(l, n):
        if n < 2:
            fetch(l * UNITS + (2, 0)[n]).start()
            return
        if l > 0:
            fetch((l - 1) * UNITS + 5).start()
        load(l, "current").wait()
        gain = vector(2 * l)
        current = hidden if saved[l][0].dtype == jnp.bfloat16 else wide_b

        def close(r):
            return norm_tile(current[r, :].astype(jnp.float32), gain, wide_a[r, :], 2 * l)

        own = count(l)

        def first(r):
            up[r, :] = up[r, :] + close(r)
        each_tile(own, first)
        if own < total:
            @pl.loop(own // ROWS, total // ROWS)
            def _(i):
                r = pl.ds(pl.multiple_of(i * ROWS, ROWS), ROWS)
                up[r, :] = close(r)
        next_load(l, "pre", "after", "att", "q", "k", "v")
        if l == 0:
            sent[...] = up[length:, :].astype(jnp.bfloat16)
            reply.start()

    reply = remote(sent, came, x_sem.at[0], x_sem.at[1], at.x())
    def start_layer(l):
        down(l)
        expand(l)

    def middle(l):
        open_heads(l)
        fill_up(l)

    before = {0: start_layer, 1: output, 2: middle, 4: fill_out}
    heads = (0, 0, 0, 1, 6, 9, 14, HEADS)
    after = {6: turn}
    later = {7: lambda l: settle(l, 0), 9: lambda l: settle(l, 1), 11: lambda l: settle(l, 2)}
    last = layers - 1
    start_copy = pltpu.make_async_copy(cot_ref, sent, x_sem.at[2])
    start_copy.start()
    for name in ("hidden", "pre", "mixed", "after", "att", "q", "k", "v", "lse"):
        load(last, name).start()
    fetch(last * UNITS + 5).start()
    tiny[...] = jnp.zeros_like(tiny)
    if count(last) < total:
        trio[2, :, count(last) :] = jnp.zeros((width, total - count(last)), jnp.bfloat16)
    at.greet()
    start_copy.wait()
    up[:length, :] = sent[...].astype(jnp.float32)

    @pl.loop(0, reduce.iterations)
    def _(i):
        reduce.step(i)
        phase, layer = lax.rem(i, 2 * UNITS), last - lax.div(i, 2 * UNITS)
        inside = (i < reduce.parts) & (phase >= UNITS)

        def tasks(some):
            for l in range(layers):
                for n, one in some:
                    @pl.when(i == (last - l) * 2 * UNITS + n)
                    def _(one=one, l=l):
                        one(l)

        tasks(before.items())
        first = sum(jnp.where(phase == n, heads[n], 0) for n in range(2, 7))
        final = sum(jnp.where(phase == n, heads[n + 1], 0) for n in range(2, 7))
        for l in range(layers):
            @pl.when((phase >= 2) & (phase < 7) & (layer == l))
            def _(l=l):
                attention(l, first, final)

        tasks(after.items())

        @pl.when(inside & (lax.rem(phase, 2) == 0))
        def _():
            fill_project(lax.div(phase - UNITS, 2))

        @pl.when(inside & (lax.rem(phase, 2) == 1))
        def _():
            project(layer, lax.div(phase - UNITS, 2))

        tasks(later.items())
        reduce.launch(i)
        for n in range(5):
            @pl.when(i == reduce.parts + n)
            def _(n=n):
                reduce.tiny_step(n)
                if n == 2:
                    reply.wait()
                    input_ref[...] = (up[:length, :] + came[...].astype(jnp.float32)).astype(jnp.bfloat16)


def backward_pass(nz, cotangent, full, vec, bias, saved):
    layers = len(saved)
    units = layers * UNITS
    length, width = cotangent.shape
    total = bias.shape[0]
    shard = width // (2 * nz)
    half, wide, low, n = shard // 2, width // 2, nz // 2, nz - 1
    parts = 2 * units
    slots = min(SLOTS, parts)
    flat = [one for group in saved for one in group]
    rows = vec.shape[0]
    dma = pltpu.SemaphoreType.DMA
    small, large = jnp.bfloat16, jnp.float32
    anywhere = pl.BlockSpec(memory_space=pl.ANY)
    inside = pl.BlockSpec(memory_space=pltpu.VMEM)
    natural, turned = (total, width), (width, total)
    return pl.pallas_call(
        functools.partial(backward_kernel, nz, layers, length, total),
        out_shape=(
            jax.ShapeDtypeStruct((units, shard, width), small),
            jax.ShapeDtypeStruct((rows, width), large),
            jax.ShapeDtypeStruct((length, width), small),
        ),
        in_specs=[anywhere, anywhere, inside, inside] + [anywhere] * len(flat),
        out_specs=(anywhere, inside, inside),
        scratch_shapes=[
            pltpu.VMEM(natural, large),
            pltpu.VMEM(natural, large),
            pltpu.VMEM(natural, large),
            pltpu.VMEM(natural, small),
            pltpu.VMEM(natural, small),
            pltpu.VMEM(natural, small),
            pltpu.VMEM(natural, small),
            pltpu.VMEM((3,) + turned, small),
            pltpu.VMEM(turned, small),
            pltpu.VMEM(turned, small),
            pltpu.VMEM((HEADS, 1, total), large),
            pltpu.VMEM((width, width), small),
            pltpu.VMEM((length, width), small),
            pltpu.VMEM((length, width), small),
            dma((layers, 11)),
            dma((1,)),
            dma((3,)),
            pltpu.VMEM((rows, width), large),
            pltpu.VMEM((nz, 2, shard, width), small),
            pltpu.VMEM((slots, nz, half, width), small),
            pltpu.VMEM((parts, low, half, wide), small),
            pltpu.VMEM((parts, low, half, wide), small),
            pltpu.VMEM((parts, 2, half, wide), small),
            pltpu.VMEM((parts, half, wide), small),
            pltpu.VMEM((parts, half, wide), small),
            pltpu.VMEM((3 + n, rows, width), large),
            dma((parts,)), dma((parts,)),
            dma((parts, 2)), dma((parts, 2)),
            dma((parts, 3)), dma((parts, 3)),
            dma((parts,)), dma((parts,)),
            dma((parts,)),
            dma((parts,)), dma((parts,)),
            dma((3 + n,)), dma((3 + n,)),
            pltpu.SemaphoreType.REGULAR,
        ],
        compiler_params=pltpu.CompilerParams(
            collective_id=2, has_side_effects=True, vmem_limit_bytes=63 << 20
        ),
    )(cotangent, full, vec, bias, *flat)


def forward_layer(current, weights, allowed, series_count, local_length, total_length):
    qkv_weight, out_weight, up_weight, down_weight, norm_gains, up_bias, down_bias, query_scale = (
        weights
    )
    token_count, model_width = current.shape
    normed, inverse_one = norm_rows(current, norm_gains[0].astype(jnp.float32))
    normed_low = normed.astype(jnp.bfloat16).reshape(series_count, local_length, model_width)
    projected = jnp.einsum(
        "bld,kdc->bkcl", normed_low, qkv_weight, preferred_element_type=jnp.float32
    ).reshape(series_count, 3 * model_width, local_length)
    query_raw = projected[:, :model_width]
    factor = query_factor(query_scale)
    query_low = (
        query_raw.reshape(series_count, HEADS, HEAD, local_length) * factor[None, None, :, None]
    ).astype(jnp.bfloat16)
    pair_low = projected[:, model_width:].astype(jnp.bfloat16)
    pair_all = lax.all_gather(pair_low, "seq", axis=2, tiled=True)
    key_all = pair_all[:, :model_width].reshape(series_count, HEADS, HEAD, total_length)
    value_all = pair_all[:, model_width:].reshape(series_count, HEADS, HEAD, total_length)
    scores = jnp.einsum("bheq,bhek->bhqk", query_low, key_all, preferred_element_type=jnp.float32)
    scores = jnp.where(allowed[:, None], scores, NEG_FILL)
    top_score = jnp.max(scores, axis=-1, keepdims=True)
    exp_scores = jnp.exp(scores - top_score)
    exp_total = jnp.sum(exp_scores, axis=-1, keepdims=True)
    probs_low = (exp_scores / exp_total).astype(jnp.bfloat16)
    log_total = top_score + jnp.log(exp_total)
    attended = jnp.einsum(
        "bhqk,bhek->bheq", probs_low, value_all, preferred_element_type=jnp.float32
    )
    attended_low = attended.astype(jnp.bfloat16).reshape(series_count, model_width, local_length)
    attn_out = jnp.einsum(
        "bdl,de->ble", attended_low, out_weight, preferred_element_type=jnp.float32
    )
    after_attn = current + attn_out.reshape(token_count, model_width)
    normed_two, inverse_two = norm_rows(after_attn, norm_gains[1].astype(jnp.float32))
    mixed_low = normed_two.astype(jnp.bfloat16)
    hidden_pre = jnp.dot(mixed_low, up_weight, preferred_element_type=jnp.float32) + up_bias.astype(
        jnp.float32
    )
    hidden_low = jax.nn.silu(hidden_pre).astype(jnp.bfloat16)
    result = after_attn + (
        jnp.dot(hidden_low, down_weight, preferred_element_type=jnp.float32)
        + down_bias.astype(jnp.float32)
    )
    stored = (
        current,
        inverse_one,
        normed_low,
        query_raw,
        query_low,
        key_all,
        value_all,
        log_total,
        attended_low,
        after_attn,
        inverse_two,
        mixed_low,
        hidden_pre,
        hidden_low,
    )
    return (result, stored)


def backward_layer(upstream, weights, stored, allowed, series_count, local_length, total_length):
    qkv_weight, out_weight, up_weight, down_weight, norm_gains, up_bias, down_bias, query_scale = (
        weights
    )
    (
        current,
        inverse_one,
        normed_low,
        query_raw,
        query_low,
        key_all,
        value_all,
        log_total,
        attended_low,
        after_attn,
        inverse_two,
        mixed_low,
        hidden_pre,
        hidden_low,
    ) = stored
    token_count, model_width = current.shape
    down_low = upstream.astype(jnp.bfloat16)
    grad_down_bias = jnp.sum(down_low, axis=0, dtype=jnp.float32)
    grad_down = jnp.einsum("tf,td->fd", hidden_low, down_low, preferred_element_type=jnp.float32)
    hidden_grad = jnp.einsum("td,fd->tf", down_low, down_weight, preferred_element_type=jnp.float32)
    sigmoid_pre = jax.nn.sigmoid(hidden_pre)
    pre_low = (hidden_grad * sigmoid_pre * (1.0 + hidden_pre * (1.0 - sigmoid_pre))).astype(
        jnp.bfloat16
    )
    grad_up_bias = jnp.sum(pre_low, axis=0, dtype=jnp.float32)
    grad_up = jnp.einsum("td,tf->df", mixed_low, pre_low, preferred_element_type=jnp.float32)
    mixed_grad = jnp.einsum("tf,df->td", pre_low, up_weight, preferred_element_type=jnp.float32)
    norm_grad_two, gain_grad_two = norm_back(
        after_attn, inverse_two, norm_gains[1].astype(jnp.float32), mixed_grad
    )
    attn_grad = upstream + norm_grad_two
    branch_low = attn_grad.astype(jnp.bfloat16).reshape(series_count, local_length, model_width)
    grad_out = jnp.einsum(
        "bdl,ble->de", attended_low, branch_low, preferred_element_type=jnp.float32
    )
    output_low = (
        jnp.einsum("ble,de->bdl", branch_low, out_weight, preferred_element_type=jnp.float32)
        .astype(jnp.bfloat16)
        .reshape(series_count, HEADS, HEAD, local_length)
    )
    scores = jnp.einsum("bheq,bhek->bhqk", query_low, key_all, preferred_element_type=jnp.float32)
    scores = jnp.where(allowed[:, None], scores, NEG_FILL)
    attn_probs = jnp.exp(scores - log_total)
    prob_grad = jnp.einsum(
        "bheq,bhek->bhqk", output_low, value_all, preferred_element_type=jnp.float32
    )
    row_inner = jnp.sum(attn_probs * prob_grad, axis=-1, keepdims=True)
    score_low = (attn_probs * (prob_grad - row_inner)).astype(jnp.bfloat16)
    value_grad = jnp.einsum(
        "bhqk,bheq->bhek",
        attn_probs.astype(jnp.bfloat16),
        output_low,
        preferred_element_type=jnp.float32,
    )
    key_grad = jnp.einsum(
        "bhqk,bheq->bhek", score_low, query_low, preferred_element_type=jnp.float32
    )
    query_grad = jnp.einsum(
        "bhqk,bhek->bheq", score_low, key_all, preferred_element_type=jnp.float32
    )
    pair_grad = jnp.concatenate(
        [
            key_grad.reshape(series_count, model_width, total_length),
            value_grad.reshape(series_count, model_width, total_length),
        ],
        axis=1,
    )
    pair_local = lax.psum_scatter(pair_grad, "seq", scatter_dimension=2, tiled=True)
    key_local, value_local = pair_local[:, :model_width], pair_local[:, model_width:]
    factor = query_factor(query_scale)
    factor_grad = jnp.sum(
        query_grad * query_raw.reshape(series_count, HEADS, HEAD, local_length), axis=(0, 1, 3)
    )
    grad_scale = (
        factor_grad * jax.nn.sigmoid(query_scale.astype(jnp.float32)) * (SOFT_ONE / math.sqrt(HEAD))
    )
    raw_low = (
        (query_grad * factor[None, None, :, None])
        .astype(jnp.bfloat16)
        .reshape(series_count, model_width, local_length)
    )
    projected_grad = jnp.concatenate(
        [raw_low, key_local.astype(jnp.bfloat16), value_local.astype(jnp.bfloat16)], axis=1
    )
    grad_qkv = jnp.einsum(
        "bld,bcl->dc", normed_low, projected_grad, preferred_element_type=jnp.float32
    )
    normed_grad = jnp.einsum(
        "bkcl,kdc->bld",
        projected_grad.reshape(series_count, 3, model_width, local_length),
        qkv_weight,
        preferred_element_type=jnp.float32,
    ).reshape(token_count, model_width)
    norm_grad_one, gain_grad_one = norm_back(
        current, inverse_one, norm_gains[0].astype(jnp.float32), normed_grad
    )
    result = attn_grad + norm_grad_one
    layer_grads = (
        grad_qkv,
        grad_out,
        grad_up,
        grad_down,
        jnp.stack([gain_grad_one, gain_grad_two]),
        grad_up_bias,
        grad_down_bias,
        grad_scale,
    )
    return (result, layer_grads)


def pack_small(norm_gains, up_bias, down_bias, query_scale):
    layers, _, shard = norm_gains.shape
    scale = jnp.pad(query_scale, ((0, 0), (0, shard - query_scale.shape[1])))
    rows = jnp.concatenate([norm_gains.reshape(2 * layers, shard), up_bias, down_bias, scale])
    return jnp.pad(rows, ((0, -rows.shape[0] % 16), (0, -shard % 128)))


def unpack_small(tiny, layers, shard, scale_shard):
    count = tiny.shape[0]
    vectors = tiny[:, : 4 * layers, :shard].transpose(1, 0, 2).reshape(4 * layers, count * shard)
    scale = tiny[:, 4 * layers : 5 * layers, :scale_shard].transpose(1, 0, 2).reshape(layers, count * scale_shard)
    gains = vectors[: 2 * layers].reshape(layers, 2, count * shard)
    return gains, vectors[2 * layers : 3 * layers], vectors[3 * layers :], scale


def pack_tiny(layer_grads, count):
    gains = jnp.concatenate([g[4] for g in layer_grads])
    vectors = jnp.concatenate(
        [gains, jnp.stack([g[5] for g in layer_grads]), jnp.stack([g[6] for g in layer_grads])]
    )
    scale = jnp.stack([g[7] for g in layer_grads])
    shard, part = vectors.shape[1] // count, scale.shape[1] // count
    vectors = vectors.reshape(-1, count, shard)
    scale = jnp.pad(scale.reshape(-1, count, part), ((0, 0), (0, 0), (0, shard - part)))
    rows = jnp.concatenate([vectors, scale]).transpose(1, 0, 2)
    return jnp.pad(rows, ((0, 0), (0, -rows.shape[1] % 16), (0, -shard % 128)))


def unpack_tiny(tiny, layers, shard, part):
    gains = tiny[: 2 * layers, :shard].reshape(layers, 2, shard)
    up, down = tiny[2 * layers : 3 * layers, :shard], tiny[3 * layers : 4 * layers, :shard]
    return gains, up, down, tiny[4 * layers : 5 * layers, :part]


def gather_plain(qkv_weight, out_weight, up_weight, down_weight, small):
    layers, shard, width = out_weight.shape
    qkv = qkv_weight.reshape(layers, shard, 3, width).transpose(0, 2, 1, 3)
    square = jnp.stack([out_weight, up_weight, down_weight], axis=1)
    units = jnp.concatenate([qkv, square], axis=1).reshape(layers * UNITS, shard, width)
    full = lax.all_gather(units, "fsdp", axis=1, tiled=True)
    return full, lax.all_gather(small, "fsdp", axis=0)


def reduce_plain(layer_grads, tiny):
    units = []
    for grads in layer_grads:
        width = grads[0].shape[1]
        units += list(grads[:3]) + [grads[3][:, k * width : (k + 1) * width] for k in range(3)]
    shares = lax.psum_scatter(jnp.stack(units), "fsdp", scatter_dimension=1, tiled=True)
    small = lax.psum_scatter(tiny, "fsdp", scatter_dimension=0, tiled=True)[0]
    return lax.psum(shares, ("replica", "seq")), lax.psum(small, ("replica", "seq"))


def plain(
    series_in,
    cotangent,
    qkv_weight,
    out_weight,
    up_weight,
    down_weight,
    norm_gains,
    up_bias,
    down_bias,
    query_scale,
    pad_length,
    span_starts,
    span_count,
):
    series_count, local_length, model_width = series_in.shape
    seq_count = lax.axis_size("seq")
    group = lax.axis_size("fsdp")
    total_length = local_length * seq_count
    offset = lax.axis_index("seq") * local_length
    allowed = visible(pad_length, span_starts, span_count, offset, local_length, total_length)
    layer_count, shard = qkv_weight.shape[:2]
    scale_shard = query_scale.shape[1]
    small = pack_small(norm_gains, up_bias, down_bias, query_scale)
    full, tiny = gather_plain(qkv_weight, out_weight, up_weight, down_weight, small)
    gains, up_full, down_full, scale_full = unpack_small(tiny, layer_count, shard, scale_shard)
    weights = [
        (
            full[UNITS * l : UNITS * l + 3],
            full[UNITS * l + 3],
            full[UNITS * l + 4],
            full[UNITS * l + 5],
            gains[l],
            up_full[l],
            down_full[l],
            scale_full[l],
        )
        for l in range(layer_count)
    ]
    current = series_in.reshape(series_count * local_length, model_width).astype(jnp.float32)
    stored_list = []
    for l in range(layer_count):
        current, stored = forward_layer(
            current, weights[l], allowed, series_count, local_length, total_length
        )
        stored_list.append(stored)
    series_out = current.reshape(series_count, local_length, model_width).astype(jnp.bfloat16)
    upstream = cotangent.reshape(series_count * local_length, model_width).astype(jnp.float32)
    order = list(reversed(range(layer_count)))
    grads_list = {}
    for l in order:
        upstream, grads_list[l] = backward_layer(
            upstream, weights[l], stored_list[l], allowed, series_count, local_length, total_length
        )
    tiny_grads = pack_tiny([grads_list[l] for l in range(layer_count)], group)
    big = [
        tuple(grads_list[l][k].astype(jnp.bfloat16) for k in (3, 2, 1, 0)) for l in order
    ]
    shares, tiny_sum = reduce_plain(big, tiny_grads)
    shares = shares.reshape(layer_count, UNITS, shard, model_width)[::-1]
    grad_gains, grad_up_bias, grad_down_bias, grad_scale = unpack_tiny(
        tiny_sum, layer_count, shard, scale_shard
    )
    grad_qkv = shares[:, 3:].transpose(0, 2, 1, 3).reshape(layer_count, shard, 3 * model_width)
    input_grad = upstream.reshape(series_count, local_length, model_width).astype(jnp.bfloat16)
    return (
        series_out,
        input_grad,
        grad_qkv.astype(jnp.float32),
        shares[:, 2].astype(jnp.float32),
        shares[:, 1].astype(jnp.float32),
        shares[:, 0].astype(jnp.float32),
        grad_gains,
        grad_up_bias,
        grad_down_bias,
        grad_scale,
    )


def finish(shares, tiny, layers, shard, width, query_scale):
    shares = shares.reshape(layers, UNITS, shard, width)[::-1]
    low = jnp.float32
    place = lax.axis_index("fsdp")
    part = query_scale.shape[1]
    vectors = lax.dynamic_slice_in_dim(tiny[: 4 * layers], place * shard, shard, axis=1)
    scale = lax.dynamic_slice_in_dim(tiny[4 * layers : 5 * layers], place * part, part, axis=1)
    raw = query_scale.astype(jnp.float32)
    scale = scale * (jax.nn.sigmoid(raw) * (SOFT_ONE / math.sqrt(HEAD))) / query_factor(query_scale)
    qkv = jnp.concatenate([shares[:, 5], shares[:, 3], shares[:, 4]], axis=2)
    return (
        qkv.astype(low),
        shares[:, 2].astype(low),
        shares[:, 1].astype(low),
        shares[:, 0].astype(low),
        vectors[: 2 * layers].reshape(layers, 2, shard),
        vectors[2 * layers : 3 * layers],
        vectors[3 * layers :],
        scale,
    )


def fused(
    series_in,
    cotangent,
    qkv_weight,
    out_weight,
    up_weight,
    down_weight,
    norm_gains,
    up_bias,
    down_bias,
    query_scale,
    pad_length,
    span_starts,
    span_count,
):
    layers, shard, width = out_weight.shape
    nz = lax.axis_size("fsdp") // 2
    full, vec, series_out, bias, saved = forward_pass(
        nz,
        series_in[0],
        (qkv_weight, out_weight, up_weight, down_weight),
        (norm_gains, up_bias, down_bias, query_scale),
        (pad_length, span_starts, span_count),
    )
    shares, tiny, input_grad = backward_pass(nz, cotangent[0], full, vec, bias, saved)
    rest = finish(shares, tiny, layers, shard, width, query_scale)
    return (series_out[None], input_grad[None]) + rest


def shards(*args):
    series_in, out_weight = args[0], args[3]
    group = lax.axis_size("fsdp")
    width = series_in.shape[2]
    block = lax.axis_size("replica") == 2 and lax.axis_size("seq") == 2 and group == 8
    block = block and series_in.shape[0] == 1 and width == out_weight.shape[2] == HEADS * HEAD
    block = block and (width // group) % 32 == 0 and width % 256 == 0
    return fused(*args) if block else plain(*args)


def solution(mesh):
    return jax.shard_map(
        shards,
        mesh=mesh,
        in_specs=(
            P(("replica", "fsdp"), "seq", None),
            P(("replica", "fsdp"), "seq", None),
            P(None, "fsdp", None),
            P(None, "fsdp", None),
            P(None, "fsdp", None),
            P(None, "fsdp", None),
            P(None, None, "fsdp"),
            P(None, "fsdp"),
            P(None, "fsdp"),
            P(None, "fsdp"),
            P(("replica", "fsdp")),
            P(("replica", "fsdp"), None),
            P(("replica", "fsdp")),
        ),
        out_specs=(
            P(("replica", "fsdp"), "seq", None),
            P(("replica", "fsdp"), "seq", None),
            P(None, "fsdp", None),
            P(None, "fsdp", None),
            P(None, "fsdp", None),
            P(None, "fsdp", None),
            P(None, None, "fsdp"),
            P(None, "fsdp"),
            P(None, "fsdp"),
            P(None, "fsdp"),
        ),
        check_vma=False,
    )
```

```python
import functools
import math

import jax
import jax.numpy as jnp
from jax import lax
from jax.experimental import pallas as pl
from jax.experimental.pallas import tpu as pltpu
from jax.sharding import PartitionSpec as P

HEADS = 16
HEAD = 80
SPAN = 32


EPSILON = 1e-06
SOFT_ONE = 1.442695041
NEG_FILL = -1e30


def visible(pad_length, span_starts, span_count, offset, local_length, total_length):
    query_pos = offset + jnp.arange(local_length, dtype=jnp.int32)
    key_pos = jnp.arange(total_length, dtype=jnp.int32)
    shared = jnp.zeros((span_starts.shape[0], local_length, total_length), dtype=bool)
    for slot_index in range(span_starts.shape[1]):
        slot_start = span_starts[:, slot_index]
        slot_used = slot_index < span_count
        query_in = (
            slot_used[:, None]
            & (query_pos[None, :] >= slot_start[:, None])
            & (query_pos[None, :] < slot_start[:, None] + SPAN)
        )
        key_in = (key_pos[None, :] >= slot_start[:, None]) & (
            key_pos[None, :] < slot_start[:, None] + SPAN
        )
        shared = shared | query_in[:, :, None] & key_in[:, None, :]
    causal = key_pos[None, :] <= query_pos[:, None]
    allowed = (key_pos[None, None, :] >= pad_length[:, None, None]) & (causal[None] | shared)
    return allowed | (key_pos[None, None, :] == query_pos[None, :, None])


def norm_rows(values, scale_gain):
    inverse = lax.rsqrt(jnp.mean(values * values, axis=-1, keepdims=True) + EPSILON)
    return (values * inverse * scale_gain, inverse)


def norm_back(values, inverse, scale_gain, upstream):
    scaled = upstream * scale_gain
    inner_term = jnp.mean(values * scaled, axis=-1, keepdims=True)
    result = inverse * scaled - values * (inverse * inverse * inverse) * inner_term
    return (result, jnp.sum(upstream * values * inverse, axis=0))


def query_factor(query_scale):
    return jax.nn.softplus(query_scale.astype(jnp.float32)) * (SOFT_ONE / math.sqrt(HEAD))


MESH = pl.DeviceIdType.MESH
UNITS = 6
LAG = 1
PASS = 1
TURN = 1
TOP = 40


class Place:
    def __init__(self, nz):
        self.nz = nz
        self.r = lax.axis_index("replica")
        f = lax.axis_index("fsdp")
        self.s = lax.axis_index("seq")
        self.z = lax.div(f, 2)
        self.c = lax.rem(f, 2)
        self.f = f

    def x(self):
        return (self.r, self.f, 1 - self.s)

    def y(self):
        return (1 - self.r, self.f, self.s)

    def core(self):
        return (self.r, self.f + 1 - 2 * self.c, self.s)

    def to(self, d):
        return (self.r, lax.rem(self.z + d, self.nz) * 2 + self.c, self.s)

    def source(self, d):
        return lax.rem(self.z - d + self.nz, self.nz)

    def greet(self):
        barrier = pltpu.get_barrier_semaphore()
        peers = [self.x(), self.y(), self.core()] + [self.to(d) for d in range(1, self.nz)]
        for peer in peers:
            pl.semaphore_signal(barrier, inc=1, device_id=peer, device_id_type=MESH)
        pl.semaphore_wait(barrier, len(peers))


def remote(src, dst, send, recv, device):
    return pltpu.make_async_remote_copy(
        src_ref=src, dst_ref=dst, send_sem=send, recv_sem=recv, device_id=device, device_id_type=MESH
    )


class Gather:
    def __init__(
        self, nz, layers, qkv_ref, out_ref, up_ref, down_ref, small_ref, full_ref, tiny_ref,
        mine, local_sem, keep_sem, zds, zdr, zs, zr, xs, xr, ys, yr, fxs, fxr, fys, fyr, cs, cr, ts, tr,
    ):
        self.__dict__.update(locals())
        self.at = Place(nz)
        self.shard, self.width = out_ref.shape[1], out_ref.shape[2]
        self.half, self.wide = self.shard // 2, self.width // 2
        self.units = layers * UNITS
        self.hops = nz - 1
        self.iterations = self.units + LAG * self.hops + PASS + TURN

    def source(self, way, k):
        return self.at.z - way * k

    def comes(self, way, k):
        z = self.at.z
        return z >= k if way > 0 else z + k < self.nz

    def goes(self, way):
        z = self.at.z
        return z + 1 < self.nz if way > 0 else z >= 1

    def next(self, way):
        at = self.at
        return (at.r, 2 * (at.z + way) + at.c, at.s)

    def slot(self, way, k):
        return 2 * (k - 1) + (0 if way > 0 else 1)

    def block(self, u, z, c, r, s):
        row = pl.multiple_of((2 * z + c) * self.shard + r * self.half, 8)
        col = pl.multiple_of(s * self.wide, 128)
        return self.full_ref.at[u, pl.ds(row, self.half), pl.ds(col, self.wide)]

    def quarter(self, u, z, c, r, s, part):
        top = self.half * TOP // 80 // 8 * 8
        row = pl.multiple_of((2 * z + c) * self.shard + r * self.half + part * top, 8)
        col = pl.multiple_of(s * self.wide, 128)
        size = self.half - top if part else top
        return self.full_ref.at[u, pl.ds(row, size), pl.ds(col, self.wide)]

    def own(self, u, c):
        row = pl.multiple_of((2 * self.at.z + c) * self.shard, 8)
        return self.full_ref.at[u, pl.ds(row, self.shard), :]

    def local(self, layer, k):
        if k < 3:
            piece = self.qkv_ref.at[layer, :, pl.ds(k * self.width, self.width)]
        else:
            piece = (self.out_ref, self.up_ref, self.down_ref)[k - 3].at[layer]
        u = layer * UNITS + k
        return pltpu.make_async_copy(piece, self.mine.at[u], self.local_sem.at[u])

    def keep(self, u):
        return pltpu.make_async_copy(self.mine.at[u], self.own(u, self.at.c), self.keep_sem.at[u])

    def z_copy(self, u, way, k):
        at, n = self.at, self.slot(way, k)
        piece = self.block(u, self.source(way, k - 1), at.c, at.r, at.s)
        held = piece
        if k == 1:
            row = pl.multiple_of(at.r * self.half, 16)
            held = self.mine.at[u, pl.ds(row, self.half), pl.ds(pl.multiple_of(at.s * self.wide, 128), self.wide)]
        return remote(held, piece, self.zs.at[u, n], self.zr.at[u, n], self.next(way))

    def z_diag(self, u, way):
        at, n = self.at, 0 if way > 0 else 1
        piece = self.block(u, at.z, at.c, 1 - at.r, 1 - at.s)
        row = pl.multiple_of((1 - at.r) * self.half, 16)
        col = pl.multiple_of((1 - at.s) * self.wide, 128)
        held = self.mine.at[u, pl.ds(row, self.half), pl.ds(col, self.wide)]
        return remote(held, piece, self.zds.at[u, n], self.zdr.at[u, n], self.next(way))

    def z_came(self, u, way, k):
        at, n = self.at, self.slot(way, k)
        piece = self.block(u, self.source(way, k), at.c, at.r, at.s)
        return remote(piece, piece, self.zs.at[u, n], self.zr.at[u, n], self.next(way))

    def x_copy(self, u, way, k):
        at, n = self.at, self.slot(way, k)
        piece = self.block(u, self.source(way, k), at.c, at.r, at.s)
        return remote(piece, piece, self.xs.at[u, n], self.xr.at[u, n], at.x())

    def y_copy(self, u, way, k):
        at, n = self.at, self.slot(way, k)
        piece = self.block(u, self.source(way, k), at.c, at.r, at.s)
        return remote(piece, piece, self.ys.at[u, n], self.yr.at[u, n], at.y())

    def fx_copy(self, u, way, k):
        at, n = self.at, self.slot(way, k)
        piece = self.quarter(u, self.source(way, k), at.c, 1 - at.r, at.s, 1)
        return remote(piece, piece, self.fxs.at[u, n], self.fxr.at[u, n], at.x())

    def fy_copy(self, u, way, k):
        at, n = self.at, self.slot(way, k)
        piece = self.quarter(u, self.source(way, k), at.c, at.r, 1 - at.s, 0)
        return remote(piece, piece, self.fys.at[u, n], self.fyr.at[u, n], at.y())

    def core_own(self, u):
        own, n = self.own(u, self.at.c), 8 * self.hops
        return remote(self.mine.at[u], own, self.cs.at[u, n], self.cr.at[u, n], self.at.core())

    def core_copy(self, u, way, k, which):
        at = self.at
        r = at.r if which in (0, 1) else 1 - at.r
        s = at.s if which in (0, 2) else 1 - at.s
        piece = self.block(u, self.source(way, k), at.c, r, s)
        n = 4 * self.slot(way, k) + which
        return remote(piece, piece, self.cs.at[u, n], self.cr.at[u, n], at.core())

    def tiny(self, d):
        piece = self.tiny_ref.at[self.at.f]
        return remote(piece, piece, self.ts.at[d - 1], self.tr.at[d - 1], self.at.to(d))

    def tiny_core(self, d):
        piece, n = self.tiny_ref.at[2 * self.at.source(d) + self.at.c], self.nz - 1 + d
        return remote(piece, piece, self.ts.at[n], self.tr.at[n], self.at.core())

    def begin(self):
        self.tiny_ref[self.at.f] = self.small_ref[...].astype(jnp.bfloat16)
        for layer in range(self.layers):
            for k in range(UNITS):
                self.local(layer, k).start()
        self.at.greet()
        for d in range(1, self.nz):
            self.tiny(d).start()
        self.tiny_core(0).start()

    def tiny_pass(self):
        for d in range(1, self.nz):
            self.tiny(d).wait_recv()
            self.tiny_core(d).start()

    def tiny_ready(self):
        for d in range(self.nz):
            self.tiny_core(d).wait_recv()

    def tiny_done(self):
        for d in range(1, self.nz):
            self.tiny(d).wait_send()
        for d in range(self.nz):
            self.tiny_core(d).wait_send()

    def when(self, cond, work):
        pl.when(cond)(work)

    def first(self, u):
        pltpu.make_async_copy(self.out_ref.at[0], self.mine.at[u], self.local_sem.at[u]).wait()
        self.keep(u).start()
        for way in (1, -1):
            def work(way=way):
                self.z_copy(u, way, 1).start()
                self.z_diag(u, way).start()
            self.when(self.goes(way), work)
        self.core_own(u).start()

    def hop(self, u, k):
        for way in (1, -1):
            def work(way=way):
                self.z_came(u, way, k).wait_recv()
                if k < self.hops:
                    self.when(self.goes(way), lambda: self.z_copy(u, way, k + 1).start())
                self.x_copy(u, way, k).start()
                self.y_copy(u, way, k).start()
                self.core_copy(u, way, k, 0).start()
                if k == 1:
                    self.z_diag(u, way).wait_recv()
                    self.core_copy(u, way, k, 3).start()
            self.when(self.comes(way, k), work)

    def forward(self, u, k):
        for way in (1, -1):
            def work(way=way):
                self.x_copy(u, way, k).wait_recv()
                if k > 1:
                    self.fy_copy(u, way, k).start()
                self.core_copy(u, way, k, 1).start()
                self.y_copy(u, way, k).wait_recv()
                if k > 1:
                    self.fx_copy(u, way, k).start()
                self.core_copy(u, way, k, 2).start()
            self.when(self.comes(way, k), work)

    def diagonal(self, u, k):
        for way in (1, -1):
            def work(way=way):
                self.fx_copy(u, way, k).wait_recv()
                self.fy_copy(u, way, k).wait_recv()
                self.core_copy(u, way, k, 3).start()
            self.when(self.comes(way, k), work)

    def step(self, i):
        def stage(lag, work):
            u = i - lag
            self.when((u >= 0) & (u < self.units), lambda: work(u))

        stage(0, self.first)
        for k in range(1, self.hops + 1):
            stage(LAG * k, lambda u, k=k: self.hop(u, k))
        for k in range(1, self.hops + 1):
            stage(LAG * k + PASS, lambda u, k=k: self.forward(u, k))
        for k in range(2, self.hops + 1):
            stage(LAG * k + PASS + TURN, lambda u, k=k: self.diagonal(u, k))

    def ready(self, u):
        self.keep(u).wait()
        self.core_own(u).wait_recv()
        for k in range(1, self.hops + 1):
            for way in (1, -1):
                def work(way=way, k=k):
                    for which in range(4):
                        self.core_copy(u, way, k, which).wait_recv()
                self.when(self.comes(way, k), work)

    def drain(self, u):
        self.core_own(u).wait_send()
        for k in range(1, self.hops + 1):
            for way in (1, -1):
                def sent(way=way, k=k):
                    self.z_copy(u, way, k).wait_send()
                    if k == 1:
                        self.z_diag(u, way).wait_send()
                came = self.goes(way)
                if k > 1:
                    came = came & self.comes(way, k - 1)
                self.when(came, sent)

                def work(way=way, k=k):
                    copies = (self.x_copy, self.y_copy, self.fx_copy, self.fy_copy)
                    for copy in copies if k > 1 else copies[:2]:
                        copy(u, way, k).wait_send()
                    for which in range(4):
                        self.core_copy(u, way, k, which).wait_send()
                self.when(self.comes(way, k), work)

    def finish(self):
        @pl.loop(0, self.units)
        def _(u):
            self.drain(u)

        self.tiny_done()


def gather_scratch(nz, layers, shard, width):
    units, n = layers * UNITS, 2 * (nz - 1)
    dma = pltpu.SemaphoreType.DMA
    return (
        [pltpu.VMEM((units, shard, width), jnp.bfloat16), dma((units,)), dma((units,))]
        + [dma((units, 2))] * 2
        + [dma((units, n))] * 10
        + [dma((units, 1 + 4 * n))] * 2
        + [dma((2 * nz,))] * 2
    )


def dot_nn(a, b):
    return jnp.dot(a, b, preferred_element_type=jnp.float32)


def dot_nt(a, b):
    return lax.dot_general(a, b, (((1,), (1,)), ((), ())), preferred_element_type=jnp.float32)


def dot_tn(a, b):
    return lax.dot_general(a, b, (((0,), (0,)), ((), ())), preferred_element_type=jnp.float32)


ROWS = 128
TALL = 256
BEGIN = 3
SOON = 5


def each_tile(count, body, rows=ROWS):
    @pl.loop(0, count // rows)
    def _(i):
        body(pl.ds(pl.multiple_of(i * rows, rows), rows))


def head_rows(h):
    return pl.ds(pl.multiple_of(h * HEAD, 16), HEAD)


def row_norm(values, gain):
    inverse = lax.rsqrt(jnp.mean(values * values, axis=-1, keepdims=True) + EPSILON)
    return (values * inverse * gain).astype(jnp.bfloat16)


def expand_small(tiny_ref, vec_ref, layers, shard, part):
    width = vec_ref.shape[1]
    count = tiny_ref.shape[0]
    rows, lanes = tiny_ref.shape[1:]
    line = lax.broadcasted_iota(jnp.int32, (lanes, width), 0)
    column = lax.broadcasted_iota(jnp.int32, (lanes, width), 1)
    inner = lax.rem(column, HEAD)

    def place(f, sums):
        plain, scale = sums
        piece = tiny_ref[f]
        hot = jnp.where((column - f * shard == line) & (line < shard), 1.0, 0.0).astype(jnp.bfloat16)
        spread = jnp.where((inner - f * part == line) & (line < part), 1.0, 0.0).astype(jnp.bfloat16)
        return plain + dot_nn(piece, hot), scale + dot_nn(piece, spread)

    zero = jnp.zeros((rows, width), jnp.float32)
    plain, scale = lax.fori_loop(0, count, place, (zero, zero))
    soft = jnp.maximum(scale, 0.0) + jnp.log(1.0 + jnp.exp(-jnp.abs(scale)))
    row = lax.broadcasted_iota(jnp.int32, (rows, width), 0)
    vec_ref[...] = jnp.where(row < 4 * layers, plain, soft * (SOFT_ONE / math.sqrt(HEAD)))


def attend(heads, q_ref, k_ref, v_ref, bias_ref, out_ref, lse_ref):
    queries = q_ref.shape[1]

    @pl.loop(*heads)
    def _(h):
        rows = head_rows(h)
        scores = dot_tn(k_ref[rows, :], q_ref[rows, :]) + bias_ref[:, :queries]
        top = jnp.max(scores, axis=0, keepdims=True)
        grown = jnp.exp(scores - top)
        total = jnp.sum(grown, axis=0, keepdims=True)
        out = dot_nn(v_ref[rows, :], grown.astype(jnp.bfloat16)) * (1.0 / total)
        out_ref[rows, :] = out.astype(jnp.bfloat16)
        lse_ref[h] = top + jnp.log(total)


def forward_kernel(nz, layers, part, *refs):
    series_ref, qkv_ref, out_ref, up_ref, down_ref = refs[:5]
    gains_ref, up_bias_ref, down_bias_ref, scale_ref, pad_ref, starts_ref, count_ref = refs[5:12]
    full_ref, vec_out, series_out, bias_out = refs[12:16]
    per = 11
    saved = [refs[16 + per * l : 16 + per * (l + 1)] for l in range(layers)]
    refs = refs[16 + per * layers :]
    names = ("current", "normed_t", "q", "k", "v", "lse", "att", "after", "mixed", "pre", "hidden")
    held = [dict(zip(names, refs[per * l : per * (l + 1)])) for l in range(layers)]
    refs = refs[per * layers :]
    normed, weights, vec, last, tiny_ref, small_ref, bias_ref, swap_sem, load_sem, save_sem = refs[:10]
    gather = Gather(
        nz, layers, qkv_ref, out_ref, up_ref, down_ref, small_ref, full_ref, tiny_ref, *refs[10:]
    )
    at = gather.at
    length = series_ref.shape[0]
    total = held[0]["normed_t"].shape[1]
    other = total - length

    own_copy = pltpu.make_async_copy(series_ref, held[0]["current"].at[pl.ds(0, length)], swap_sem.at[0])
    swap_copy = remote(
        series_ref, held[0]["current"].at[pl.ds(length, other)], swap_sem.at[1], swap_sem.at[2], at.x()
    )

    def save(l, n):
        return pltpu.make_async_copy(held[l][names[n]], saved[l][n], save_sem.at[l, n])

    def fetch(u):
        return pltpu.make_async_copy(full_ref.at[u], weights.at[u % 2], load_sem.at[u % 2])

    def arrived(u):
        fetch(u).wait()
        return weights.at[u % 2]

    def vector(n):
        return vec[n : n + 1, :]

    def normalize(l):
        b = held[l]
        gain = vector(2 * l)

        def body(r):
            values = row_norm(b["current"][r, :].astype(jnp.float32), gain)
            normed[r, :] = values
            b["normed_t"][:, r] = values.T
        each_tile(total, body)
        save(l, 1).start()

    def project(l, n):
        b = held[l]
        target = b[("q", "k", "v")[n]]
        weight = arrived(l * UNITS + n)

        def body(r):
            values = dot_nn(normed[r, :], weight[...])
            if n == 0:
                values = values * vector(4 * layers + l)
            target[:, r] = values.astype(jnp.bfloat16).T
        each_tile(target.shape[1], body)
        save(l, 2 + n).start()

    def attention(l, first):
        b = held[l]
        heads = (0, HEADS // 2) if first else (HEADS // 2, HEADS)
        attend(heads, b["q"], b["k"], b["v"], bias_ref, b["att"], b["lse"])
        if not first:
            save(l, 5).start()
            save(l, 6).start()

    def output(l):
        b = held[l]
        weight = arrived(l * UNITS + 3)
        gain = vector(2 * l + 1)

        def body(r):
            after = b["current"][r, :].astype(jnp.float32) + dot_tn(b["att"][:, r], weight[...])
            b["after"][r, :] = after
            b["mixed"][r, :] = row_norm(after, gain)
        each_tile(b["after"].shape[0], body)
        save(l, 7).start()
        save(l, 8).start()

    def expand(l):
        b = held[l]
        weight = arrived(l * UNITS + 4)
        bias = vector(2 * layers + l)

        def body(r):
            pre = dot_nn(b["mixed"][r, :], weight[...]) + bias
            b["pre"][r, :] = pre
            b["hidden"][r, :] = (pre * (1.0 / (1.0 + jnp.exp(-pre)))).astype(jnp.bfloat16)
        each_tile(b["pre"].shape[0], body)
        save(l, 9).start()
        save(l, 10).start()

    def contract(l):
        b = held[l]
        weight = arrived(l * UNITS + 5)
        bias = vector(3 * layers + l)

        def body(r):
            values = b["after"][r, :] + (dot_nn(b["hidden"][r, :], weight[...]) + bias)
            if l + 1 < layers:
                held[l + 1]["current"][r, :] = values
            else:
                last[r, :] = values.astype(jnp.bfloat16)
        each_tile(b["after"].shape[0], body)
        if l + 1 < layers:
            save(l + 1, 0).start()
            normalize(l + 1)
        else:
            pltpu.make_async_copy(last, series_out, swap_sem.at[3]).start()

    tasks = {}

    def add(i, work):
        tasks.setdefault(i, []).append(work)

    lag = gather.iterations - layers * UNITS

    def early():
        gather.tiny_pass()
        gather.tiny_ready()
        expand_small(tiny_ref, vec, layers, gather.shard, part)
        pltpu.make_async_copy(vec, vec_out, swap_sem.at[4]).start()
        fill_bias(bias_ref, length, pad_ref, starts_ref, count_ref)
        pltpu.make_async_copy(bias_ref, bias_out, swap_sem.at[5]).start()

    def begin():
        own_copy.wait()
        swap_copy.wait_recv()
        save(0, 0).start()
        normalize(0)

    def pull(u):
        gather.ready(u)
        fetch(u).start()

    add(1, early)
    add(BEGIN, begin)
    units = layers * UNITS
    computing = []
    for l in range(layers):
        computing += [[lambda l=l, n=n: project(l, n)] for n in range(3)]
        computing[-1].append(lambda l=l: attention(l, True))
        computing.append([lambda l=l: attention(l, False), lambda l=l: output(l)])
        computing.append([lambda l=l: expand(l)])
        computing.append([lambda l=l: contract(l)])
    for u in range(units):
        add(u + lag, lambda u=u: pull(u))
        late = u >= units - SOON
        for one in computing[u]:
            add(u + lag + (0 if late else 1), one)

    own_copy.start()
    small_ref[...] = jnp.zeros_like(small_ref)
    shard = gather.shard
    for l in range(layers):
        for n in range(2):
            small_ref[2 * l + n : 2 * l + n + 1, :shard] = gains_ref[l, n : n + 1, :].astype(jnp.float32)
    groups = ((2 * layers, up_bias_ref, shard), (3 * layers, down_bias_ref, shard), (4 * layers, scale_ref, part))
    for base, ref, size in groups:
        small_ref[base : base + layers, :size] = ref[...].astype(jnp.float32)
    gather.begin()
    swap_copy.start()

    @pl.loop(0, gather.iterations)
    def _(i):
        gather.step(i)
        for when, work in sorted(tasks.items()):
            @pl.when(i == when)
            def _(work=work):
                for one in work:
                    one()

    swap_copy.wait_send()
    pltpu.make_async_copy(last, series_out, swap_sem.at[3]).wait()
    pltpu.make_async_copy(vec, vec_out, swap_sem.at[4]).wait()
    pltpu.make_async_copy(bias_ref, bias_out, swap_sem.at[5]).wait()
    for l in range(layers):
        for n in range(per):
            save(l, n).wait()
    gather.finish()


def saved_shapes(layers, length, total, width):
    low, wide = jnp.bfloat16, jnp.float32
    shapes = []
    for l in range(layers):
        count = length if l == layers - 1 else total
        kind = low if l == 0 else wide
        shapes.append(
            [
                ((total, width), kind),
                ((width, total), low),
                ((width, count), low),
                ((width, total), low),
                ((width, total), low),
                ((HEADS, 1, count), wide),
                ((width, count), low),
                ((count, width), wide),
                ((count, width), low),
                ((count, width), wide),
                ((count, width), low),
            ]
        )
    return shapes


def forward_pass(nz, series, matrices, vectors, spans):
    layers, shard, width = matrices[1].shape
    length, part = series.shape[0], vectors[3].shape[1]
    total = 2 * length
    units = layers * UNITS
    low, wide = jnp.bfloat16, jnp.float32
    shapes = [one for group in saved_shapes(layers, length, total, width) for one in group]
    small = (5 * layers + -5 * layers % 16, shard + -shard % 128)
    dma = pltpu.SemaphoreType.DMA
    anywhere = pl.BlockSpec(memory_space=pl.ANY)
    inside = pl.BlockSpec(memory_space=pltpu.VMEM)
    scalars = pl.BlockSpec(memory_space=pltpu.SMEM)
    count = 2 * nz
    results = pl.pallas_call(
        functools.partial(forward_kernel, nz, layers, part),
        out_shape=(
            jax.ShapeDtypeStruct((units, count * shard, width), low),
            jax.ShapeDtypeStruct((small[0], width), wide),
            jax.ShapeDtypeStruct((length, width), low),
            jax.ShapeDtypeStruct((total, total), wide),
        )
        + tuple(jax.ShapeDtypeStruct(*one) for one in shapes),
        in_specs=[anywhere] * 5 + [inside] * 4 + [scalars] * 3,
        out_specs=(anywhere,) * (4 + len(shapes)),
        scratch_shapes=[pltpu.VMEM(*one) for one in shapes]
        + [
            pltpu.VMEM((total, width), low),
            pltpu.VMEM((2, width, width), low),
            pltpu.VMEM((small[0], width), wide),
            pltpu.VMEM((length, width), low),
            pltpu.VMEM((count,) + small, low),
            pltpu.VMEM(small, wide),
            pltpu.VMEM((total, total), wide),
            dma((6,)),
            dma((2,)),
            dma((layers, 11)),
        ]
        + gather_scratch(nz, layers, shard, width),
        compiler_params=pltpu.CompilerParams(
            collective_id=1, has_side_effects=True, vmem_limit_bytes=60 << 20
        ),
    )(series, *matrices, *vectors, *spans)
    full, vec, out, bias = results[:4]
    saved = [results[4 + 11 * l : 15 + 11 * l] for l in range(layers)]
    return full, vec, out, bias, saved


def fill_bias(bias_ref, length, pad_ref, starts_ref, count_ref):
    s = lax.axis_index("seq")
    total = bias_ref.shape[0]
    pad, count = pad_ref[0], count_ref[0]

    def place(index):
        return jnp.where(index < length, s * length + index, -s * length + index)

    query = place(lax.broadcasted_iota(jnp.int32, (ROWS, total), 1))

    @pl.loop(0, total // ROWS)
    def _(i):
        key = place(lax.broadcasted_iota(jnp.int32, (ROWS, total), 0) + i * ROWS)
        seen = key <= query
        for slot in range(starts_ref.shape[1]):
            start = jnp.where(slot < count, starts_ref[0, slot], -2 * SPAN)
            stop = start + SPAN
            seen = seen | (key >= start) & (key < stop) & (query >= start) & (query < stop)
        allowed = (seen & (key >= pad)) | (key == query)
        rows = pl.ds(pl.multiple_of(i * ROWS, ROWS), ROWS)
        bias_ref[rows, :] = jnp.where(allowed, 0.0, NEG_FILL)


SLOTS = 14
LAGS = (1, 3, 6, 8, 10, 12)


class Reduce:
    def __init__(
        self, nz, units, full_ref, tiny, tiny_out, grads, held, bx, by, near, far, swap, tiny_in,
        as_, ar, bs, br, zs, zr, es, er, ls, ps, pr, ts, tr, free,
    ):
        self.__dict__.update(locals())
        self.at = Place(nz)
        self.slots, _, self.half, self.width = held.shape
        self.shard = 2 * self.half
        self.wide, self.low = self.width // 2, nz // 2
        self.steps = range(1, nz)
        self.parts = 2 * units
        self.iterations = self.parts + LAGS[-1]
        self.side = self.column(self.at.z)

    def column(self, z):
        return jnp.where(z < self.low, self.at.s, self.at.r)

    def cols(self, side):
        return pl.ds(pl.multiple_of(side * self.wide, 128), self.wide)

    def slot(self, h):
        return lax.rem(h, self.slots)

    def band(self, h):
        return pl.ds(pl.multiple_of(lax.rem(h, 2) * self.half, 16), self.half)

    def z_peer(self, d):
        at = self.at
        z = lax.rem(at.z + d, self.nz) if 2 * d == self.nz else at.z + 1 - 2 * lax.rem(at.z, 2)
        return z, (at.r, 2 * z + at.c, at.s)

    def pair_peer(self):
        at, first = self.at, self.at.z < self.low
        return (jnp.where(first, 1 - at.r, at.r), at.f, jnp.where(first, at.s, 1 - at.s))

    def last_peer(self):
        at, first = self.at, self.at.z < self.low
        return (jnp.where(first, at.r, 1 - at.r), at.f, jnp.where(first, 1 - at.s, at.s))

    def a_copy(self, h):
        piece = self.grads.at[:, 1 - self.at.c, self.band(h), :]
        return remote(piece, self.held.at[self.slot(h)], self.as_.at[h], self.ar.at[h], self.at.core())

    def bx_copy(self, h):
        piece = self.held.at[self.slot(h), pl.ds(0, self.low), :, self.cols(1 - self.at.s)]
        return remote(piece, self.bx.at[h], self.bs.at[h, 0], self.br.at[h, 0], self.at.x())

    def by_copy(self, h):
        piece = self.held.at[self.slot(h), pl.ds(self.low, self.low), :, self.cols(1 - self.at.r)]
        return remote(piece, self.by.at[h], self.bs.at[h, 1], self.br.at[h, 1], self.at.y())

    def near_copy(self, h, n):
        target = n * 2 + 1 - lax.rem(self.at.z, 2)
        side = (self.at.s, self.at.r)[n]
        piece = self.held.at[self.slot(h), target, :, self.cols(side)]
        return remote(piece, self.near.at[h, n], self.zs.at[h, n], self.zr.at[h, n], self.z_peer(1)[1])

    def far_copy(self, h):
        z, peer = self.z_peer(2)
        piece = self.held.at[self.slot(h), z, :, self.cols(self.column(z))]
        return remote(piece, self.far.at[h], self.zs.at[h, 2], self.zr.at[h, 2], peer)

    def pair_copy(self, h):
        piece = self.held.at[self.slot(h), self.at.z, :, self.cols(self.side)]
        return remote(piece, self.swap.at[h], self.es.at[h], self.er.at[h], self.pair_peer())

    def spot(self, h):
        return self.full_ref.at[lax.div(h, 2), self.band(h), self.cols(self.side)]

    def put_copy(self, h):
        return pltpu.make_async_copy(self.bx.at[h, 0], self.spot(h), self.ls.at[h])

    def last_copy(self, h):
        return remote(self.bx.at[h, 0], self.spot(h), self.ps.at[h], self.pr.at[h], self.last_peer())

    def plus(self, *values):
        return sum(v.astype(jnp.float32) for v in values).astype(jnp.bfloat16)

    def a_start(self, h):
        @pl.when(h >= self.slots)
        def _():
            pl.semaphore_wait(self.free, 1)
        self.a_copy(h).start()

    def a_stage(self, h):
        held, slot, c = self.held, self.slot(h), self.at.c
        self.a_copy(h).wait_recv()

        @pl.loop(0, self.nz)
        def _(z):
            held[slot, z] = self.plus(held[slot, z], self.grads[z, c, self.band(h), :])
        self.bx_copy(h).start()
        self.by_copy(h).start()
        self.a_copy(h).wait_send()

    def b_stage(self, h):
        held, slot, at = self.held, self.slot(h), self.at
        for copy, came, base, side in (
            (self.bx_copy(h), self.bx, 0, at.s),
            (self.by_copy(h), self.by, self.low, at.r),
        ):
            copy.wait()

            @pl.loop(0, self.low)
            def _(z, came=came, base=base, side=side):
                mine = self.cols(side)
                held[slot, base + z, :, mine] = self.plus(held[slot, base + z, :, mine], came[h, z])
        for n in range(2):
            self.near_copy(h, n).start()

    def near_stage(self, h):
        held, slot, at = self.held, self.slot(h), self.at
        for n in range(2):
            self.near_copy(h, n).wait()
            target, mine = 2 * n + lax.rem(at.z, 2), self.cols((at.s, at.r)[n])
            held[slot, target, :, mine] = self.plus(held[slot, target, :, mine], self.near[h, n])
        self.far_copy(h).start()

    def far_stage(self, h):
        held, slot, z, mine = self.held, self.slot(h), self.at.z, self.cols(self.side)
        self.far_copy(h).wait()
        held[slot, z, :, mine] = self.plus(held[slot, z, :, mine], self.far[h])
        self.pair_copy(h).start()

    def pair_stage(self, h):
        held, slot, z, mine = self.held, self.slot(h), self.at.z, self.cols(self.side)
        self.pair_copy(h).wait()
        self.bx[h, 0] = self.plus(held[slot, z, :, mine], self.swap[h])

        @pl.when(h + self.slots < self.parts)
        def _():
            pl.semaphore_signal(self.free, inc=1, device_id=self.at.core(), device_id_type=MESH)
        self.put_copy(h).start()
        self.last_copy(h).start()

    def close(self, h):
        self.put_copy(h).wait()
        self.last_copy(h).wait()

    def step(self, i):
        def stage(lag, work):
            h = i - lag
            pl.when((h >= 0) & (h < self.parts))(lambda: work(h))

        works = (self.a_stage, self.b_stage, self.near_stage, self.far_stage, self.pair_stage, self.close)
        for lag, work in zip(LAGS, works):
            stage(lag, work)

    def launch(self, i):
        @pl.when((lax.rem(i, 2) == 0) & (i < self.parts))
        def _():
            self.a_start(i)
            self.a_start(i + 1)

    def tiny_copy(self, n, peer):
        return remote(self.tiny, self.tiny_in.at[n], self.ts.at[n], self.tr.at[n], peer)

    def tiny_z(self, d):
        return remote(self.tiny, self.tiny_in.at[2 + d], self.ts.at[2 + d], self.tr.at[2 + d], self.at.to(d))

    def tiny_step(self, n):
        peers = (self.at.core(), self.at.x(), self.at.y())
        if 0 < n <= 3:
            copy = self.tiny_copy(n - 1, peers[n - 1])
            copy.wait()
            self.tiny[...] = self.tiny[...] + self.tiny_in[n - 1]
        if n < 3:
            self.tiny_copy(n, peers[n]).start()
        if n == 3:
            for d in self.steps:
                self.tiny_z(d).start()
        if n == 4:
            for d in self.steps:
                self.tiny_z(d).wait()
            self.tiny_out[...] = self.tiny[...] + sum(self.tiny_in[2 + d] for d in self.steps)


def backward_kernel(nz, layers, length, total, *refs):
    cot_ref, full_ref, vec, bias_ref = refs[:4]
    per = 11
    saved = [refs[4 + per * l : 4 + per * (l + 1)] for l in range(layers)]
    refs = refs[4 + per * layers :]
    share_ref, tiny_out, input_ref = refs[:3]
    (
        up, wide_a, wide_b, hidden, mixed, pre_low, low, trio, att, do, lse, weight, came, sent,
        load_sem, weight_sem, x_sem, tiny, grads,
    ) = refs[3:22]
    units = layers * UNITS
    k, v, q = trio.at[0], trio.at[1], trio.at[2]
    reduce = Reduce(nz, units, share_ref, tiny, tiny_out, grads, *refs[22:])
    at = reduce.at
    width = up.shape[1]
    wide, half_z = width // 2, nz // 2
    shard = reduce.shard
    names = ("current", "normed_t", "q", "k", "v", "lse", "att", "after", "mixed", "pre", "hidden")
    homes = dict(
        normed_t=att, q=q, k=k, v=v, lse=lse, att=att, after=wide_b, mixed=mixed, pre=wide_a, hidden=hidden
    )

    def load(l, name):
        n = names.index(name)
        source = saved[l][n]
        home = homes.get(name, hidden if source.dtype == jnp.bfloat16 else wide_b)
        if home.shape != source.shape:
            if len(source.shape) == 3:
                home = home.at[:, :, pl.ds(0, source.shape[2])]
            elif source.shape[0] != home.shape[0]:
                home = home.at[pl.ds(0, source.shape[0]), :]
            else:
                home = home.at[:, pl.ds(0, source.shape[1])]
        return pltpu.make_async_copy(source, home, load_sem.at[l, n])

    def fetch(u):
        return pltpu.make_async_copy(full_ref.at[u], weight, weight_sem.at[0])

    def fill(product):
        @pl.loop(0, 2)
        def _(i):
            @pl.loop(0, 2)
            def _(j):
                r = pl.ds(pl.multiple_of(i * wide, 128), wide)
                c = pl.ds(pl.multiple_of(j * wide, 128), wide)
                value = product(r, c).astype(jnp.bfloat16).reshape(half_z, 2, shard, wide)
                grads[pl.ds(i * half_z, half_z), :, :, c] = value

    def vector(n):
        return vec[n : n + 1, :]

    def gather_row(n, values):
        tiny[n : n + 1, :] = tiny[n : n + 1, :] + jnp.sum(values, axis=0, keepdims=True)

    def norm_tile(values, gain, w, n):
        inverse = lax.rsqrt(jnp.mean(values * values, axis=-1, keepdims=True) + EPSILON)
        scaled = w * gain
        inner = jnp.mean(values * scaled, axis=-1, keepdims=True)
        gather_row(n, w * values * inverse)
        return inverse * scaled - values * (inverse * inverse * inverse) * inner

    def count(l):
        return length if l == layers - 1 else total

    def next_load(l, *which):
        if l > 0:
            for name in which:
                load(l - 1, name).start()

    def down(l):
        m = count(l)
        load(l, "hidden").wait()

        def body(r):
            value = up[r, :].astype(jnp.bfloat16)
            low[r, :] = value
            gather_row(3 * layers + l, value.astype(jnp.float32))
        each_tile(m, body)
        fill(lambda r, c: dot_tn(hidden[:m, r], low[:m, c]))
        if saved[l][0].dtype == jnp.bfloat16:
            load(l, "current").start()
        else:
            next_load(l, "hidden")

    def expand(l):
        fetch(l * UNITS + 5).wait()
        load(l, "pre").wait()

        def body(r):
            grown = dot_nt(low[r, :], weight[...])
            value = wide_a[r, :]
            gate = 1.0 / (1.0 + jnp.exp(-value))
            result = (grown * gate * (1.0 + value * (1.0 - gate))).astype(jnp.bfloat16)
            pre_low[r, :] = result
            gather_row(2 * layers + l, result.astype(jnp.float32))
        each_tile(count(l), body, TALL)
        fetch(l * UNITS + 4).start()

    def fill_up(l):
        m = count(l)
        load(l, "mixed").wait()
        fill(lambda r, c: dot_tn(mixed[:m, r], pre_low[:m, c]))
        next_load(l, "mixed")

    def output(l):
        fetch(l * UNITS + 4).wait()
        load(l, "after").wait()
        gain = vector(2 * l + 1)

        def body(r):
            w = dot_nt(pre_low[r, :], weight[...])
            value = up[r, :] + norm_tile(wide_b[r, :], gain, w, 2 * l + 1)
            up[r, :] = value
            low[r, :] = value.astype(jnp.bfloat16)
        each_tile(count(l), body, TALL)
        fetch(l * UNITS + 3).start()
        if saved[l][0].dtype != jnp.bfloat16:
            load(l, "current").start()

    def fill_out(l):
        m = count(l)
        load(l, "att").wait()
        fill(lambda r, c: dot_nn(att[r, :m], low[:m, c]))
        load(l, "normed_t").start()

    def attention(l, start, stop):
        m = count(l)
        row = 4 * layers + l
        factor = jnp.broadcast_to(vec[row : row + 1, 0:128], (128, 128)).T[0:HEAD, 0:1]

        def head(h, sums):
            rows = head_rows(h)
            kh, vh, qh, oh = k[rows, :], v[rows, :], q[rows, :m], do[rows, :m]
            scores = dot_tn(kh, qh) + bias_ref[:, :m]
            probs = jnp.exp(scores - lse[h, :, :m])
            weighted = probs * dot_tn(vh, oh)
            inner = jnp.sum(weighted, axis=0, keepdims=True)
            score = (weighted - probs * inner).astype(jnp.bfloat16)
            v[rows, :] = dot_nt(oh, probs.astype(jnp.bfloat16)).astype(jnp.bfloat16)
            k[rows, :] = dot_nt(qh, score).astype(jnp.bfloat16)
            query = dot_nn(kh, score)
            q[rows, :m] = (query * factor).astype(jnp.bfloat16)
            return sums + jnp.sum(query * qh.astype(jnp.float32), axis=1, keepdims=True)

        sums = lax.fori_loop(start, stop, head, jnp.zeros((HEAD, 1), jnp.float32))
        flat = jnp.broadcast_to(sums, (HEAD, 128)).T
        tiny[row : row + 1, 0:HEAD] = tiny[row : row + 1, 0:HEAD] + flat[0:1, :]

    def open_heads(l):
        m = count(l)
        fetch(l * UNITS + 3).wait()

        def body(r):
            do[r, :m] = dot_nt(weight[r, :], low[:m, :]).astype(jnp.bfloat16)
        each_tile(width, body, wide)
        fetch(l * UNITS + 1).start()
        for name in ("q", "k", "v", "lse"):
            load(l, name).wait()

    def turn(l):
        next_load(l, "lse")
        load(l, "normed_t").wait()

    def fill_project(n):
        fill(lambda r, c: dot_nt(att[r, :], trio[n, c, :]))

    def project(l, n):
        fetch(l * UNITS + lax.rem(n + 1, 3)).wait()
        count = jnp.where((n == 2) & (l == layers - 1), length, total)

        @pl.loop(0, lax.div(count, TALL))
        def _(i):
            r = pl.ds(pl.multiple_of(i * TALL, TALL), TALL)
            value = dot_nt(trio[n, :, r].T, weight[...])
            wide_a[r, :] = value + jnp.where(n > 0, wide_a[r, :], 0.0)

    def settle(l, n):
        if n < 2:
            fetch(l * UNITS + (2, 0)[n]).start()
            return
        if l > 0:
            fetch((l - 1) * UNITS + 5).start()
        load(l, "current").wait()
        gain = vector(2 * l)
        current = hidden if saved[l][0].dtype == jnp.bfloat16 else wide_b

        def close(r):
            return norm_tile(current[r, :].astype(jnp.float32), gain, wide_a[r, :], 2 * l)

        own = count(l)

        def first(r):
            up[r, :] = up[r, :] + close(r)
        each_tile(own, first)
        if own < total:
            @pl.loop(own // ROWS, total // ROWS)
            def _(i):
                r = pl.ds(pl.multiple_of(i * ROWS, ROWS), ROWS)
                up[r, :] = close(r)
        next_load(l, "pre", "after", "att", "q", "k", "v")
        if l == 0:
            sent[...] = up[length:, :].astype(jnp.bfloat16)

    reply = remote(sent, came, x_sem.at[0], x_sem.at[1], at.x())
    def start_layer(l):
        down(l)
        expand(l)

    def middle(l):
        open_heads(l)
        fill_up(l)

    before = {0: start_layer, 1: output, 2: middle, 4: fill_out}
    heads = (0, 0, 0, 1, 6, 9, 14, HEADS)
    after = {6: turn}
    later = {7: lambda l: settle(l, 0), 9: lambda l: settle(l, 1), 11: lambda l: settle(l, 2)}
    last = layers - 1
    start_copy = pltpu.make_async_copy(cot_ref, sent, x_sem.at[2])
    start_copy.start()
    for name in ("hidden", "pre", "mixed", "after", "att", "q", "k", "v", "lse"):
        load(last, name).start()
    fetch(last * UNITS + 5).start()
    tiny[...] = jnp.zeros_like(tiny)
    if count(last) < total:
        trio[2, :, count(last) :] = jnp.zeros((width, total - count(last)), jnp.bfloat16)
    at.greet()
    start_copy.wait()
    up[:length, :] = sent[...].astype(jnp.float32)

    @pl.loop(0, reduce.iterations)
    def _(i):
        reduce.step(i)
        phase, layer = lax.rem(i, 2 * UNITS), last - lax.div(i, 2 * UNITS)
        inside = (i < reduce.parts) & (phase >= UNITS)

        def tasks(some):
            for l in range(layers):
                for n, one in some:
                    @pl.when(i == (last - l) * 2 * UNITS + n)
                    def _(one=one, l=l):
                        one(l)

        tasks(before.items())
        first = sum(jnp.where(phase == n, heads[n], 0) for n in range(2, 7))
        final = sum(jnp.where(phase == n, heads[n + 1], 0) for n in range(2, 7))
        for l in range(layers):
            @pl.when((phase >= 2) & (phase < 7) & (layer == l))
            def _(l=l):
                attention(l, first, final)

        tasks(after.items())

        @pl.when(inside & (lax.rem(phase, 2) == 0))
        def _():
            fill_project(lax.div(phase - UNITS, 2))

        @pl.when(inside & (lax.rem(phase, 2) == 1))
        def _():
            project(layer, lax.div(phase - UNITS, 2))

        tasks(later.items())
        reduce.launch(i)

        @pl.when(i == reduce.parts)
        def _():
            reply.start()

        for n in range(5):
            @pl.when(i == reduce.parts + 1 + 2 * n)
            def _(n=n):
                reduce.tiny_step(n)

    reply.wait()
    input_ref[...] = (up[:length, :] + came[...].astype(jnp.float32)).astype(jnp.bfloat16)


def backward_pass(nz, cotangent, full, vec, bias, saved):
    layers = len(saved)
    units = layers * UNITS
    length, width = cotangent.shape
    total = bias.shape[0]
    shard = width // (2 * nz)
    half, wide, low, n = shard // 2, width // 2, nz // 2, nz - 1
    parts = 2 * units
    slots = min(SLOTS, parts)
    flat = [one for group in saved for one in group]
    rows = vec.shape[0]
    dma = pltpu.SemaphoreType.DMA
    small, large = jnp.bfloat16, jnp.float32
    anywhere = pl.BlockSpec(memory_space=pl.ANY)
    inside = pl.BlockSpec(memory_space=pltpu.VMEM)
    natural, turned = (total, width), (width, total)
    return pl.pallas_call(
        functools.partial(backward_kernel, nz, layers, length, total),
        out_shape=(
            jax.ShapeDtypeStruct((units, shard, width), small),
            jax.ShapeDtypeStruct((rows, width), large),
            jax.ShapeDtypeStruct((length, width), small),
        ),
        in_specs=[anywhere, anywhere, inside, inside] + [anywhere] * len(flat),
        out_specs=(anywhere, inside, inside),
        scratch_shapes=[
            pltpu.VMEM(natural, large),
            pltpu.VMEM(natural, large),
            pltpu.VMEM(natural, large),
            pltpu.VMEM(natural, small),
            pltpu.VMEM(natural, small),
            pltpu.VMEM(natural, small),
            pltpu.VMEM(natural, small),
            pltpu.VMEM((3,) + turned, small),
            pltpu.VMEM(turned, small),
            pltpu.VMEM(turned, small),
            pltpu.VMEM((HEADS, 1, total), large),
            pltpu.VMEM((width, width), small),
            pltpu.VMEM((length, width), small),
            pltpu.VMEM((length, width), small),
            dma((layers, 11)),
            dma((1,)),
            dma((3,)),
            pltpu.VMEM((rows, width), large),
            pltpu.VMEM((nz, 2, shard, width), small),
            pltpu.VMEM((slots, nz, half, width), small),
            pltpu.VMEM((parts, low, half, wide), small),
            pltpu.VMEM((parts, low, half, wide), small),
            pltpu.VMEM((parts, 2, half, wide), small),
            pltpu.VMEM((parts, half, wide), small),
            pltpu.VMEM((parts, half, wide), small),
            pltpu.VMEM((3 + n, rows, width), large),
            dma((parts,)), dma((parts,)),
            dma((parts, 2)), dma((parts, 2)),
            dma((parts, 3)), dma((parts, 3)),
            dma((parts,)), dma((parts,)),
            dma((parts,)),
            dma((parts,)), dma((parts,)),
            dma((3 + n,)), dma((3 + n,)),
            pltpu.SemaphoreType.REGULAR,
        ],
        compiler_params=pltpu.CompilerParams(
            collective_id=2, has_side_effects=True, vmem_limit_bytes=63 << 20
        ),
    )(cotangent, full, vec, bias, *flat)


def forward_layer(current, weights, allowed, series_count, local_length, total_length):
    qkv_weight, out_weight, up_weight, down_weight, norm_gains, up_bias, down_bias, query_scale = (
        weights
    )
    token_count, model_width = current.shape
    normed, inverse_one = norm_rows(current, norm_gains[0].astype(jnp.float32))
    normed_low = normed.astype(jnp.bfloat16).reshape(series_count, local_length, model_width)
    projected = jnp.einsum(
        "bld,kdc->bkcl", normed_low, qkv_weight, preferred_element_type=jnp.float32
    ).reshape(series_count, 3 * model_width, local_length)
    query_raw = projected[:, :model_width]
    factor = query_factor(query_scale)
    query_low = (
        query_raw.reshape(series_count, HEADS, HEAD, local_length) * factor[None, None, :, None]
    ).astype(jnp.bfloat16)
    pair_low = projected[:, model_width:].astype(jnp.bfloat16)
    pair_all = lax.all_gather(pair_low, "seq", axis=2, tiled=True)
    key_all = pair_all[:, :model_width].reshape(series_count, HEADS, HEAD, total_length)
    value_all = pair_all[:, model_width:].reshape(series_count, HEADS, HEAD, total_length)
    scores = jnp.einsum("bheq,bhek->bhqk", query_low, key_all, preferred_element_type=jnp.float32)
    scores = jnp.where(allowed[:, None], scores, NEG_FILL)
    top_score = jnp.max(scores, axis=-1, keepdims=True)
    exp_scores = jnp.exp(scores - top_score)
    exp_total = jnp.sum(exp_scores, axis=-1, keepdims=True)
    probs_low = (exp_scores / exp_total).astype(jnp.bfloat16)
    log_total = top_score + jnp.log(exp_total)
    attended = jnp.einsum(
        "bhqk,bhek->bheq", probs_low, value_all, preferred_element_type=jnp.float32
    )
    attended_low = attended.astype(jnp.bfloat16).reshape(series_count, model_width, local_length)
    attn_out = jnp.einsum(
        "bdl,de->ble", attended_low, out_weight, preferred_element_type=jnp.float32
    )
    after_attn = current + attn_out.reshape(token_count, model_width)
    normed_two, inverse_two = norm_rows(after_attn, norm_gains[1].astype(jnp.float32))
    mixed_low = normed_two.astype(jnp.bfloat16)
    hidden_pre = jnp.dot(mixed_low, up_weight, preferred_element_type=jnp.float32) + up_bias.astype(
        jnp.float32
    )
    hidden_low = jax.nn.silu(hidden_pre).astype(jnp.bfloat16)
    result = after_attn + (
        jnp.dot(hidden_low, down_weight, preferred_element_type=jnp.float32)
        + down_bias.astype(jnp.float32)
    )
    stored = (
        current,
        inverse_one,
        normed_low,
        query_raw,
        query_low,
        key_all,
        value_all,
        log_total,
        attended_low,
        after_attn,
        inverse_two,
        mixed_low,
        hidden_pre,
        hidden_low,
    )
    return (result, stored)


def backward_layer(upstream, weights, stored, allowed, series_count, local_length, total_length):
    qkv_weight, out_weight, up_weight, down_weight, norm_gains, up_bias, down_bias, query_scale = (
        weights
    )
    (
        current,
        inverse_one,
        normed_low,
        query_raw,
        query_low,
        key_all,
        value_all,
        log_total,
        attended_low,
        after_attn,
        inverse_two,
        mixed_low,
        hidden_pre,
        hidden_low,
    ) = stored
    token_count, model_width = current.shape
    down_low = upstream.astype(jnp.bfloat16)
    grad_down_bias = jnp.sum(down_low, axis=0, dtype=jnp.float32)
    grad_down = jnp.einsum("tf,td->fd", hidden_low, down_low, preferred_element_type=jnp.float32)
    hidden_grad = jnp.einsum("td,fd->tf", down_low, down_weight, preferred_element_type=jnp.float32)
    sigmoid_pre = jax.nn.sigmoid(hidden_pre)
    pre_low = (hidden_grad * sigmoid_pre * (1.0 + hidden_pre * (1.0 - sigmoid_pre))).astype(
        jnp.bfloat16
    )
    grad_up_bias = jnp.sum(pre_low, axis=0, dtype=jnp.float32)
    grad_up = jnp.einsum("td,tf->df", mixed_low, pre_low, preferred_element_type=jnp.float32)
    mixed_grad = jnp.einsum("tf,df->td", pre_low, up_weight, preferred_element_type=jnp.float32)
    norm_grad_two, gain_grad_two = norm_back(
        after_attn, inverse_two, norm_gains[1].astype(jnp.float32), mixed_grad
    )
    attn_grad = upstream + norm_grad_two
    branch_low = attn_grad.astype(jnp.bfloat16).reshape(series_count, local_length, model_width)
    grad_out = jnp.einsum(
        "bdl,ble->de", attended_low, branch_low, preferred_element_type=jnp.float32
    )
    output_low = (
        jnp.einsum("ble,de->bdl", branch_low, out_weight, preferred_element_type=jnp.float32)
        .astype(jnp.bfloat16)
        .reshape(series_count, HEADS, HEAD, local_length)
    )
    scores = jnp.einsum("bheq,bhek->bhqk", query_low, key_all, preferred_element_type=jnp.float32)
    scores = jnp.where(allowed[:, None], scores, NEG_FILL)
    attn_probs = jnp.exp(scores - log_total)
    prob_grad = jnp.einsum(
        "bheq,bhek->bhqk", output_low, value_all, preferred_element_type=jnp.float32
    )
    row_inner = jnp.sum(attn_probs * prob_grad, axis=-1, keepdims=True)
    score_low = (attn_probs * (prob_grad - row_inner)).astype(jnp.bfloat16)
    value_grad = jnp.einsum(
        "bhqk,bheq->bhek",
        attn_probs.astype(jnp.bfloat16),
        output_low,
        preferred_element_type=jnp.float32,
    )
    key_grad = jnp.einsum(
        "bhqk,bheq->bhek", score_low, query_low, preferred_element_type=jnp.float32
    )
    query_grad = jnp.einsum(
        "bhqk,bhek->bheq", score_low, key_all, preferred_element_type=jnp.float32
    )
    pair_grad = jnp.concatenate(
        [
            key_grad.reshape(series_count, model_width, total_length),
            value_grad.reshape(series_count, model_width, total_length),
        ],
        axis=1,
    )
    pair_local = lax.psum_scatter(pair_grad, "seq", scatter_dimension=2, tiled=True)
    key_local, value_local = pair_local[:, :model_width], pair_local[:, model_width:]
    factor = query_factor(query_scale)
    factor_grad = jnp.sum(
        query_grad * query_raw.reshape(series_count, HEADS, HEAD, local_length), axis=(0, 1, 3)
    )
    grad_scale = (
        factor_grad * jax.nn.sigmoid(query_scale.astype(jnp.float32)) * (SOFT_ONE / math.sqrt(HEAD))
    )
    raw_low = (
        (query_grad * factor[None, None, :, None])
        .astype(jnp.bfloat16)
        .reshape(series_count, model_width, local_length)
    )
    projected_grad = jnp.concatenate(
        [raw_low, key_local.astype(jnp.bfloat16), value_local.astype(jnp.bfloat16)], axis=1
    )
    grad_qkv = jnp.einsum(
        "bld,bcl->dc", normed_low, projected_grad, preferred_element_type=jnp.float32
    )
    normed_grad = jnp.einsum(
        "bkcl,kdc->bld",
        projected_grad.reshape(series_count, 3, model_width, local_length),
        qkv_weight,
        preferred_element_type=jnp.float32,
    ).reshape(token_count, model_width)
    norm_grad_one, gain_grad_one = norm_back(
        current, inverse_one, norm_gains[0].astype(jnp.float32), normed_grad
    )
    result = attn_grad + norm_grad_one
    layer_grads = (
        grad_qkv,
        grad_out,
        grad_up,
        grad_down,
        jnp.stack([gain_grad_one, gain_grad_two]),
        grad_up_bias,
        grad_down_bias,
        grad_scale,
    )
    return (result, layer_grads)


def pack_small(norm_gains, up_bias, down_bias, query_scale):
    layers, _, shard = norm_gains.shape
    scale = jnp.pad(query_scale, ((0, 0), (0, shard - query_scale.shape[1])))
    rows = jnp.concatenate([norm_gains.reshape(2 * layers, shard), up_bias, down_bias, scale])
    return jnp.pad(rows, ((0, -rows.shape[0] % 16), (0, -shard % 128)))


def unpack_small(tiny, layers, shard, scale_shard):
    count = tiny.shape[0]
    vectors = tiny[:, : 4 * layers, :shard].transpose(1, 0, 2).reshape(4 * layers, count * shard)
    scale = tiny[:, 4 * layers : 5 * layers, :scale_shard].transpose(1, 0, 2).reshape(layers, count * scale_shard)
    gains = vectors[: 2 * layers].reshape(layers, 2, count * shard)
    return gains, vectors[2 * layers : 3 * layers], vectors[3 * layers :], scale


def pack_tiny(layer_grads, count):
    gains = jnp.concatenate([g[4] for g in layer_grads])
    vectors = jnp.concatenate(
        [gains, jnp.stack([g[5] for g in layer_grads]), jnp.stack([g[6] for g in layer_grads])]
    )
    scale = jnp.stack([g[7] for g in layer_grads])
    shard, part = vectors.shape[1] // count, scale.shape[1] // count
    vectors = vectors.reshape(-1, count, shard)
    scale = jnp.pad(scale.reshape(-1, count, part), ((0, 0), (0, 0), (0, shard - part)))
    rows = jnp.concatenate([vectors, scale]).transpose(1, 0, 2)
    return jnp.pad(rows, ((0, 0), (0, -rows.shape[1] % 16), (0, -shard % 128)))


def unpack_tiny(tiny, layers, shard, part):
    gains = tiny[: 2 * layers, :shard].reshape(layers, 2, shard)
    up, down = tiny[2 * layers : 3 * layers, :shard], tiny[3 * layers : 4 * layers, :shard]
    return gains, up, down, tiny[4 * layers : 5 * layers, :part]


def gather_plain(qkv_weight, out_weight, up_weight, down_weight, small):
    layers, shard, width = out_weight.shape
    qkv = qkv_weight.reshape(layers, shard, 3, width).transpose(0, 2, 1, 3)
    square = jnp.stack([out_weight, up_weight, down_weight], axis=1)
    units = jnp.concatenate([qkv, square], axis=1).reshape(layers * UNITS, shard, width)
    full = lax.all_gather(units, "fsdp", axis=1, tiled=True)
    return full, lax.all_gather(small, "fsdp", axis=0)


def reduce_plain(layer_grads, tiny):
    units = []
    for grads in layer_grads:
        width = grads[0].shape[1]
        units += list(grads[:3]) + [grads[3][:, k * width : (k + 1) * width] for k in range(3)]
    shares = lax.psum_scatter(jnp.stack(units), "fsdp", scatter_dimension=1, tiled=True)
    small = lax.psum_scatter(tiny, "fsdp", scatter_dimension=0, tiled=True)[0]
    return lax.psum(shares, ("replica", "seq")), lax.psum(small, ("replica", "seq"))


def plain(
    series_in,
    cotangent,
    qkv_weight,
    out_weight,
    up_weight,
    down_weight,
    norm_gains,
    up_bias,
    down_bias,
    query_scale,
    pad_length,
    span_starts,
    span_count,
):
    series_count, local_length, model_width = series_in.shape
    seq_count = lax.axis_size("seq")
    group = lax.axis_size("fsdp")
    total_length = local_length * seq_count
    offset = lax.axis_index("seq") * local_length
    allowed = visible(pad_length, span_starts, span_count, offset, local_length, total_length)
    layer_count, shard = qkv_weight.shape[:2]
    scale_shard = query_scale.shape[1]
    small = pack_small(norm_gains, up_bias, down_bias, query_scale)
    full, tiny = gather_plain(qkv_weight, out_weight, up_weight, down_weight, small)
    gains, up_full, down_full, scale_full = unpack_small(tiny, layer_count, shard, scale_shard)
    weights = [
        (
            full[UNITS * l : UNITS * l + 3],
            full[UNITS * l + 3],
            full[UNITS * l + 4],
            full[UNITS * l + 5],
            gains[l],
            up_full[l],
            down_full[l],
            scale_full[l],
        )
        for l in range(layer_count)
    ]
    current = series_in.reshape(series_count * local_length, model_width).astype(jnp.float32)
    stored_list = []
    for l in range(layer_count):
        current, stored = forward_layer(
            current, weights[l], allowed, series_count, local_length, total_length
        )
        stored_list.append(stored)
    series_out = current.reshape(series_count, local_length, model_width).astype(jnp.bfloat16)
    upstream = cotangent.reshape(series_count * local_length, model_width).astype(jnp.float32)
    order = list(reversed(range(layer_count)))
    grads_list = {}
    for l in order:
        upstream, grads_list[l] = backward_layer(
            upstream, weights[l], stored_list[l], allowed, series_count, local_length, total_length
        )
    tiny_grads = pack_tiny([grads_list[l] for l in range(layer_count)], group)
    big = [
        tuple(grads_list[l][k].astype(jnp.bfloat16) for k in (3, 2, 1, 0)) for l in order
    ]
    shares, tiny_sum = reduce_plain(big, tiny_grads)
    shares = shares.reshape(layer_count, UNITS, shard, model_width)[::-1]
    grad_gains, grad_up_bias, grad_down_bias, grad_scale = unpack_tiny(
        tiny_sum, layer_count, shard, scale_shard
    )
    grad_qkv = shares[:, 3:].transpose(0, 2, 1, 3).reshape(layer_count, shard, 3 * model_width)
    input_grad = upstream.reshape(series_count, local_length, model_width).astype(jnp.bfloat16)
    return (
        series_out,
        input_grad,
        grad_qkv.astype(jnp.float32),
        shares[:, 2].astype(jnp.float32),
        shares[:, 1].astype(jnp.float32),
        shares[:, 0].astype(jnp.float32),
        grad_gains,
        grad_up_bias,
        grad_down_bias,
        grad_scale,
    )


def finish(shares, tiny, layers, shard, width, query_scale):
    shares = shares.reshape(layers, UNITS, shard, width)[::-1]
    low = jnp.float32
    place = lax.axis_index("fsdp")
    part = query_scale.shape[1]
    vectors = lax.dynamic_slice_in_dim(tiny[: 4 * layers], place * shard, shard, axis=1)
    scale = lax.dynamic_slice_in_dim(tiny[4 * layers : 5 * layers], place * part, part, axis=1)
    raw = query_scale.astype(jnp.float32)
    scale = scale * (jax.nn.sigmoid(raw) * (SOFT_ONE / math.sqrt(HEAD))) / query_factor(query_scale)
    qkv = jnp.concatenate([shares[:, 5], shares[:, 3], shares[:, 4]], axis=2)
    return (
        qkv.astype(low),
        shares[:, 2].astype(low),
        shares[:, 1].astype(low),
        shares[:, 0].astype(low),
        vectors[: 2 * layers].reshape(layers, 2, shard),
        vectors[2 * layers : 3 * layers],
        vectors[3 * layers :],
        scale,
    )


def fused(
    series_in,
    cotangent,
    qkv_weight,
    out_weight,
    up_weight,
    down_weight,
    norm_gains,
    up_bias,
    down_bias,
    query_scale,
    pad_length,
    span_starts,
    span_count,
):
    layers, shard, width = out_weight.shape
    nz = lax.axis_size("fsdp") // 2
    full, vec, series_out, bias, saved = forward_pass(
        nz,
        series_in[0],
        (qkv_weight, out_weight, up_weight, down_weight),
        (norm_gains, up_bias, down_bias, query_scale),
        (pad_length, span_starts, span_count),
    )
    shares, tiny, input_grad = backward_pass(nz, cotangent[0], full, vec, bias, saved)
    rest = finish(shares, tiny, layers, shard, width, query_scale)
    return (series_out[None], input_grad[None]) + rest


def shards(*args):
    series_in, out_weight = args[0], args[3]
    group = lax.axis_size("fsdp")
    width = series_in.shape[2]
    block = lax.axis_size("replica") == 2 and lax.axis_size("seq") == 2 and group == 8
    block = block and series_in.shape[0] == 1 and width == out_weight.shape[2] == HEADS * HEAD
    block = block and (width // group) % 32 == 0 and width % 256 == 0
    return fused(*args) if block else plain(*args)


def solution(mesh):
    return jax.shard_map(
        shards,
        mesh=mesh,
        in_specs=(
            P(("replica", "fsdp"), "seq", None),
            P(("replica", "fsdp"), "seq", None),
            P(None, "fsdp", None),
            P(None, "fsdp", None),
            P(None, "fsdp", None),
            P(None, "fsdp", None),
            P(None, None, "fsdp"),
            P(None, "fsdp"),
            P(None, "fsdp"),
            P(None, "fsdp"),
            P(("replica", "fsdp")),
            P(("replica", "fsdp"), None),
            P(("replica", "fsdp")),
        ),
        out_specs=(
            P(("replica", "fsdp"), "seq", None),
            P(("replica", "fsdp"), "seq", None),
            P(None, "fsdp", None),
            P(None, "fsdp", None),
            P(None, "fsdp", None),
            P(None, "fsdp", None),
            P(None, None, "fsdp"),
            P(None, "fsdp"),
            P(None, "fsdp"),
            P(None, "fsdp"),
        ),
        check_vma=False,
    )
```

```python
import functools
import math

import jax
import jax.numpy as jnp
from jax import lax
from jax.experimental import pallas as pl
from jax.experimental.pallas import tpu as pltpu
from jax.sharding import PartitionSpec as P

HEADS = 16
HEAD = 80
SPAN = 32


EPSILON = 1e-06
SOFT_ONE = 1.442695041
NEG_FILL = -1e30


def visible(pad_length, span_starts, span_count, offset, local_length, total_length):
    query_pos = offset + jnp.arange(local_length, dtype=jnp.int32)
    key_pos = jnp.arange(total_length, dtype=jnp.int32)
    shared = jnp.zeros((span_starts.shape[0], local_length, total_length), dtype=bool)
    for slot_index in range(span_starts.shape[1]):
        slot_start = span_starts[:, slot_index]
        slot_used = slot_index < span_count
        query_in = (
            slot_used[:, None]
            & (query_pos[None, :] >= slot_start[:, None])
            & (query_pos[None, :] < slot_start[:, None] + SPAN)
        )
        key_in = (key_pos[None, :] >= slot_start[:, None]) & (
            key_pos[None, :] < slot_start[:, None] + SPAN
        )
        shared = shared | query_in[:, :, None] & key_in[:, None, :]
    causal = key_pos[None, :] <= query_pos[:, None]
    allowed = (key_pos[None, None, :] >= pad_length[:, None, None]) & (causal[None] | shared)
    return allowed | (key_pos[None, None, :] == query_pos[None, :, None])


def norm_rows(values, scale_gain):
    inverse = lax.rsqrt(jnp.mean(values * values, axis=-1, keepdims=True) + EPSILON)
    return (values * inverse * scale_gain, inverse)


def norm_back(values, inverse, scale_gain, upstream):
    scaled = upstream * scale_gain
    inner_term = jnp.mean(values * scaled, axis=-1, keepdims=True)
    result = inverse * scaled - values * (inverse * inverse * inverse) * inner_term
    return (result, jnp.sum(upstream * values * inverse, axis=0))


def query_factor(query_scale):
    return jax.nn.softplus(query_scale.astype(jnp.float32)) * (SOFT_ONE / math.sqrt(HEAD))


MESH = pl.DeviceIdType.MESH
UNITS = 6
LAG = 1
PASS = 1
TURN = 1
TOP = 40


class Place:
    def __init__(self, nz):
        self.nz = nz
        self.r = lax.axis_index("replica")
        f = lax.axis_index("fsdp")
        self.s = lax.axis_index("seq")
        self.z = lax.div(f, 2)
        self.c = lax.rem(f, 2)
        self.f = f

    def x(self):
        return (self.r, self.f, 1 - self.s)

    def y(self):
        return (1 - self.r, self.f, self.s)

    def core(self):
        return (self.r, self.f + 1 - 2 * self.c, self.s)

    def to(self, d):
        return (self.r, lax.rem(self.z + d, self.nz) * 2 + self.c, self.s)

    def source(self, d):
        return lax.rem(self.z - d + self.nz, self.nz)

    def peers(self):
        return [self.x(), self.y(), self.core()] + [self.to(d) for d in range(1, self.nz)]

    def hail(self):
        barrier = pltpu.get_barrier_semaphore()
        for peer in self.peers():
            pl.semaphore_signal(barrier, inc=1, device_id=peer, device_id_type=MESH)

    def hear(self):
        pl.semaphore_wait(pltpu.get_barrier_semaphore(), len(self.peers()))


def remote(src, dst, send, recv, device):
    return pltpu.make_async_remote_copy(
        src_ref=src, dst_ref=dst, send_sem=send, recv_sem=recv, device_id=device, device_id_type=MESH
    )


class Gather:
    def __init__(
        self, nz, layers, qkv_ref, out_ref, up_ref, down_ref, small_ref, full_ref, tiny_ref,
        mine, local_sem, keep_sem, zds, zdr, zs, zr, xs, xr, ys, yr, fxs, fxr, fys, fyr, cs, cr, ts, tr,
    ):
        self.__dict__.update(locals())
        self.at = Place(nz)
        self.shard, self.width = out_ref.shape[1], out_ref.shape[2]
        self.half, self.wide = self.shard // 2, self.width // 2
        self.units = layers * UNITS
        self.hops = nz - 1
        self.iterations = self.units + LAG * self.hops + PASS + TURN

    def source(self, way, k):
        return self.at.z - way * k

    def comes(self, way, k):
        z = self.at.z
        return z >= k if way > 0 else z + k < self.nz

    def goes(self, way):
        z = self.at.z
        return z + 1 < self.nz if way > 0 else z >= 1

    def next(self, way):
        at = self.at
        return (at.r, 2 * (at.z + way) + at.c, at.s)

    def slot(self, way, k):
        return 2 * (k - 1) + (0 if way > 0 else 1)

    def block(self, u, z, c, r, s):
        row = pl.multiple_of((2 * z + c) * self.shard + r * self.half, 8)
        col = pl.multiple_of(s * self.wide, 128)
        return self.full_ref.at[u, pl.ds(row, self.half), pl.ds(col, self.wide)]

    def quarter(self, u, z, c, r, s, part):
        top = self.half * TOP // 80 // 8 * 8
        row = pl.multiple_of((2 * z + c) * self.shard + r * self.half + part * top, 8)
        col = pl.multiple_of(s * self.wide, 128)
        size = self.half - top if part else top
        return self.full_ref.at[u, pl.ds(row, size), pl.ds(col, self.wide)]

    def own(self, u, c):
        row = pl.multiple_of((2 * self.at.z + c) * self.shard, 8)
        return self.full_ref.at[u, pl.ds(row, self.shard), :]

    def local(self, layer, k):
        if k < 3:
            piece = self.qkv_ref.at[layer, :, pl.ds(k * self.width, self.width)]
        else:
            piece = (self.out_ref, self.up_ref, self.down_ref)[k - 3].at[layer]
        u = layer * UNITS + k
        return pltpu.make_async_copy(piece, self.mine.at[u], self.local_sem.at[u])

    def keep(self, u):
        return pltpu.make_async_copy(self.mine.at[u], self.own(u, self.at.c), self.keep_sem.at[u])

    def z_copy(self, u, way, k):
        at, n = self.at, self.slot(way, k)
        piece = self.block(u, self.source(way, k - 1), at.c, at.r, at.s)
        held = piece
        if k == 1:
            row = pl.multiple_of(at.r * self.half, 16)
            held = self.mine.at[u, pl.ds(row, self.half), pl.ds(pl.multiple_of(at.s * self.wide, 128), self.wide)]
        return remote(held, piece, self.zs.at[u, n], self.zr.at[u, n], self.next(way))

    def z_diag(self, u, way):
        at, n = self.at, 0 if way > 0 else 1
        piece = self.block(u, at.z, at.c, 1 - at.r, 1 - at.s)
        row = pl.multiple_of((1 - at.r) * self.half, 16)
        col = pl.multiple_of((1 - at.s) * self.wide, 128)
        held = self.mine.at[u, pl.ds(row, self.half), pl.ds(col, self.wide)]
        return remote(held, piece, self.zds.at[u, n], self.zdr.at[u, n], self.next(way))

    def z_came(self, u, way, k):
        at, n = self.at, self.slot(way, k)
        piece = self.block(u, self.source(way, k), at.c, at.r, at.s)
        return remote(piece, piece, self.zs.at[u, n], self.zr.at[u, n], self.next(way))

    def x_copy(self, u, way, k):
        at, n = self.at, self.slot(way, k)
        piece = self.block(u, self.source(way, k), at.c, at.r, at.s)
        return remote(piece, piece, self.xs.at[u, n], self.xr.at[u, n], at.x())

    def y_copy(self, u, way, k):
        at, n = self.at, self.slot(way, k)
        piece = self.block(u, self.source(way, k), at.c, at.r, at.s)
        return remote(piece, piece, self.ys.at[u, n], self.yr.at[u, n], at.y())

    def fx_copy(self, u, way, k):
        at, n = self.at, self.slot(way, k)
        piece = self.quarter(u, self.source(way, k), at.c, 1 - at.r, at.s, 1)
        return remote(piece, piece, self.fxs.at[u, n], self.fxr.at[u, n], at.x())

    def fy_copy(self, u, way, k):
        at, n = self.at, self.slot(way, k)
        piece = self.quarter(u, self.source(way, k), at.c, at.r, 1 - at.s, 0)
        return remote(piece, piece, self.fys.at[u, n], self.fyr.at[u, n], at.y())

    def core_own(self, u):
        own, n = self.own(u, self.at.c), 8 * self.hops
        return remote(self.mine.at[u], own, self.cs.at[u, n], self.cr.at[u, n], self.at.core())

    def core_copy(self, u, way, k, which):
        at = self.at
        r = at.r if which in (0, 1) else 1 - at.r
        s = at.s if which in (0, 2) else 1 - at.s
        piece = self.block(u, self.source(way, k), at.c, r, s)
        n = 4 * self.slot(way, k) + which
        return remote(piece, piece, self.cs.at[u, n], self.cr.at[u, n], at.core())

    def tiny(self, d):
        piece = self.tiny_ref.at[self.at.f]
        return remote(piece, piece, self.ts.at[d - 1], self.tr.at[d - 1], self.at.to(d))

    def tiny_core(self, d):
        piece, n = self.tiny_ref.at[2 * self.at.source(d) + self.at.c], self.nz - 1 + d
        return remote(piece, piece, self.ts.at[n], self.tr.at[n], self.at.core())

    def begin(self):
        self.tiny_ref[self.at.f] = self.small_ref[...].astype(jnp.bfloat16)
        for layer in range(self.layers):
            for k in range(UNITS):
                self.local(layer, k).start()
        self.at.hear()
        for d in range(1, self.nz):
            self.tiny(d).start()
        self.tiny_core(0).start()

    def tiny_pass(self):
        for d in range(1, self.nz):
            self.tiny(d).wait_recv()
            self.tiny_core(d).start()

    def tiny_ready(self):
        for d in range(self.nz):
            self.tiny_core(d).wait_recv()

    def tiny_done(self):
        for d in range(1, self.nz):
            self.tiny(d).wait_send()
        for d in range(self.nz):
            self.tiny_core(d).wait_send()

    def when(self, cond, work):
        pl.when(cond)(work)

    def first(self, u):
        pltpu.make_async_copy(self.out_ref.at[0], self.mine.at[u], self.local_sem.at[u]).wait()
        self.keep(u).start()
        for way in (1, -1):
            def work(way=way):
                self.z_copy(u, way, 1).start()
                self.z_diag(u, way).start()
            self.when(self.goes(way), work)
        self.core_own(u).start()

    def hop(self, u, k):
        for way in (1, -1):
            def work(way=way):
                self.z_came(u, way, k).wait_recv()
                if k < self.hops:
                    self.when(self.goes(way), lambda: self.z_copy(u, way, k + 1).start())
                self.x_copy(u, way, k).start()
                self.y_copy(u, way, k).start()
                self.core_copy(u, way, k, 0).start()
                if k == 1:
                    self.z_diag(u, way).wait_recv()
                    self.core_copy(u, way, k, 3).start()
            self.when(self.comes(way, k), work)

    def forward(self, u, k):
        for way in (1, -1):
            def work(way=way):
                self.x_copy(u, way, k).wait_recv()
                if k > 1:
                    self.fy_copy(u, way, k).start()
                self.core_copy(u, way, k, 1).start()
                self.y_copy(u, way, k).wait_recv()
                if k > 1:
                    self.fx_copy(u, way, k).start()
                self.core_copy(u, way, k, 2).start()
            self.when(self.comes(way, k), work)

    def diagonal(self, u, k):
        for way in (1, -1):
            def work(way=way):
                self.fx_copy(u, way, k).wait_recv()
                self.fy_copy(u, way, k).wait_recv()
                self.core_copy(u, way, k, 3).start()
            self.when(self.comes(way, k), work)

    def step(self, i):
        def stage(lag, work):
            u = i - lag
            self.when((u >= 0) & (u < self.units), lambda: work(u))

        stage(0, self.first)
        for k in range(1, self.hops + 1):
            stage(LAG * k, lambda u, k=k: self.hop(u, k))
        for k in range(1, self.hops + 1):
            stage(LAG * k + PASS, lambda u, k=k: self.forward(u, k))
        for k in range(2, self.hops + 1):
            stage(LAG * k + PASS + TURN, lambda u, k=k: self.diagonal(u, k))

    def ready(self, u):
        self.keep(u).wait()
        self.core_own(u).wait_recv()
        for k in range(1, self.hops + 1):
            for way in (1, -1):
                def work(way=way, k=k):
                    for which in range(4):
                        self.core_copy(u, way, k, which).wait_recv()
                self.when(self.comes(way, k), work)

    def drain(self, u):
        self.core_own(u).wait_send()
        for k in range(1, self.hops + 1):
            for way in (1, -1):
                def sent(way=way, k=k):
                    self.z_copy(u, way, k).wait_send()
                    if k == 1:
                        self.z_diag(u, way).wait_send()
                came = self.goes(way)
                if k > 1:
                    came = came & self.comes(way, k - 1)
                self.when(came, sent)

                def work(way=way, k=k):
                    copies = (self.x_copy, self.y_copy, self.fx_copy, self.fy_copy)
                    for copy in copies if k > 1 else copies[:2]:
                        copy(u, way, k).wait_send()
                    for which in range(4):
                        self.core_copy(u, way, k, which).wait_send()
                self.when(self.comes(way, k), work)

    def finish(self):
        @pl.loop(0, self.units)
        def _(u):
            self.drain(u)

        self.tiny_done()


def gather_scratch(nz, layers, shard, width):
    units, n = layers * UNITS, 2 * (nz - 1)
    dma = pltpu.SemaphoreType.DMA
    return (
        [pltpu.VMEM((units, shard, width), jnp.bfloat16), dma((units,)), dma((units,))]
        + [dma((units, 2))] * 2
        + [dma((units, n))] * 10
        + [dma((units, 1 + 4 * n))] * 2
        + [dma((2 * nz,))] * 2
    )


def dot_nn(a, b):
    return jnp.dot(a, b, preferred_element_type=jnp.float32)


def dot_nt(a, b):
    return lax.dot_general(a, b, (((1,), (1,)), ((), ())), preferred_element_type=jnp.float32)


def dot_tn(a, b):
    return lax.dot_general(a, b, (((0,), (0,)), ((), ())), preferred_element_type=jnp.float32)


ROWS = 128
TALL = 256
BEGIN = 3
SOON = 5


def each_tile(count, body, rows=ROWS):
    @pl.loop(0, count // rows)
    def _(i):
        body(pl.ds(pl.multiple_of(i * rows, rows), rows))


def head_rows(h):
    return pl.ds(pl.multiple_of(h * HEAD, 16), HEAD)


def row_norm(values, gain):
    inverse = lax.rsqrt(jnp.mean(values * values, axis=-1, keepdims=True) + EPSILON)
    return (values * inverse * gain).astype(jnp.bfloat16)


def expand_small(tiny_ref, vec_ref, layers, shard, part):
    width = vec_ref.shape[1]
    count = tiny_ref.shape[0]
    rows, lanes = tiny_ref.shape[1:]
    line = lax.broadcasted_iota(jnp.int32, (lanes, width), 0)
    column = lax.broadcasted_iota(jnp.int32, (lanes, width), 1)
    inner = lax.rem(column, HEAD)

    def place(f, sums):
        plain, scale = sums
        piece = tiny_ref[f]
        hot = jnp.where((column - f * shard == line) & (line < shard), 1.0, 0.0).astype(jnp.bfloat16)
        spread = jnp.where((inner - f * part == line) & (line < part), 1.0, 0.0).astype(jnp.bfloat16)
        return plain + dot_nn(piece, hot), scale + dot_nn(piece, spread)

    zero = jnp.zeros((rows, width), jnp.float32)
    plain, scale = lax.fori_loop(0, count, place, (zero, zero))
    soft = jnp.maximum(scale, 0.0) + jnp.log(1.0 + jnp.exp(-jnp.abs(scale)))
    row = lax.broadcasted_iota(jnp.int32, (rows, width), 0)
    vec_ref[...] = jnp.where(row < 4 * layers, plain, soft * (SOFT_ONE / math.sqrt(HEAD)))


def attend(heads, q_ref, k_ref, v_ref, bias_ref, out_ref, lse_ref):
    queries = q_ref.shape[1]

    @pl.loop(*heads)
    def _(h):
        rows = head_rows(h)
        scores = dot_tn(k_ref[rows, :], q_ref[rows, :]) + bias_ref[:, :queries]
        top = jnp.max(scores, axis=0, keepdims=True)
        grown = jnp.exp(scores - top)
        total = jnp.sum(grown, axis=0, keepdims=True)
        out = dot_nn(v_ref[rows, :], grown.astype(jnp.bfloat16)) * (1.0 / total)
        out_ref[rows, :] = out.astype(jnp.bfloat16)
        lse_ref[h] = top + jnp.log(total)


def forward_kernel(nz, layers, part, *refs):
    series_ref, qkv_ref, out_ref, up_ref, down_ref = refs[:5]
    gains_ref, up_bias_ref, down_bias_ref, scale_ref, pad_ref, starts_ref, count_ref = refs[5:12]
    full_ref, vec_out, series_out, bias_out = refs[12:16]
    per = 11
    saved = [refs[16 + per * l : 16 + per * (l + 1)] for l in range(layers)]
    refs = refs[16 + per * layers :]
    names = ("current", "normed_t", "q", "k", "v", "lse", "att", "after", "mixed", "pre", "hidden")
    held = [dict(zip(names, refs[per * l : per * (l + 1)])) for l in range(layers)]
    refs = refs[per * layers :]
    normed, weights, vec, last, tiny_ref, small_ref, bias_ref, swap_sem, load_sem, save_sem = refs[:10]
    gather = Gather(
        nz, layers, qkv_ref, out_ref, up_ref, down_ref, small_ref, full_ref, tiny_ref, *refs[10:]
    )
    at = gather.at
    length = series_ref.shape[0]
    total = held[0]["normed_t"].shape[1]
    other = total - length

    own_copy = pltpu.make_async_copy(series_ref, held[0]["current"].at[pl.ds(0, length)], swap_sem.at[0])
    swap_copy = remote(
        series_ref, held[0]["current"].at[pl.ds(length, other)], swap_sem.at[1], swap_sem.at[2], at.x()
    )

    def save(l, n):
        return pltpu.make_async_copy(held[l][names[n]], saved[l][n], save_sem.at[l, n])

    def fetch(u):
        return pltpu.make_async_copy(full_ref.at[u], weights.at[u % 2], load_sem.at[u % 2])

    units = layers * UNITS

    def half_fetch(n):
        c = pl.ds(n * gather.wide, gather.wide)
        home = weights.at[(units - 1) % 2, :, c]
        return pltpu.make_async_copy(full_ref.at[units - 1, :, c], home, load_sem.at[2 + n])

    def arrived(u):
        fetch(u).wait()
        return weights.at[u % 2]

    def vector(n):
        return vec[n : n + 1, :]

    def normalize(l):
        b = held[l]
        gain = vector(2 * l)

        def body(r):
            values = row_norm(b["current"][r, :].astype(jnp.float32), gain)
            normed[r, :] = values
            b["normed_t"][:, r] = values.T
        each_tile(total, body)
        save(l, 1).start()

    def project(l, n):
        b = held[l]
        target = b[("q", "k", "v")[n]]
        weight = arrived(l * UNITS + n)

        def body(r):
            values = dot_nn(normed[r, :], weight[...])
            if n == 0:
                values = values * vector(4 * layers + l)
            target[:, r] = values.astype(jnp.bfloat16).T
        each_tile(target.shape[1], body)
        save(l, 2 + n).start()

    def attention(l, first):
        b = held[l]
        heads = (0, HEADS // 2) if first else (HEADS // 2, HEADS)
        attend(heads, b["q"], b["k"], b["v"], bias_ref, b["att"], b["lse"])
        if not first:
            save(l, 5).start()
            save(l, 6).start()

    def output(l):
        b = held[l]
        weight = arrived(l * UNITS + 3)
        gain = vector(2 * l + 1)

        def body(r):
            after = b["current"][r, :].astype(jnp.float32) + dot_tn(b["att"][:, r], weight[...])
            b["after"][r, :] = after
            b["mixed"][r, :] = row_norm(after, gain)
        each_tile(b["after"].shape[0], body)
        save(l, 7).start()
        save(l, 8).start()

    def expand(l):
        b = held[l]
        weight = arrived(l * UNITS + 4)
        bias = vector(2 * layers + l)

        def body(r):
            pre = dot_nn(b["mixed"][r, :], weight[...]) + bias
            b["pre"][r, :] = pre
            b["hidden"][r, :] = (pre * (1.0 / (1.0 + jnp.exp(-pre)))).astype(jnp.bfloat16)
        each_tile(b["pre"].shape[0], body)
        save(l, 9).start()
        save(l, 10).start()

    def close_out(l):
        b = held[l]
        bias = vector(3 * layers + l)
        for n in range(2):
            half_fetch(n).wait()
            c = slice(n * gather.wide, (n + 1) * gather.wide)

            def body(r, c=c):
                values = b["after"][r, c] + (dot_nn(b["hidden"][r, :], weights[(units - 1) % 2, :, c]) + bias[:, c])
                last[r, c] = values.astype(jnp.bfloat16)
            each_tile(b["after"].shape[0], body)
        pltpu.make_async_copy(last, series_out, swap_sem.at[3]).start()

    def contract(l):
        if l + 1 == layers:
            return close_out(l)
        b = held[l]
        weight = arrived(l * UNITS + 5)
        bias = vector(3 * layers + l)

        def body(r):
            values = b["after"][r, :] + (dot_nn(b["hidden"][r, :], weight[...]) + bias)
            held[l + 1]["current"][r, :] = values
        each_tile(b["after"].shape[0], body)
        save(l + 1, 0).start()
        normalize(l + 1)

    tasks = {}

    def add(i, work):
        tasks.setdefault(i, []).append(work)

    lag = gather.iterations - layers * UNITS

    def early():
        gather.tiny_pass()
        gather.tiny_ready()
        expand_small(tiny_ref, vec, layers, gather.shard, part)
        pltpu.make_async_copy(vec, vec_out, swap_sem.at[4]).start()
        fill_bias(bias_ref, length, pad_ref, starts_ref, count_ref)
        pltpu.make_async_copy(bias_ref, bias_out, swap_sem.at[5]).start()

    def begin():
        own_copy.wait()
        swap_copy.wait_recv()
        save(0, 0).start()
        normalize(0)

    def pull(u):
        gather.ready(u)
        if u < units - 1:
            fetch(u).start()
            return
        for n in range(2):
            half_fetch(n).start()

    add(1, early)
    add(BEGIN, begin)
    units = layers * UNITS
    computing = []
    for l in range(layers):
        computing += [[lambda l=l, n=n: project(l, n)] for n in range(3)]
        computing[-1].append(lambda l=l: attention(l, True))
        computing.append([lambda l=l: attention(l, False), lambda l=l: output(l)])
        computing.append([lambda l=l: expand(l)])
        computing.append([lambda l=l: contract(l)])
    for u in range(units):
        add(u + lag, lambda u=u: pull(u))
        late = u >= units - SOON
        for one in computing[u]:
            add(u + lag + (0 if late else 1), one)

    at.hail()
    own_copy.start()
    small_ref[...] = jnp.zeros_like(small_ref)
    shard = gather.shard
    for l in range(layers):
        for n in range(2):
            small_ref[2 * l + n : 2 * l + n + 1, :shard] = gains_ref[l, n : n + 1, :].astype(jnp.float32)
    groups = ((2 * layers, up_bias_ref, shard), (3 * layers, down_bias_ref, shard), (4 * layers, scale_ref, part))
    for base, ref, size in groups:
        small_ref[base : base + layers, :size] = ref[...].astype(jnp.float32)
    gather.begin()
    swap_copy.start()

    @pl.loop(0, gather.iterations)
    def _(i):
        gather.step(i)
        for when, work in sorted(tasks.items()):
            @pl.when(i == when)
            def _(work=work):
                for one in work:
                    one()

    swap_copy.wait_send()
    pltpu.make_async_copy(last, series_out, swap_sem.at[3]).wait()
    pltpu.make_async_copy(vec, vec_out, swap_sem.at[4]).wait()
    pltpu.make_async_copy(bias_ref, bias_out, swap_sem.at[5]).wait()
    for l in range(layers):
        for n in range(per):
            save(l, n).wait()
    gather.finish()


def saved_shapes(layers, length, total, width):
    low, wide = jnp.bfloat16, jnp.float32
    shapes = []
    for l in range(layers):
        count = length if l == layers - 1 else total
        kind = low if l == 0 else wide
        shapes.append(
            [
                ((total, width), kind),
                ((width, total), low),
                ((width, count), low),
                ((width, total), low),
                ((width, total), low),
                ((HEADS, 1, count), wide),
                ((width, count), low),
                ((count, width), wide),
                ((count, width), low),
                ((count, width), wide),
                ((count, width), low),
            ]
        )
    return shapes


def forward_pass(nz, series, matrices, vectors, spans):
    layers, shard, width = matrices[1].shape
    length, part = series.shape[0], vectors[3].shape[1]
    total = 2 * length
    units = layers * UNITS
    low, wide = jnp.bfloat16, jnp.float32
    shapes = [one for group in saved_shapes(layers, length, total, width) for one in group]
    small = (5 * layers + -5 * layers % 16, shard + -shard % 128)
    dma = pltpu.SemaphoreType.DMA
    anywhere = pl.BlockSpec(memory_space=pl.ANY)
    inside = pl.BlockSpec(memory_space=pltpu.VMEM)
    scalars = pl.BlockSpec(memory_space=pltpu.SMEM)
    count = 2 * nz
    results = pl.pallas_call(
        functools.partial(forward_kernel, nz, layers, part),
        out_shape=(
            jax.ShapeDtypeStruct((units, count * shard, width), low),
            jax.ShapeDtypeStruct((small[0], width), wide),
            jax.ShapeDtypeStruct((length, width), low),
            jax.ShapeDtypeStruct((total, total), wide),
        )
        + tuple(jax.ShapeDtypeStruct(*one) for one in shapes),
        in_specs=[anywhere] * 5 + [inside] * 4 + [scalars] * 3,
        out_specs=(anywhere,) * (4 + len(shapes)),
        scratch_shapes=[pltpu.VMEM(*one) for one in shapes]
        + [
            pltpu.VMEM((total, width), low),
            pltpu.VMEM((2, width, width), low),
            pltpu.VMEM((small[0], width), wide),
            pltpu.VMEM((length, width), low),
            pltpu.VMEM((count,) + small, low),
            pltpu.VMEM(small, wide),
            pltpu.VMEM((total, total), wide),
            dma((6,)),
            dma((4,)),
            dma((layers, 11)),
        ]
        + gather_scratch(nz, layers, shard, width),
        compiler_params=pltpu.CompilerParams(
            collective_id=1, has_side_effects=True, vmem_limit_bytes=60 << 20
        ),
    )(series, *matrices, *vectors, *spans)
    full, vec, out, bias = results[:4]
    saved = [results[4 + 11 * l : 15 + 11 * l] for l in range(layers)]
    return full, vec, out, bias, saved


def fill_bias(bias_ref, length, pad_ref, starts_ref, count_ref):
    s = lax.axis_index("seq")
    total = bias_ref.shape[0]
    pad, count = pad_ref[0], count_ref[0]

    def place(index):
        return jnp.where(index < length, s * length + index, -s * length + index)

    query = place(lax.broadcasted_iota(jnp.int32, (ROWS, total), 1))

    @pl.loop(0, total // ROWS)
    def _(i):
        key = place(lax.broadcasted_iota(jnp.int32, (ROWS, total), 0) + i * ROWS)
        seen = key <= query
        for slot in range(starts_ref.shape[1]):
            start = jnp.where(slot < count, starts_ref[0, slot], -2 * SPAN)
            stop = start + SPAN
            seen = seen | (key >= start) & (key < stop) & (query >= start) & (query < stop)
        allowed = (seen & (key >= pad)) | (key == query)
        rows = pl.ds(pl.multiple_of(i * ROWS, ROWS), ROWS)
        bias_ref[rows, :] = jnp.where(allowed, 0.0, NEG_FILL)


SLOTS = 14
LAGS = (1, 3, 6, 8, 10, 12)


class Reduce:
    def __init__(
        self, nz, units, full_ref, tiny, tiny_out, grads, held, bx, by, near, far, swap, tiny_in,
        as_, ar, bs, br, zs, zr, es, er, ls, ps, pr, ts, tr, free,
    ):
        self.__dict__.update(locals())
        self.at = Place(nz)
        self.slots, _, self.half, self.width = held.shape
        self.shard = 2 * self.half
        self.wide, self.low = self.width // 2, nz // 2
        self.steps = range(1, nz)
        self.parts = 2 * units
        self.iterations = self.parts + LAGS[-1]
        self.side = self.column(self.at.z)

    def column(self, z):
        return jnp.where(z < self.low, self.at.s, self.at.r)

    def cols(self, side):
        return pl.ds(pl.multiple_of(side * self.wide, 128), self.wide)

    def slot(self, h):
        return lax.rem(h, self.slots)

    def band(self, h):
        return pl.ds(pl.multiple_of(lax.rem(h, 2) * self.half, 16), self.half)

    def z_peer(self, d):
        at = self.at
        z = lax.rem(at.z + d, self.nz) if 2 * d == self.nz else at.z + 1 - 2 * lax.rem(at.z, 2)
        return z, (at.r, 2 * z + at.c, at.s)

    def pair_peer(self):
        at, first = self.at, self.at.z < self.low
        return (jnp.where(first, 1 - at.r, at.r), at.f, jnp.where(first, at.s, 1 - at.s))

    def last_peer(self):
        at, first = self.at, self.at.z < self.low
        return (jnp.where(first, at.r, 1 - at.r), at.f, jnp.where(first, 1 - at.s, at.s))

    def a_copy(self, h):
        piece = self.grads.at[:, 1 - self.at.c, self.band(h), :]
        return remote(piece, self.held.at[self.slot(h)], self.as_.at[h], self.ar.at[h], self.at.core())

    def bx_copy(self, h):
        piece = self.held.at[self.slot(h), pl.ds(0, self.low), :, self.cols(1 - self.at.s)]
        return remote(piece, self.bx.at[h], self.bs.at[h, 0], self.br.at[h, 0], self.at.x())

    def by_copy(self, h):
        piece = self.held.at[self.slot(h), pl.ds(self.low, self.low), :, self.cols(1 - self.at.r)]
        return remote(piece, self.by.at[h], self.bs.at[h, 1], self.br.at[h, 1], self.at.y())

    def near_copy(self, h, n):
        target = n * 2 + 1 - lax.rem(self.at.z, 2)
        side = (self.at.s, self.at.r)[n]
        piece = self.held.at[self.slot(h), target, :, self.cols(side)]
        return remote(piece, self.near.at[h, n], self.zs.at[h, n], self.zr.at[h, n], self.z_peer(1)[1])

    def far_copy(self, h):
        z, peer = self.z_peer(2)
        piece = self.held.at[self.slot(h), z, :, self.cols(self.column(z))]
        return remote(piece, self.far.at[h], self.zs.at[h, 2], self.zr.at[h, 2], peer)

    def pair_copy(self, h):
        piece = self.held.at[self.slot(h), self.at.z, :, self.cols(self.side)]
        return remote(piece, self.swap.at[h], self.es.at[h], self.er.at[h], self.pair_peer())

    def spot(self, h):
        return self.full_ref.at[lax.div(h, 2), self.band(h), self.cols(self.side)]

    def put_copy(self, h):
        return pltpu.make_async_copy(self.bx.at[h, 0], self.spot(h), self.ls.at[h])

    def last_copy(self, h):
        return remote(self.bx.at[h, 0], self.spot(h), self.ps.at[h], self.pr.at[h], self.last_peer())

    def plus(self, *values):
        return sum(v.astype(jnp.float32) for v in values).astype(jnp.bfloat16)

    def a_start(self, h):
        @pl.when(h >= self.slots)
        def _():
            pl.semaphore_wait(self.free, 1)
        self.a_copy(h).start()

    def a_stage(self, h):
        held, slot, c = self.held, self.slot(h), self.at.c
        self.a_copy(h).wait_recv()

        @pl.loop(0, self.nz)
        def _(z):
            held[slot, z] = self.plus(held[slot, z], self.grads[z, c, self.band(h), :])
        self.bx_copy(h).start()
        self.by_copy(h).start()
        self.a_copy(h).wait_send()

    def b_stage(self, h):
        held, slot, at = self.held, self.slot(h), self.at
        for copy, came, base, side in (
            (self.bx_copy(h), self.bx, 0, at.s),
            (self.by_copy(h), self.by, self.low, at.r),
        ):
            copy.wait()

            @pl.loop(0, self.low)
            def _(z, came=came, base=base, side=side):
                mine = self.cols(side)
                held[slot, base + z, :, mine] = self.plus(held[slot, base + z, :, mine], came[h, z])
        for n in range(2):
            self.near_copy(h, n).start()

    def near_stage(self, h):
        held, slot, at = self.held, self.slot(h), self.at
        for n in range(2):
            self.near_copy(h, n).wait()
            target, mine = 2 * n + lax.rem(at.z, 2), self.cols((at.s, at.r)[n])
            held[slot, target, :, mine] = self.plus(held[slot, target, :, mine], self.near[h, n])
        self.far_copy(h).start()

    def far_stage(self, h):
        held, slot, z, mine = self.held, self.slot(h), self.at.z, self.cols(self.side)
        self.far_copy(h).wait()
        held[slot, z, :, mine] = self.plus(held[slot, z, :, mine], self.far[h])
        self.pair_copy(h).start()

    def pair_stage(self, h):
        held, slot, z, mine = self.held, self.slot(h), self.at.z, self.cols(self.side)
        self.pair_copy(h).wait()
        self.bx[h, 0] = self.plus(held[slot, z, :, mine], self.swap[h])

        @pl.when(h + self.slots < self.parts)
        def _():
            pl.semaphore_signal(self.free, inc=1, device_id=self.at.core(), device_id_type=MESH)
        self.put_copy(h).start()
        self.last_copy(h).start()

    def close(self, h):
        self.put_copy(h).wait()
        self.last_copy(h).wait()

    def step(self, i):
        def stage(lag, work):
            h = i - lag
            pl.when((h >= 0) & (h < self.parts))(lambda: work(h))

        works = (self.a_stage, self.b_stage, self.near_stage, self.far_stage, self.pair_stage, self.close)
        for lag, work in zip(LAGS, works):
            stage(lag, work)

    def launch(self, i):
        @pl.when((lax.rem(i, 2) == 0) & (i < self.parts))
        def _():
            self.a_start(i)
            self.a_start(i + 1)

    def tiny_copy(self, n, peer):
        return remote(self.tiny, self.tiny_in.at[n], self.ts.at[n], self.tr.at[n], peer)

    def tiny_z(self, d):
        return remote(self.tiny, self.tiny_in.at[2 + d], self.ts.at[2 + d], self.tr.at[2 + d], self.at.to(d))

    def tiny_step(self, n):
        peers = (self.at.core(), self.at.x(), self.at.y())
        if 0 < n <= 3:
            copy = self.tiny_copy(n - 1, peers[n - 1])
            copy.wait()
            self.tiny[...] = self.tiny[...] + self.tiny_in[n - 1]
        if n < 3:
            self.tiny_copy(n, peers[n]).start()
        if n == 3:
            for d in self.steps:
                self.tiny_z(d).start()
        if n == 4:
            for d in self.steps:
                self.tiny_z(d).wait()
            self.tiny_out[...] = self.tiny[...] + sum(self.tiny_in[2 + d] for d in self.steps)


def backward_kernel(nz, layers, length, total, *refs):
    cot_ref, full_ref, vec, bias_ref = refs[:4]
    per = 11
    saved = [refs[4 + per * l : 4 + per * (l + 1)] for l in range(layers)]
    refs = refs[4 + per * layers :]
    share_ref, tiny_out, input_ref = refs[:3]
    (
        up, wide_a, wide_b, hidden, mixed, pre_low, low, trio, att, do, lse, weight, came, sent,
        load_sem, weight_sem, x_sem, tiny, grads,
    ) = refs[3:22]
    units = layers * UNITS
    k, v, q = trio.at[0], trio.at[1], trio.at[2]
    reduce = Reduce(nz, units, share_ref, tiny, tiny_out, grads, *refs[22:])
    at = reduce.at
    width = up.shape[1]
    wide, half_z = width // 2, nz // 2
    shard = reduce.shard
    names = ("current", "normed_t", "q", "k", "v", "lse", "att", "after", "mixed", "pre", "hidden")
    homes = dict(
        normed_t=att, q=q, k=k, v=v, lse=lse, att=att, after=wide_b, mixed=mixed, pre=wide_a, hidden=hidden
    )

    def load(l, name):
        n = names.index(name)
        source = saved[l][n]
        home = homes.get(name, hidden if source.dtype == jnp.bfloat16 else wide_b)
        if home.shape != source.shape:
            if len(source.shape) == 3:
                home = home.at[:, :, pl.ds(0, source.shape[2])]
            elif source.shape[0] != home.shape[0]:
                home = home.at[pl.ds(0, source.shape[0]), :]
            else:
                home = home.at[:, pl.ds(0, source.shape[1])]
        return pltpu.make_async_copy(source, home, load_sem.at[l, n])

    def fetch(u):
        return pltpu.make_async_copy(full_ref.at[u], weight, weight_sem.at[0])

    def fill(product):
        @pl.loop(0, 2)
        def _(i):
            @pl.loop(0, 2)
            def _(j):
                r = pl.ds(pl.multiple_of(i * wide, 128), wide)
                c = pl.ds(pl.multiple_of(j * wide, 128), wide)
                value = product(r, c).astype(jnp.bfloat16).reshape(half_z, 2, shard, wide)
                grads[pl.ds(i * half_z, half_z), :, :, c] = value

    def vector(n):
        return vec[n : n + 1, :]

    def gather_row(n, values):
        tiny[n : n + 1, :] = tiny[n : n + 1, :] + jnp.sum(values, axis=0, keepdims=True)

    def norm_tile(values, gain, w, n):
        inverse = lax.rsqrt(jnp.mean(values * values, axis=-1, keepdims=True) + EPSILON)
        scaled = w * gain
        inner = jnp.mean(values * scaled, axis=-1, keepdims=True)
        gather_row(n, w * values * inverse)
        return inverse * scaled - values * (inverse * inverse * inverse) * inner

    def count(l):
        return length if l == layers - 1 else total

    def next_load(l, *which):
        if l > 0:
            for name in which:
                load(l - 1, name).start()

    def down(l):
        m = count(l)
        load(l, "hidden").wait()

        def body(r):
            value = up[r, :].astype(jnp.bfloat16)
            low[r, :] = value
            gather_row(3 * layers + l, value.astype(jnp.float32))
        each_tile(m, body)
        fill(lambda r, c: dot_tn(hidden[:m, r], low[:m, c]))
        if saved[l][0].dtype == jnp.bfloat16:
            load(l, "current").start()
        else:
            next_load(l, "hidden")

    def expand(l):
        fetch(l * UNITS + 5).wait()
        load(l, "pre").wait()

        def body(r):
            grown = dot_nt(low[r, :], weight[...])
            value = wide_a[r, :]
            gate = 1.0 / (1.0 + jnp.exp(-value))
            result = (grown * gate * (1.0 + value * (1.0 - gate))).astype(jnp.bfloat16)
            pre_low[r, :] = result
            gather_row(2 * layers + l, result.astype(jnp.float32))
        each_tile(count(l), body, TALL)
        fetch(l * UNITS + 4).start()

    def fill_up(l):
        m = count(l)
        load(l, "mixed").wait()
        fill(lambda r, c: dot_tn(mixed[:m, r], pre_low[:m, c]))
        next_load(l, "mixed")

    def output(l):
        fetch(l * UNITS + 4).wait()
        load(l, "after").wait()
        gain = vector(2 * l + 1)

        def body(r):
            w = dot_nt(pre_low[r, :], weight[...])
            value = up[r, :] + norm_tile(wide_b[r, :], gain, w, 2 * l + 1)
            up[r, :] = value
            low[r, :] = value.astype(jnp.bfloat16)
        each_tile(count(l), body, TALL)
        fetch(l * UNITS + 3).start()
        if saved[l][0].dtype != jnp.bfloat16:
            load(l, "current").start()

    def fill_out(l):
        m = count(l)
        load(l, "att").wait()
        fill(lambda r, c: dot_nn(att[r, :m], low[:m, c]))
        load(l, "normed_t").start()

    def attention(l, start, stop):
        m = count(l)
        row = 4 * layers + l
        factor = jnp.broadcast_to(vec[row : row + 1, 0:128], (128, 128)).T[0:HEAD, 0:1]

        def head(h, sums):
            rows = head_rows(h)
            kh, vh, qh, oh = k[rows, :], v[rows, :], q[rows, :m], do[rows, :m]
            scores = dot_tn(kh, qh) + bias_ref[:, :m]
            probs = jnp.exp(scores - lse[h, :, :m])
            weighted = probs * dot_tn(vh, oh)
            inner = jnp.sum(weighted, axis=0, keepdims=True)
            score = (weighted - probs * inner).astype(jnp.bfloat16)
            v[rows, :] = dot_nt(oh, probs.astype(jnp.bfloat16)).astype(jnp.bfloat16)
            k[rows, :] = dot_nt(qh, score).astype(jnp.bfloat16)
            query = dot_nn(kh, score)
            q[rows, :m] = (query * factor).astype(jnp.bfloat16)
            return sums + jnp.sum(query * qh.astype(jnp.float32), axis=1, keepdims=True)

        sums = lax.fori_loop(start, stop, head, jnp.zeros((HEAD, 1), jnp.float32))
        flat = jnp.broadcast_to(sums, (HEAD, 128)).T
        tiny[row : row + 1, 0:HEAD] = tiny[row : row + 1, 0:HEAD] + flat[0:1, :]

    def open_heads(l):
        m = count(l)
        fetch(l * UNITS + 3).wait()

        def body(r):
            do[r, :m] = dot_nt(weight[r, :], low[:m, :]).astype(jnp.bfloat16)
        each_tile(width, body, wide)
        fetch(l * UNITS + 1).start()
        for name in ("q", "k", "v", "lse"):
            load(l, name).wait()

    def turn(l):
        next_load(l, "lse")
        load(l, "normed_t").wait()

    def fill_project(n):
        fill(lambda r, c: dot_nt(att[r, :], trio[n, c, :]))

    def project(l, n):
        fetch(l * UNITS + lax.rem(n + 1, 3)).wait()
        count = jnp.where((n == 2) & (l == layers - 1), length, total)

        @pl.loop(0, lax.div(count, TALL))
        def _(i):
            r = pl.ds(pl.multiple_of(i * TALL, TALL), TALL)
            value = dot_nt(trio[n, :, r].T, weight[...])
            wide_a[r, :] = value + jnp.where(n > 0, wide_a[r, :], 0.0)

    def settle(l, n):
        if n < 2:
            fetch(l * UNITS + (2, 0)[n]).start()
            return
        if l > 0:
            fetch((l - 1) * UNITS + 5).start()
        load(l, "current").wait()
        gain = vector(2 * l)
        current = hidden if saved[l][0].dtype == jnp.bfloat16 else wide_b

        def close(r):
            return norm_tile(current[r, :].astype(jnp.float32), gain, wide_a[r, :], 2 * l)

        own = count(l)

        def first(r):
            up[r, :] = up[r, :] + close(r)
        each_tile(own, first)
        if own < total:
            @pl.loop(own // ROWS, total // ROWS)
            def _(i):
                r = pl.ds(pl.multiple_of(i * ROWS, ROWS), ROWS)
                up[r, :] = close(r)
        next_load(l, "pre", "after", "att", "q", "k", "v")
        if l == 0:
            sent[...] = up[length:, :].astype(jnp.bfloat16)

    reply = remote(sent, came, x_sem.at[0], x_sem.at[1], at.x())
    def start_layer(l):
        down(l)
        expand(l)

    def middle(l):
        open_heads(l)
        fill_up(l)

    before = {0: start_layer, 1: output, 2: middle, 4: fill_out}
    heads = (0, 0, 0, 1, 6, 9, 14, HEADS)
    after = {6: turn}
    later = {7: lambda l: settle(l, 0), 9: lambda l: settle(l, 1), 11: lambda l: settle(l, 2)}
    last = layers - 1
    start_copy = pltpu.make_async_copy(cot_ref, sent, x_sem.at[2])
    at.hail()
    start_copy.start()
    for name in ("hidden", "pre", "mixed", "after", "att", "q", "k", "v", "lse"):
        load(last, name).start()
    fetch(last * UNITS + 5).start()
    tiny[...] = jnp.zeros_like(tiny)
    if count(last) < total:
        trio[2, :, count(last) :] = jnp.zeros((width, total - count(last)), jnp.bfloat16)
    start_copy.wait()
    up[:length, :] = sent[...].astype(jnp.float32)
    start_layer(last)
    at.hear()

    @pl.loop(0, reduce.iterations)
    def _(i):
        reduce.step(i)
        phase, layer = lax.rem(i, 2 * UNITS), last - lax.div(i, 2 * UNITS)
        inside = (i < reduce.parts) & (phase >= UNITS)

        def tasks(some):
            for l in range(layers):
                for n, one in some:
                    if l == last and n == 0:
                        continue

                    @pl.when(i == (last - l) * 2 * UNITS + n)
                    def _(one=one, l=l):
                        one(l)

        tasks(before.items())
        first = sum(jnp.where(phase == n, heads[n], 0) for n in range(2, 7))
        final = sum(jnp.where(phase == n, heads[n + 1], 0) for n in range(2, 7))
        for l in range(layers):
            @pl.when((phase >= 2) & (phase < 7) & (layer == l))
            def _(l=l):
                attention(l, first, final)

        tasks(after.items())

        @pl.when(inside & (lax.rem(phase, 2) == 0))
        def _():
            fill_project(lax.div(phase - UNITS, 2))

        @pl.when(inside & (lax.rem(phase, 2) == 1))
        def _():
            project(layer, lax.div(phase - UNITS, 2))

        tasks(later.items())
        reduce.launch(i)

        @pl.when(i == reduce.parts)
        def _():
            reply.start()

        for n in range(5):
            @pl.when(i == reduce.parts + 1 + 2 * n)
            def _(n=n):
                reduce.tiny_step(n)

    reply.wait()
    input_ref[...] = (up[:length, :] + came[...].astype(jnp.float32)).astype(jnp.bfloat16)


def backward_pass(nz, cotangent, full, vec, bias, saved):
    layers = len(saved)
    units = layers * UNITS
    length, width = cotangent.shape
    total = bias.shape[0]
    shard = width // (2 * nz)
    half, wide, low, n = shard // 2, width // 2, nz // 2, nz - 1
    parts = 2 * units
    slots = min(SLOTS, parts)
    flat = [one for group in saved for one in group]
    rows = vec.shape[0]
    dma = pltpu.SemaphoreType.DMA
    small, large = jnp.bfloat16, jnp.float32
    anywhere = pl.BlockSpec(memory_space=pl.ANY)
    inside = pl.BlockSpec(memory_space=pltpu.VMEM)
    natural, turned = (total, width), (width, total)
    return pl.pallas_call(
        functools.partial(backward_kernel, nz, layers, length, total),
        out_shape=(
            jax.ShapeDtypeStruct((units, shard, width), small),
            jax.ShapeDtypeStruct((rows, width), large),
            jax.ShapeDtypeStruct((length, width), small),
        ),
        in_specs=[anywhere, anywhere, inside, inside] + [anywhere] * len(flat),
        out_specs=(anywhere, inside, inside),
        scratch_shapes=[
            pltpu.VMEM(natural, large),
            pltpu.VMEM(natural, large),
            pltpu.VMEM(natural, large),
            pltpu.VMEM(natural, small),
            pltpu.VMEM(natural, small),
            pltpu.VMEM(natural, small),
            pltpu.VMEM(natural, small),
            pltpu.VMEM((3,) + turned, small),
            pltpu.VMEM(turned, small),
            pltpu.VMEM(turned, small),
            pltpu.VMEM((HEADS, 1, total), large),
            pltpu.VMEM((width, width), small),
            pltpu.VMEM((length, width), small),
            pltpu.VMEM((length, width), small),
            dma((layers, 11)),
            dma((1,)),
            dma((3,)),
            pltpu.VMEM((rows, width), large),
            pltpu.VMEM((nz, 2, shard, width), small),
            pltpu.VMEM((slots, nz, half, width), small),
            pltpu.VMEM((parts, low, half, wide), small),
            pltpu.VMEM((parts, low, half, wide), small),
            pltpu.VMEM((parts, 2, half, wide), small),
            pltpu.VMEM((parts, half, wide), small),
            pltpu.VMEM((parts, half, wide), small),
            pltpu.VMEM((3 + n, rows, width), large),
            dma((parts,)), dma((parts,)),
            dma((parts, 2)), dma((parts, 2)),
            dma((parts, 3)), dma((parts, 3)),
            dma((parts,)), dma((parts,)),
            dma((parts,)),
            dma((parts,)), dma((parts,)),
            dma((3 + n,)), dma((3 + n,)),
            pltpu.SemaphoreType.REGULAR,
        ],
        compiler_params=pltpu.CompilerParams(
            collective_id=2, has_side_effects=True, vmem_limit_bytes=63 << 20
        ),
    )(cotangent, full, vec, bias, *flat)


def forward_layer(current, weights, allowed, series_count, local_length, total_length):
    qkv_weight, out_weight, up_weight, down_weight, norm_gains, up_bias, down_bias, query_scale = (
        weights
    )
    token_count, model_width = current.shape
    normed, inverse_one = norm_rows(current, norm_gains[0].astype(jnp.float32))
    normed_low = normed.astype(jnp.bfloat16).reshape(series_count, local_length, model_width)
    projected = jnp.einsum(
        "bld,kdc->bkcl", normed_low, qkv_weight, preferred_element_type=jnp.float32
    ).reshape(series_count, 3 * model_width, local_length)
    query_raw = projected[:, :model_width]
    factor = query_factor(query_scale)
    query_low = (
        query_raw.reshape(series_count, HEADS, HEAD, local_length) * factor[None, None, :, None]
    ).astype(jnp.bfloat16)
    pair_low = projected[:, model_width:].astype(jnp.bfloat16)
    pair_all = lax.all_gather(pair_low, "seq", axis=2, tiled=True)
    key_all = pair_all[:, :model_width].reshape(series_count, HEADS, HEAD, total_length)
    value_all = pair_all[:, model_width:].reshape(series_count, HEADS, HEAD, total_length)
    scores = jnp.einsum("bheq,bhek->bhqk", query_low, key_all, preferred_element_type=jnp.float32)
    scores = jnp.where(allowed[:, None], scores, NEG_FILL)
    top_score = jnp.max(scores, axis=-1, keepdims=True)
    exp_scores = jnp.exp(scores - top_score)
    exp_total = jnp.sum(exp_scores, axis=-1, keepdims=True)
    probs_low = (exp_scores / exp_total).astype(jnp.bfloat16)
    log_total = top_score + jnp.log(exp_total)
    attended = jnp.einsum(
        "bhqk,bhek->bheq", probs_low, value_all, preferred_element_type=jnp.float32
    )
    attended_low = attended.astype(jnp.bfloat16).reshape(series_count, model_width, local_length)
    attn_out = jnp.einsum(
        "bdl,de->ble", attended_low, out_weight, preferred_element_type=jnp.float32
    )
    after_attn = current + attn_out.reshape(token_count, model_width)
    normed_two, inverse_two = norm_rows(after_attn, norm_gains[1].astype(jnp.float32))
    mixed_low = normed_two.astype(jnp.bfloat16)
    hidden_pre = jnp.dot(mixed_low, up_weight, preferred_element_type=jnp.float32) + up_bias.astype(
        jnp.float32
    )
    hidden_low = jax.nn.silu(hidden_pre).astype(jnp.bfloat16)
    result = after_attn + (
        jnp.dot(hidden_low, down_weight, preferred_element_type=jnp.float32)
        + down_bias.astype(jnp.float32)
    )
    stored = (
        current,
        inverse_one,
        normed_low,
        query_raw,
        query_low,
        key_all,
        value_all,
        log_total,
        attended_low,
        after_attn,
        inverse_two,
        mixed_low,
        hidden_pre,
        hidden_low,
    )
    return (result, stored)


def backward_layer(upstream, weights, stored, allowed, series_count, local_length, total_length):
    qkv_weight, out_weight, up_weight, down_weight, norm_gains, up_bias, down_bias, query_scale = (
        weights
    )
    (
        current,
        inverse_one,
        normed_low,
        query_raw,
        query_low,
        key_all,
        value_all,
        log_total,
        attended_low,
        after_attn,
        inverse_two,
        mixed_low,
        hidden_pre,
        hidden_low,
    ) = stored
    token_count, model_width = current.shape
    down_low = upstream.astype(jnp.bfloat16)
    grad_down_bias = jnp.sum(down_low, axis=0, dtype=jnp.float32)
    grad_down = jnp.einsum("tf,td->fd", hidden_low, down_low, preferred_element_type=jnp.float32)
    hidden_grad = jnp.einsum("td,fd->tf", down_low, down_weight, preferred_element_type=jnp.float32)
    sigmoid_pre = jax.nn.sigmoid(hidden_pre)
    pre_low = (hidden_grad * sigmoid_pre * (1.0 + hidden_pre * (1.0 - sigmoid_pre))).astype(
        jnp.bfloat16
    )
    grad_up_bias = jnp.sum(pre_low, axis=0, dtype=jnp.float32)
    grad_up = jnp.einsum("td,tf->df", mixed_low, pre_low, preferred_element_type=jnp.float32)
    mixed_grad = jnp.einsum("tf,df->td", pre_low, up_weight, preferred_element_type=jnp.float32)
    norm_grad_two, gain_grad_two = norm_back(
        after_attn, inverse_two, norm_gains[1].astype(jnp.float32), mixed_grad
    )
    attn_grad = upstream + norm_grad_two
    branch_low = attn_grad.astype(jnp.bfloat16).reshape(series_count, local_length, model_width)
    grad_out = jnp.einsum(
        "bdl,ble->de", attended_low, branch_low, preferred_element_type=jnp.float32
    )
    output_low = (
        jnp.einsum("ble,de->bdl", branch_low, out_weight, preferred_element_type=jnp.float32)
        .astype(jnp.bfloat16)
        .reshape(series_count, HEADS, HEAD, local_length)
    )
    scores = jnp.einsum("bheq,bhek->bhqk", query_low, key_all, preferred_element_type=jnp.float32)
    scores = jnp.where(allowed[:, None], scores, NEG_FILL)
    attn_probs = jnp.exp(scores - log_total)
    prob_grad = jnp.einsum(
        "bheq,bhek->bhqk", output_low, value_all, preferred_element_type=jnp.float32
    )
    row_inner = jnp.sum(attn_probs * prob_grad, axis=-1, keepdims=True)
    score_low = (attn_probs * (prob_grad - row_inner)).astype(jnp.bfloat16)
    value_grad = jnp.einsum(
        "bhqk,bheq->bhek",
        attn_probs.astype(jnp.bfloat16),
        output_low,
        preferred_element_type=jnp.float32,
    )
    key_grad = jnp.einsum(
        "bhqk,bheq->bhek", score_low, query_low, preferred_element_type=jnp.float32
    )
    query_grad = jnp.einsum(
        "bhqk,bhek->bheq", score_low, key_all, preferred_element_type=jnp.float32
    )
    pair_grad = jnp.concatenate(
        [
            key_grad.reshape(series_count, model_width, total_length),
            value_grad.reshape(series_count, model_width, total_length),
        ],
        axis=1,
    )
    pair_local = lax.psum_scatter(pair_grad, "seq", scatter_dimension=2, tiled=True)
    key_local, value_local = pair_local[:, :model_width], pair_local[:, model_width:]
    factor = query_factor(query_scale)
    factor_grad = jnp.sum(
        query_grad * query_raw.reshape(series_count, HEADS, HEAD, local_length), axis=(0, 1, 3)
    )
    grad_scale = (
        factor_grad * jax.nn.sigmoid(query_scale.astype(jnp.float32)) * (SOFT_ONE / math.sqrt(HEAD))
    )
    raw_low = (
        (query_grad * factor[None, None, :, None])
        .astype(jnp.bfloat16)
        .reshape(series_count, model_width, local_length)
    )
    projected_grad = jnp.concatenate(
        [raw_low, key_local.astype(jnp.bfloat16), value_local.astype(jnp.bfloat16)], axis=1
    )
    grad_qkv = jnp.einsum(
        "bld,bcl->dc", normed_low, projected_grad, preferred_element_type=jnp.float32
    )
    normed_grad = jnp.einsum(
        "bkcl,kdc->bld",
        projected_grad.reshape(series_count, 3, model_width, local_length),
        qkv_weight,
        preferred_element_type=jnp.float32,
    ).reshape(token_count, model_width)
    norm_grad_one, gain_grad_one = norm_back(
        current, inverse_one, norm_gains[0].astype(jnp.float32), normed_grad
    )
    result = attn_grad + norm_grad_one
    layer_grads = (
        grad_qkv,
        grad_out,
        grad_up,
        grad_down,
        jnp.stack([gain_grad_one, gain_grad_two]),
        grad_up_bias,
        grad_down_bias,
        grad_scale,
    )
    return (result, layer_grads)


def pack_small(norm_gains, up_bias, down_bias, query_scale):
    layers, _, shard = norm_gains.shape
    scale = jnp.pad(query_scale, ((0, 0), (0, shard - query_scale.shape[1])))
    rows = jnp.concatenate([norm_gains.reshape(2 * layers, shard), up_bias, down_bias, scale])
    return jnp.pad(rows, ((0, -rows.shape[0] % 16), (0, -shard % 128)))


def unpack_small(tiny, layers, shard, scale_shard):
    count = tiny.shape[0]
    vectors = tiny[:, : 4 * layers, :shard].transpose(1, 0, 2).reshape(4 * layers, count * shard)
    scale = tiny[:, 4 * layers : 5 * layers, :scale_shard].transpose(1, 0, 2).reshape(layers, count * scale_shard)
    gains = vectors[: 2 * layers].reshape(layers, 2, count * shard)
    return gains, vectors[2 * layers : 3 * layers], vectors[3 * layers :], scale


def pack_tiny(layer_grads, count):
    gains = jnp.concatenate([g[4] for g in layer_grads])
    vectors = jnp.concatenate(
        [gains, jnp.stack([g[5] for g in layer_grads]), jnp.stack([g[6] for g in layer_grads])]
    )
    scale = jnp.stack([g[7] for g in layer_grads])
    shard, part = vectors.shape[1] // count, scale.shape[1] // count
    vectors = vectors.reshape(-1, count, shard)
    scale = jnp.pad(scale.reshape(-1, count, part), ((0, 0), (0, 0), (0, shard - part)))
    rows = jnp.concatenate([vectors, scale]).transpose(1, 0, 2)
    return jnp.pad(rows, ((0, 0), (0, -rows.shape[1] % 16), (0, -shard % 128)))


def unpack_tiny(tiny, layers, shard, part):
    gains = tiny[: 2 * layers, :shard].reshape(layers, 2, shard)
    up, down = tiny[2 * layers : 3 * layers, :shard], tiny[3 * layers : 4 * layers, :shard]
    return gains, up, down, tiny[4 * layers : 5 * layers, :part]


def gather_plain(qkv_weight, out_weight, up_weight, down_weight, small):
    layers, shard, width = out_weight.shape
    qkv = qkv_weight.reshape(layers, shard, 3, width).transpose(0, 2, 1, 3)
    square = jnp.stack([out_weight, up_weight, down_weight], axis=1)
    units = jnp.concatenate([qkv, square], axis=1).reshape(layers * UNITS, shard, width)
    full = lax.all_gather(units, "fsdp", axis=1, tiled=True)
    return full, lax.all_gather(small, "fsdp", axis=0)


def reduce_plain(layer_grads, tiny):
    units = []
    for grads in layer_grads:
        width = grads[0].shape[1]
        units += list(grads[:3]) + [grads[3][:, k * width : (k + 1) * width] for k in range(3)]
    shares = lax.psum_scatter(jnp.stack(units), "fsdp", scatter_dimension=1, tiled=True)
    small = lax.psum_scatter(tiny, "fsdp", scatter_dimension=0, tiled=True)[0]
    return lax.psum(shares, ("replica", "seq")), lax.psum(small, ("replica", "seq"))


def plain(
    series_in,
    cotangent,
    qkv_weight,
    out_weight,
    up_weight,
    down_weight,
    norm_gains,
    up_bias,
    down_bias,
    query_scale,
    pad_length,
    span_starts,
    span_count,
):
    series_count, local_length, model_width = series_in.shape
    seq_count = lax.axis_size("seq")
    group = lax.axis_size("fsdp")
    total_length = local_length * seq_count
    offset = lax.axis_index("seq") * local_length
    allowed = visible(pad_length, span_starts, span_count, offset, local_length, total_length)
    layer_count, shard = qkv_weight.shape[:2]
    scale_shard = query_scale.shape[1]
    small = pack_small(norm_gains, up_bias, down_bias, query_scale)
    full, tiny = gather_plain(qkv_weight, out_weight, up_weight, down_weight, small)
    gains, up_full, down_full, scale_full = unpack_small(tiny, layer_count, shard, scale_shard)
    weights = [
        (
            full[UNITS * l : UNITS * l + 3],
            full[UNITS * l + 3],
            full[UNITS * l + 4],
            full[UNITS * l + 5],
            gains[l],
            up_full[l],
            down_full[l],
            scale_full[l],
        )
        for l in range(layer_count)
    ]
    current = series_in.reshape(series_count * local_length, model_width).astype(jnp.float32)
    stored_list = []
    for l in range(layer_count):
        current, stored = forward_layer(
            current, weights[l], allowed, series_count, local_length, total_length
        )
        stored_list.append(stored)
    series_out = current.reshape(series_count, local_length, model_width).astype(jnp.bfloat16)
    upstream = cotangent.reshape(series_count * local_length, model_width).astype(jnp.float32)
    order = list(reversed(range(layer_count)))
    grads_list = {}
    for l in order:
        upstream, grads_list[l] = backward_layer(
            upstream, weights[l], stored_list[l], allowed, series_count, local_length, total_length
        )
    tiny_grads = pack_tiny([grads_list[l] for l in range(layer_count)], group)
    big = [
        tuple(grads_list[l][k].astype(jnp.bfloat16) for k in (3, 2, 1, 0)) for l in order
    ]
    shares, tiny_sum = reduce_plain(big, tiny_grads)
    shares = shares.reshape(layer_count, UNITS, shard, model_width)[::-1]
    grad_gains, grad_up_bias, grad_down_bias, grad_scale = unpack_tiny(
        tiny_sum, layer_count, shard, scale_shard
    )
    grad_qkv = shares[:, 3:].transpose(0, 2, 1, 3).reshape(layer_count, shard, 3 * model_width)
    input_grad = upstream.reshape(series_count, local_length, model_width).astype(jnp.bfloat16)
    return (
        series_out,
        input_grad,
        grad_qkv.astype(jnp.float32),
        shares[:, 2].astype(jnp.float32),
        shares[:, 1].astype(jnp.float32),
        shares[:, 0].astype(jnp.float32),
        grad_gains,
        grad_up_bias,
        grad_down_bias,
        grad_scale,
    )


def finish(shares, tiny, layers, shard, width, query_scale):
    shares = shares.reshape(layers, UNITS, shard, width)[::-1]
    low = jnp.float32
    place = lax.axis_index("fsdp")
    part = query_scale.shape[1]
    vectors = lax.dynamic_slice_in_dim(tiny[: 4 * layers], place * shard, shard, axis=1)
    scale = lax.dynamic_slice_in_dim(tiny[4 * layers : 5 * layers], place * part, part, axis=1)
    raw = query_scale.astype(jnp.float32)
    scale = scale * (jax.nn.sigmoid(raw) * (SOFT_ONE / math.sqrt(HEAD))) / query_factor(query_scale)
    qkv = jnp.concatenate([shares[:, 5], shares[:, 3], shares[:, 4]], axis=2)
    return (
        qkv.astype(low),
        shares[:, 2].astype(low),
        shares[:, 1].astype(low),
        shares[:, 0].astype(low),
        vectors[: 2 * layers].reshape(layers, 2, shard),
        vectors[2 * layers : 3 * layers],
        vectors[3 * layers :],
        scale,
    )


def fused(
    series_in,
    cotangent,
    qkv_weight,
    out_weight,
    up_weight,
    down_weight,
    norm_gains,
    up_bias,
    down_bias,
    query_scale,
    pad_length,
    span_starts,
    span_count,
):
    layers, shard, width = out_weight.shape
    nz = lax.axis_size("fsdp") // 2
    full, vec, series_out, bias, saved = forward_pass(
        nz,
        series_in[0],
        (qkv_weight, out_weight, up_weight, down_weight),
        (norm_gains, up_bias, down_bias, query_scale),
        (pad_length, span_starts, span_count),
    )
    shares, tiny, input_grad = backward_pass(nz, cotangent[0], full, vec, bias, saved)
    rest = finish(shares, tiny, layers, shard, width, query_scale)
    return (series_out[None], input_grad[None]) + rest


def shards(*args):
    series_in, out_weight = args[0], args[3]
    group = lax.axis_size("fsdp")
    width = series_in.shape[2]
    block = lax.axis_size("replica") == 2 and lax.axis_size("seq") == 2 and group == 8
    block = block and series_in.shape[0] == 1 and width == out_weight.shape[2] == HEADS * HEAD
    block = block and (width // group) % 32 == 0 and width % 256 == 0
    return fused(*args) if block else plain(*args)


def solution(mesh):
    return jax.shard_map(
        shards,
        mesh=mesh,
        in_specs=(
            P(("replica", "fsdp"), "seq", None),
            P(("replica", "fsdp"), "seq", None),
            P(None, "fsdp", None),
            P(None, "fsdp", None),
            P(None, "fsdp", None),
            P(None, "fsdp", None),
            P(None, None, "fsdp"),
            P(None, "fsdp"),
            P(None, "fsdp"),
            P(None, "fsdp"),
            P(("replica", "fsdp")),
            P(("replica", "fsdp"), None),
            P(("replica", "fsdp")),
        ),
        out_specs=(
            P(("replica", "fsdp"), "seq", None),
            P(("replica", "fsdp"), "seq", None),
            P(None, "fsdp", None),
            P(None, "fsdp", None),
            P(None, "fsdp", None),
            P(None, "fsdp", None),
            P(None, None, "fsdp"),
            P(None, "fsdp"),
            P(None, "fsdp"),
            P(None, "fsdp"),
        ),
        check_vma=False,
    )
```
